32 devices in a mesh: rep: 4 (over y, x), grp: 8 (over z, core).
Axes of the slice: x: 2, y: 2, z: 4, core: 2. Of those that a mesh axis runs over, the one named last changes fastest.
Arguments:
- hidden_in: bfloat16 [2, 4, 1024, 768], P(None, 'rep', 'grp'), may hold values from -6 to 6
- seq_lengths: int32 [2, 4], P(None, 'rep'), may hold values from 256 to 1024, as said below
- latent_query: float32 [768, 768], P('grp'), may hold values from -0.3125 to 0.3125
- latent_key: float32 [768, 768], P('grp'), may hold values from -0.3125 to 0.3125
- latent_value: float32 [768, 768], P('grp'), may hold values from -0.21875 to 0.21875
- latent_out: float32 [768, 768], P('grp'), may hold values from -4 to 4
- latent_up: float32 [3072, 768], P('grp'), may hold values from -0.3125 to 0.3125
- latent_down: float32 [768, 3072], P('grp'), may hold values from -0.3125 to 0.3125
- bias_query: float32 [768], replicated, may hold values from -3 to 3
- bias_value: float32 [768], replicated, may hold values from -3 to 3
- bias_out: float32 [768], replicated, may hold values from -3 to 3
- bias_up: float32 [3072], replicated, may hold values from -3 to 3
- bias_down: float32 [768], replicated, may hold values from -3 to 3
- gain_first: float32 [768], replicated, may hold values from 0.5 to 1.5
- shift_first: float32 [768], replicated, may hold values from -3 to 3
- gain_second: float32 [768], replicated, may hold values from 0.5 to 1.5
- shift_second: float32 [768], replicated, may hold values from -3 to 3
- clip_input: float32 [768], replicated, may hold values from 1 to 3
- teacher_query: bfloat16 [768, 768], P('grp'), may hold values from -0.3125 to 0.3125
- teacher_key: bfloat16 [768, 768], P('grp'), may hold values from -0.3125 to 0.3125
- teacher_value: bfloat16 [768, 768], P('grp'), may hold values from -0.21875 to 0.21875
- teacher_out: bfloat16 [768, 768], P('grp'), may hold values from -4 to 4
- teacher_up: bfloat16 [3072, 768], P('grp'), may hold values from -0.3125 to 0.3125
- teacher_down: bfloat16 [768, 3072], P('grp'), may hold values from -0.3125 to 0.3125
- teacher_biases: float32 [4, 768], replicated, may hold values from -3 to 3
- teacher_inner: float32 [3072], replicated, may hold values from -3 to 3
- teacher_gains: float32 [2, 768], replicated, may hold values from 0.5 to 1.5
- teacher_shifts: float32 [2, 768], replicated, may hold values from -3 to 3
Outputs:
- layer_out: bfloat16 [2, 4, 1024, 768], P(None, 'rep', 'grp')
- distill_loss: float32 [], replicated
- grad_input: float32 [2, 4, 1024, 768], P(None, 'rep', 'grp')
- grad_query: float32 [768, 768], P('grp')
- grad_key: float32 [768, 768], P('grp')
- grad_value: float32 [768, 768], P('grp')
- grad_out: float32 [768, 768], P('grp')
- grad_up: float32 [3072, 768], P('grp')
- grad_down: float32 [768, 3072], P('grp')
- grad_bias_query: float32 [768], P('grp')
- grad_bias_value: float32 [768], P('grp')
- grad_bias_out: float32 [768], P('grp')
- grad_bias_up: float32 [3072], P('grp')
- grad_bias_down: float32 [768], P('grp')
- grad_gain_first: float32 [768], P('grp')
- grad_shift_first: float32 [768], P('grp')
- grad_gain_second: float32 [768], P('grp')
- grad_shift_second: float32 [768], P('grp')
The draws below stay inside these ranges and needn't reach their ends.
Inputs may be any that keep to these rules, and one draw needn't show every extreme that they name: `seq_lengths`: A sequence's valid positions are its first ones; in every draw some sequence is valid over all 1024 positions.
All inputs are finite; a program needn't handle non-finite values.
Results may differ from the reference program's by a relative error of at most 0.023.
Values may be sent and summed in bfloat16 or wider, within the bound.
No kernel may reach another device: no remote copies, remote signals or barrier semaphores. Data moves between devices by JAX's collectives and lax.ppermute only.
A program may use at most 192 MiB of HBM per device.

```python
import math
import jax
import jax.numpy as jnp
from jax import lax

D = 768
H = 12
DH = 64
FF = 3072
MB = 2
SEQ = 1024
NSEQ = 4


def draw_seq_lengths(key, part):
    length_key = jax.random.fold_in(key, 11)
    chosen_key = jax.random.fold_in(key, 23)
    drawn = jax.random.randint(length_key, (MB * NSEQ,), SEQ // 4, SEQ + 1)
    chosen = jax.random.randint(chosen_key, (), 0, MB * NSEQ)
    merged = jnp.where(jnp.arange(MB * NSEQ) == chosen, SEQ, drawn)
    return merged.reshape(MB, NSEQ).astype(jnp.int32)


def steps_of(rng, extent, shards, least, high):
    def one(position, shards_of):
        draws = jax.random.uniform(jax.random.fold_in(jax.random.fold_in(rng, 6), position), (shards_of,), jnp.float32, least / len(shards), high / len(shards))
        return jnp.repeat(jnp.exp(draws), extent[position] // shards_of).reshape((-1,) + (1,) * (len(extent) - position - 1))

    loudness = one(*shards[0])
    for cut in shards[1:]:
        loudness = loudness * one(*cut)
    return loudness


def normal_values(stream_key, shape, deviation, limit, split=(), kind=jnp.bfloat16):
    level = steps_of(stream_key, shape, split, -0.22, 0.18) if split else 1.0
    values = jax.random.normal(stream_key, shape, jnp.float32) * deviation * level
    return jnp.minimum(jnp.maximum(values, -limit), limit).astype(kind)


def setup_inputs(seed: int = 0) -> dict:
    key_of = jax.random.split(jax.random.key(seed), 29)
    hidden_in = normal_values(key_of[0], (MB, NSEQ, SEQ, D), 1.0, 6.0, ((1, 4), (2, 8)))
    seq_lengths = draw_seq_lengths(jax.random.fold_in(key_of[28], 71), 0)
    latent_query = normal_values(key_of[2], (D, D), (D // 2) ** -0.5, 0.3125, ((0, 8),), jnp.float32)
    latent_key = normal_values(key_of[3], (D, D), (D // 2) ** -0.5, 0.3125, ((0, 8),), jnp.float32)
    latent_value = normal_values(key_of[4], (D, D), D ** -0.5, 0.21875, ((0, 8),), jnp.float32)
    latent_out = normal_values(key_of[5], (D, D), 2 ** -0.5, 4.0, ((0, 8),), jnp.float32)
    latent_up = normal_values(key_of[6], (FF, D), (D // 2) ** -0.5, 0.3125, ((0, 8),), jnp.float32)
    latent_down = normal_values(key_of[7], (D, FF), (FF // 8) ** -0.5, 0.3125, ((0, 8),), jnp.float32)
    bias_query = normal_values(key_of[8], (D,), 0.5, 3.0, (), jnp.float32)
    bias_value = normal_values(key_of[9], (D,), 0.5, 3.0, (), jnp.float32)
    bias_out = normal_values(key_of[10], (D,), 0.5, 3.0, (), jnp.float32)
    bias_up = normal_values(key_of[11], (FF,), 0.5, 3.0, (), jnp.float32)
    bias_down = normal_values(key_of[12], (D,), 0.5, 3.0, (), jnp.float32)
    gain_first = jnp.clip(1.0 + 0.1 * jax.random.normal(key_of[13], (D,), jnp.float32), 0.5, 1.5)
    shift_first = normal_values(key_of[14], (D,), 0.5, 3.0, (), jnp.float32)
    gain_second = jnp.clip(1.0 + 0.1 * jax.random.normal(key_of[15], (D,), jnp.float32), 0.5, 1.5)
    shift_second = normal_values(key_of[16], (D,), 0.5, 3.0, (), jnp.float32)
    clip_input = jnp.clip(jnp.exp(jax.random.uniform(key_of[17], (D,), jnp.float32, math.log(1.0), math.log(3.0))), 1.0, 3.0)
    teacher_query = normal_values(key_of[18], (D, D), (D // 2) ** -0.5, 0.3125, ((0, 8),))
    teacher_key = normal_values(key_of[19], (D, D), (D // 2) ** -0.5, 0.3125, ((0, 8),))
    teacher_value = normal_values(key_of[20], (D, D), D ** -0.5, 0.21875, ((0, 8),))
    teacher_out = normal_values(key_of[21], (D, D), 2 ** -0.5, 4.0, ((0, 8),))
    teacher_up = normal_values(key_of[22], (FF, D), (D // 2) ** -0.5, 0.3125, ((0, 8),))
    teacher_down = normal_values(key_of[23], (D, FF), (FF // 8) ** -0.5, 0.3125, ((0, 8),))
    teacher_biases = normal_values(key_of[24], (4, D), 0.5, 3.0, (), jnp.float32)
    teacher_inner = normal_values(key_of[25], (FF,), 0.5, 3.0, (), jnp.float32)
    teacher_gains = jnp.clip(1.0 + 0.1 * jax.random.normal(key_of[26], (2, D), jnp.float32), 0.5, 1.5)
    teacher_shifts = normal_values(key_of[27], (2, D), 0.5, 3.0, (), jnp.float32)
    return {"hidden_in": hidden_in, "seq_lengths": seq_lengths, "latent_query": latent_query, "latent_key": latent_key, "latent_value": latent_value, "latent_out": latent_out, "latent_up": latent_up, "latent_down": latent_down, "bias_query": bias_query, "bias_value": bias_value, "bias_out": bias_out, "bias_up": bias_up, "bias_down": bias_down, "gain_first": gain_first, "shift_first": shift_first, "gain_second": gain_second, "shift_second": shift_second, "clip_input": clip_input, "teacher_query": teacher_query, "teacher_key": teacher_key, "teacher_value": teacher_value, "teacher_out": teacher_out, "teacher_up": teacher_up, "teacher_down": teacher_down, "teacher_biases": teacher_biases, "teacher_inner": teacher_inner, "teacher_gains": teacher_gains, "teacher_shifts": teacher_shifts}


@jax.custom_vjp
def low(v):
    return lax.optimization_barrier(v.astype(jnp.bfloat16)).astype(jnp.float32)

@jax.custom_vjp
def low_back(v):
    return v

def low_keep(v):
    return (low(v), None)

def low_pass(kept, grad):
    return (grad,)

def back_keep(v):
    return (v, None)

def back_low(kept, grad):
    return (low(grad),)
low.defvjp(low_keep, low_pass)
low_back.defvjp(back_keep, back_low)
NEG_FILL = -1e+30
NORM_EPS = 1e-05
HIGHEST = lax.Precision.HIGHEST

def rounded(tensor):
    return low(low_back(tensor))

def project_rows(operand, weight):
    return jnp.einsum('ri,oi->ro', operand, weight, precision=HIGHEST)

def layer_norm(tensor, gain_row, shift_row):
    centre = tensor - lax.optimization_barrier(jnp.mean(tensor, axis=-1, keepdims=True))
    spread = lax.optimization_barrier(jnp.mean(centre * centre, axis=-1, keepdims=True))
    return centre * lax.rsqrt(spread + NORM_EPS) * gain_row + shift_row

def gelu_exact(tensor):
    return 0.5 * tensor * (1.0 + lax.erf(tensor * 0.7071067811865476))

def attend(queries, keys, values, length):
    seq_total = queries.shape[0]
    key_heads = keys.reshape(seq_total, H, DH)
    value_heads = values.reshape(seq_total, H, DH)
    key_valid = jnp.arange(seq_total, dtype=jnp.int32) < length
    block_rows = 512 if seq_total % 512 == 0 else seq_total

    def one_block(query_block):
        query_heads = query_block.reshape(block_rows, H, DH)
        raw_scores = low_back(jnp.einsum('chd,nhd->hcn', query_heads, key_heads, precision=HIGHEST) * DH ** (-0.5))
        scores = jnp.where(key_valid[None, None, :], raw_scores, NEG_FILL)
        row_top = lax.optimization_barrier(jnp.max(scores, axis=-1, keepdims=True))
        exponent = jnp.exp(scores - row_top)
        softmax_w = exponent / lax.optimization_barrier(jnp.sum(exponent, axis=-1, keepdims=True))
        context = jnp.einsum('hcn,nhd->chd', low(softmax_w), value_heads, precision=HIGHEST)
        return context.reshape(block_rows, H * DH)
    blocks = queries.reshape(seq_total // block_rows, block_rows, H * DH)
    return lax.map(jax.checkpoint(one_block), blocks).reshape(seq_total, H * DH)

def block_forward(hidden, length, weights, vectors, clips):
    w_query, w_key, w_value, w_out, w_up, w_down = weights
    b_query, b_value, b_out, b_up, b_down, gain_one, shift_one, gain_two, shift_two = vectors
    entering = hidden if clips is None else jnp.clip(hidden, -clips[0], clips[0])
    inputs = low(entering)
    queries = rounded(project_rows(inputs, w_query) + b_query)
    keys = rounded(project_rows(inputs, w_key))
    values = rounded(project_rows(inputs, w_value) + b_value)
    context = rounded(attend(queries, keys, values, length))
    first_sum = hidden + (low_back(project_rows(context, w_out)) + b_out)
    first_norm = layer_norm(first_sum, gain_one, shift_one)
    upper_in = low(first_norm)
    gate_pre = low_back(project_rows(upper_in, w_up)) + b_up
    lower_in = low(gelu_exact(gate_pre))
    second_sum = first_norm + (low_back(project_rows(lower_in, w_down)) + b_down)
    return layer_norm(second_sum, gain_two, shift_two)

def reference(hidden_in, seq_lengths, latent_query, latent_key, latent_value, latent_out, latent_up, latent_down, bias_query, bias_value, bias_out, bias_up, bias_down, gain_first, shift_first, gain_second, shift_second, clip_input, teacher_query, teacher_key, teacher_value, teacher_out, teacher_up, teacher_down, teacher_biases, teacher_inner, teacher_gains, teacher_shifts):
    seq_count = MB * NSEQ
    inputs_all = hidden_in.astype(jnp.float32).reshape(seq_count, SEQ, D)
    lengths_all = seq_lengths.reshape(seq_count).astype(jnp.int32)
    tutor_weights = tuple((weight.astype(jnp.float32) for weight in (teacher_query, teacher_key, teacher_value, teacher_out, teacher_up, teacher_down)))
    tutor_vectors = (teacher_biases[0], teacher_biases[1], teacher_biases[2], teacher_inner, teacher_biases[3], teacher_gains[0], teacher_shifts[0], teacher_gains[1], teacher_shifts[1])

    def tutor_one(paired):
        return block_forward(paired[0], paired[1], tutor_weights, tutor_vectors, None)
    targets = lax.map(tutor_one, (inputs_all, lengths_all))
    latents = (latent_query, latent_key, latent_value, latent_out, latent_up, latent_down)
    held_latents = latents
    signs_fixed = tuple((lax.optimization_barrier(jnp.mean(jnp.abs(latent), axis=1, keepdims=True)) * jnp.sign(latent) for latent in latents))
    vectors = (bias_query, bias_value, bias_out, bias_up, bias_down, gain_first, shift_first, gain_second, shift_second)
    clips = (clip_input,)

    def student(inputs_in, latents_in, vectors_in):
        weights = tuple((low(fixed + (latent - held)) for fixed, latent, held in zip(signs_fixed, latents_in, held_latents)))

        def seq_step(running, item):
            seq_in, seq_len, seq_target = item
            result = block_forward(seq_in, seq_len, weights, vectors_in, clips)
            keep_rows = (jnp.arange(SEQ, dtype=jnp.int32) < seq_len).astype(result.dtype)[:, None]
            difference = result - seq_target
            return (running + 0.5 * jnp.sum(keep_rows * difference * difference), result)
        error, results = lax.scan(jax.checkpoint(seq_step), jnp.zeros((), jnp.float32), (inputs_in, lengths_all, targets))
        return (results, error)
    (results, error), pull_back = jax.vjp(student, inputs_all, latents, vectors)
    grads_in, grads_latent, grads_vector = pull_back((jnp.zeros_like(results), jnp.ones_like(error)))
    full_shape = (MB, NSEQ, SEQ, D)
    layer_out = results.reshape(full_shape).astype(jnp.bfloat16)
    distill_loss = error / (MB * NSEQ * SEQ * D)
    grad_input = grads_in.reshape(full_shape)
    return (layer_out, distill_loss, grad_input, grads_latent[0], grads_latent[1], grads_latent[2], grads_latent[3], grads_latent[4], grads_latent[5], grads_vector[0], grads_vector[1], grads_vector[2], grads_vector[3], grads_vector[4], grads_vector[5], grads_vector[6], grads_vector[7], grads_vector[8])
```

```python
import functools

import jax
import jax.numpy as jnp
from jax import lax
from jax.experimental import pallas as pl
from jax.experimental.pallas import tpu as pltpu
from jax.sharding import PartitionSpec as P

H = 12
DH = 64


NEG_FILL = -1e30
NORM_EPS = 1e-05


def layer_norm(tensor, gain_row, shift_row):
    centre = tensor - jnp.mean(tensor, axis=-1, keepdims=True)
    spread = jnp.mean(centre * centre, axis=-1, keepdims=True)
    return centre * lax.rsqrt(spread + NORM_EPS) * gain_row + shift_row


def gelu_exact(tensor):
    return 0.5 * tensor * (1.0 + lax.erf(tensor * 0.7071067811865476))


def times_rows(operand, weight):
    return lax.dot_general(
        operand, weight, (((1,), (1,)), ((), ())), preferred_element_type=jnp.float32
    )


def binarize(latent_rows):
    magnitude = jnp.mean(jnp.abs(latent_rows), axis=1, keepdims=True)
    return (magnitude * jnp.sign(latent_rows)).astype(jnp.bfloat16)


def student_project(operand, latent):
    return times_rows(
        operand,
        binarize(
            lax.all_gather(latent.astype(jnp.bfloat16), "grp", axis=0, tiled=True).astype(
                jnp.float32
            )
        ),
    )


def teacher_project(operand, weight):
    return times_rows(operand, lax.all_gather(weight, "grp", axis=0, tiled=True))


def add_columns(grads_low, weight_rows):
    return jnp.dot(grads_low, weight_rows, preferred_element_type=jnp.float32)


def student_back(grads_low, latent):
    return add_columns(
        grads_low,
        binarize(
            lax.all_gather(latent.astype(jnp.bfloat16), "grp", axis=0, tiled=True).astype(
                jnp.float32
            )
        ),
    )


def weight_grad(grads_low, operand):
    return lax.dot_general(
        grads_low, operand, (((0,), (0,)), ((), ())), preferred_element_type=jnp.float32
    )


def head_scores(queries, keys):
    seq_count, query_rows = (queries.shape[0], queries.shape[1])
    key_rows = keys.shape[1]
    query_heads = queries.reshape(seq_count, query_rows, H, DH)
    key_heads = keys.reshape(seq_count, key_rows, H, DH)
    return jnp.einsum(
        "schd,snhd->shcn", query_heads, key_heads, preferred_element_type=jnp.float32
    ) * DH ** (-0.5)


def key_mask(lengths, first_row, key_rows):
    positions = first_row + jnp.arange(key_rows, dtype=jnp.int32)
    return (positions[None, :] < lengths[:, None])[:, None, None, :]


def in_blocks(block_step, state_in, pieces):
    total_rows = pieces[0].shape[1]
    block_rows = 512

    def scan_step(running, block_index):
        offset = block_index * block_rows
        sliced = tuple(
            (lax.dynamic_slice_in_dim(member, offset, block_rows, 1) for member in pieces)
        )
        return (block_step(running, sliced, offset), None)

    state_out, unused = lax.scan(
        scan_step, state_in, jnp.arange(total_rows // block_rows, dtype=jnp.int32)
    )
    return state_out


def attention_forward(queries, keys, values, lengths):
    seq_count, query_rows, width_all = queries.shape
    stat_shape = (seq_count, H, query_rows)

    def stat_step(state_in, pieces, first_row):
        row_top, row_sum = state_in
        key_part = pieces[0]
        scores = jnp.where(
            key_mask(lengths, first_row, key_part.shape[1]),
            head_scores(queries, key_part),
            NEG_FILL,
        )
        new_top = jnp.maximum(row_top, jnp.max(scores, axis=3))
        row_sum = row_sum * jnp.exp(row_top - new_top) + jnp.sum(
            jnp.exp(scores - new_top[..., None]), axis=3
        )
        return (new_top, row_sum)

    stat_init = (jnp.full(stat_shape, NEG_FILL, jnp.float32), jnp.zeros(stat_shape, jnp.float32))
    row_top, row_sum = in_blocks(
        stat_step, stat_init, (lax.all_gather(keys, "grp", axis=1, tiled=True),)
    )
    log_total = row_top + jnp.log(row_sum)
    head_shape = (seq_count, query_rows, H, DH)

    def mix_step(state_in, pieces, first_row):
        key_part, value_part = pieces
        key_rows = key_part.shape[1]
        scores = jnp.where(
            key_mask(lengths, first_row, key_rows), head_scores(queries, key_part), NEG_FILL
        )
        softmax_w = jnp.exp(scores - log_total[..., None])
        value_heads = value_part.reshape(seq_count, key_rows, H, DH)
        return state_in + jnp.einsum(
            "shcn,snhd->schd",
            softmax_w.astype(jnp.bfloat16),
            value_heads,
            preferred_element_type=jnp.float32,
        )

    context_heads = in_blocks(
        mix_step,
        jnp.zeros(head_shape, jnp.float32),
        (
            lax.all_gather(keys, "grp", axis=1, tiled=True),
            lax.all_gather(values, "grp", axis=1, tiled=True),
        ),
    )
    return (context_heads, log_total)


def query_grads(queries, keys, values, lengths, log_total, delta_heads, dcontext):
    seq_count, query_rows, width_all = queries.shape
    dcontext_heads = dcontext.reshape(seq_count, query_rows, H, DH)

    def query_grad_step(running, pieces, first_row):
        key_part, value_part = pieces
        key_rows = key_part.shape[1]
        scores = jnp.where(
            key_mask(lengths, first_row, key_rows), head_scores(queries, key_part), NEG_FILL
        )
        softmax_w = jnp.exp(scores - log_total[..., None])
        value_heads = value_part.reshape(seq_count, key_rows, H, DH)
        key_heads = key_part.reshape(seq_count, key_rows, H, DH)
        dweights = jnp.einsum(
            "schd,snhd->shcn", dcontext_heads, value_heads, preferred_element_type=jnp.float32
        )
        dscores = (softmax_w * (dweights - delta_heads[..., None])).astype(jnp.bfloat16)
        return running + jnp.einsum(
            "shcn,snhd->schd", dscores, key_heads, preferred_element_type=jnp.float32
        )

    zero_heads = jnp.zeros((seq_count, query_rows, H, DH), jnp.float32)
    folded = in_blocks(
        query_grad_step,
        zero_heads,
        (
            lax.all_gather(keys, "grp", axis=1, tiled=True),
            lax.all_gather(values, "grp", axis=1, tiled=True),
        ),
    )
    return (folded * DH ** (-0.5)).reshape(seq_count, query_rows, width_all)


def key_grads(queries, keys, values, lengths, log_rows, delta_rows, dcontext):
    seq_count, key_rows, width_all = keys.shape
    log_all, delta_all = (
        lax.all_gather(log_rows, "grp", axis=1, tiled=True),
        lax.all_gather(delta_rows, "grp", axis=1, tiled=True),
    )
    own_mask = key_mask(lengths, lax.axis_index("grp") * key_rows, key_rows)
    value_heads = values.reshape(seq_count, key_rows, H, DH)

    def key_grad_step(running, pieces, first_row):
        query_part, dcontext_part = pieces
        query_count = query_part.shape[1]
        log_part = jnp.transpose(
            lax.dynamic_slice_in_dim(log_all, first_row, query_count, 1), (0, 2, 1)
        )
        delta_part = jnp.transpose(
            lax.dynamic_slice_in_dim(delta_all, first_row, query_count, 1), (0, 2, 1)
        )
        scores = jnp.where(own_mask, head_scores(query_part, keys), NEG_FILL)
        softmax_w = jnp.exp(scores - log_part[..., None])
        dcontext_heads = dcontext_part.reshape(seq_count, query_count, H, DH)
        query_heads = query_part.reshape(seq_count, query_count, H, DH)
        dweights = jnp.einsum(
            "schd,snhd->shcn", dcontext_heads, value_heads, preferred_element_type=jnp.float32
        )
        dscores = (softmax_w * (dweights - delta_part[..., None])).astype(jnp.bfloat16)
        dkey_sum = running[0] + jnp.einsum(
            "shcn,schd->snhd", dscores, query_heads, preferred_element_type=jnp.float32
        )
        dvalue_sum = running[1] + jnp.einsum(
            "shcn,schd->snhd",
            softmax_w.astype(jnp.bfloat16),
            dcontext_heads,
            preferred_element_type=jnp.float32,
        )
        return (dkey_sum, dvalue_sum)

    zero_heads = jnp.zeros((seq_count, key_rows, H, DH), jnp.float32)
    dkey_sum, dvalue_sum = in_blocks(
        key_grad_step,
        (zero_heads, zero_heads),
        (
            lax.all_gather(queries, "grp", axis=1, tiled=True),
            lax.all_gather(dcontext, "grp", axis=1, tiled=True),
        ),
    )
    return (
        (dkey_sum * DH ** (-0.5)).reshape(seq_count, key_rows, width_all),
        dvalue_sum.reshape(seq_count, key_rows, width_all),
    )


def forward(hidden, lengths, project, vectors, clips):
    b_query, b_value, b_out, b_up, b_down, gain_one, shift_one, gain_two, shift_two = vectors
    seq_count = lengths.shape[0]
    query_rows = hidden.shape[0] // seq_count
    width_all = hidden.shape[1]
    entering = hidden if clips is None else jnp.clip(hidden, -clips[0], clips[0])
    inputs = entering.astype(jnp.bfloat16)
    queries = (
        (project(inputs, 0) + b_query)
        .astype(jnp.bfloat16)
        .reshape(seq_count, query_rows, width_all)
    )
    keys = project(inputs, 1).astype(jnp.bfloat16).reshape(seq_count, query_rows, width_all)
    values = (
        (project(inputs, 2) + b_value)
        .astype(jnp.bfloat16)
        .reshape(seq_count, query_rows, width_all)
    )
    context_heads, log_total = attention_forward(queries, keys, values, lengths)
    context_low = context_heads.reshape(hidden.shape).astype(jnp.bfloat16)
    first_sum = hidden + project(context_low, 3) + b_out
    first_norm = layer_norm(first_sum, gain_one, shift_one)
    upper_in = first_norm.astype(jnp.bfloat16)
    gate_pre = project(upper_in, 4) + b_up
    lower_in = gelu_exact(gate_pre).astype(jnp.bfloat16)
    second_sum = first_norm + project(lower_in, 5) + b_down
    output = layer_norm(second_sum, gain_two, shift_two)
    kept_values = (
        inputs,
        queries,
        keys,
        values,
        context_heads,
        log_total,
        context_low,
        first_sum,
        first_norm,
        upper_in,
        gate_pre,
        lower_in,
        second_sum,
    )
    return (output, kept_values)


def backward(grad_output, hidden, lengths, latents, vectors, clips, kept_values):
    (
        inputs,
        queries,
        keys,
        values,
        context_heads,
        log_total,
        context_low,
        first_sum,
        first_norm,
        upper_in,
        gate_pre,
        lower_in,
        second_sum,
    ) = kept_values
    w_query, w_key, w_value, w_out, w_up, w_down = latents
    gain_one, shift_one, gain_two, shift_two = (vectors[5], vectors[6], vectors[7], vectors[8])
    seq_count, query_rows, width_all = queries.shape
    unused, pull_two = jax.vjp(layer_norm, second_sum, gain_two, shift_two)
    dsecond, dgain_two, dshift_two = pull_two(grad_output)
    dsecond_low = dsecond.astype(jnp.bfloat16)
    grad_down = weight_grad(dsecond_low, lower_in)
    dlower = student_back(dsecond_low, w_down)
    unused, pull_gate = jax.vjp(gelu_exact, gate_pre)
    dgate = pull_gate(dlower)[0]
    dgate_low = dgate.astype(jnp.bfloat16)
    grad_up = weight_grad(dgate_low, upper_in)
    dupper = student_back(dgate_low, w_up)
    dfirst = dsecond + dupper
    unused, pull_one = jax.vjp(layer_norm, first_sum, gain_one, shift_one)
    dfirst_sum, dgain_one, dshift_one = pull_one(dfirst)
    dbranch_low = dfirst_sum.astype(jnp.bfloat16)
    grad_out = weight_grad(dbranch_low, context_low)
    dcontext = (
        student_back(dbranch_low, w_out)
        .astype(jnp.bfloat16)
        .reshape(seq_count, query_rows, width_all)
    )
    delta_rows = jnp.sum(
        dcontext.reshape(seq_count, query_rows, H, DH).astype(jnp.float32) * context_heads, axis=3
    )
    dqueries = query_grads(
        queries, keys, values, lengths, log_total, jnp.transpose(delta_rows, (0, 2, 1)), dcontext
    )
    dkeys, dvalues = key_grads(
        queries, keys, values, lengths, jnp.transpose(log_total, (0, 2, 1)), delta_rows, dcontext
    )
    all_rows = seq_count * query_rows
    dqueries_low = dqueries.reshape(all_rows, width_all).astype(jnp.bfloat16)
    dkeys_low = dkeys.reshape(all_rows, width_all).astype(jnp.bfloat16)
    dvalues_low = dvalues.reshape(all_rows, width_all).astype(jnp.bfloat16)
    grad_query = weight_grad(dqueries_low, inputs)
    grad_key = weight_grad(dkeys_low, inputs)
    grad_value = weight_grad(dvalues_low, inputs)
    dinputs = (
        student_back(dqueries_low, w_query)
        + student_back(dkeys_low, w_key)
        + student_back(dvalues_low, w_value)
    )
    unused, pull_input = jax.vjp(lambda tensor: jnp.clip(tensor, -clips[0], clips[0]), hidden)
    grad_hidden = dfirst_sum + pull_input(dinputs)[0]
    weight_parts = (grad_query, grad_key, grad_value, grad_out, grad_up, grad_down)
    vector_parts = (
        jnp.sum(dqueries_low.astype(jnp.float32), axis=0),
        jnp.sum(dvalues_low.astype(jnp.float32), axis=0),
        jnp.sum(dfirst_sum, axis=0),
        jnp.sum(dgate, axis=0),
        jnp.sum(dsecond, axis=0),
        dgain_one,
        dshift_one,
        dgain_two,
        dshift_two,
    )
    return (weight_parts, vector_parts, grad_hidden)


def shards(
    hidden_in,
    seq_lengths,
    latent_query,
    latent_key,
    latent_value,
    latent_out,
    latent_up,
    latent_down,
    bias_query,
    bias_value,
    bias_out,
    bias_up,
    bias_down,
    gain_first,
    shift_first,
    gain_second,
    shift_second,
    clip_input,
    teacher_query,
    teacher_key,
    teacher_value,
    teacher_out,
    teacher_up,
    teacher_down,
    teacher_biases,
    teacher_inner,
    teacher_gains,
    teacher_shifts,
):
    latents = (latent_query, latent_key, latent_value, latent_out, latent_up, latent_down)
    tutors = (teacher_query, teacher_key, teacher_value, teacher_out, teacher_up, teacher_down)
    vectors = (
        bias_query,
        bias_value,
        bias_out,
        bias_up,
        bias_down,
        gain_first,
        shift_first,
        gain_second,
        shift_second,
    )
    tutor_vectors = (
        teacher_biases[0],
        teacher_biases[1],
        teacher_biases[2],
        teacher_inner,
        teacher_biases[3],
        teacher_gains[0],
        teacher_shifts[0],
        teacher_gains[1],
        teacher_shifts[1],
    )
    clips = (clip_input,)
    micro_count, seq_count, local_rows, width_all = hidden_in.shape
    positions = lax.axis_index("grp") * local_rows + jnp.arange(local_rows, dtype=jnp.int32)

    def student_weight(operand, slot_index):
        return student_project(operand, latents[slot_index])

    def tutor_weight(operand, slot_index):
        return teacher_project(operand, tutors[slot_index])

    weight_sums = None
    vector_sums = [jnp.zeros(vector.shape, jnp.float32) for vector in vectors]
    error_sum = jnp.zeros((), jnp.float32)
    outputs_all = []
    grads_all = []
    for micro_index in range(micro_count):
        hidden = (
            hidden_in[micro_index].astype(jnp.float32).reshape(seq_count * local_rows, width_all)
        )
        lengths = seq_lengths[micro_index]
        targets, unused = forward(hidden, lengths, tutor_weight, tutor_vectors, None)
        output, kept_values = forward(hidden, lengths, student_weight, vectors, clips)
        row_keep = (
            (positions[None, :] < lengths[:, None])
            .astype(jnp.float32)
            .reshape(seq_count * local_rows, 1)
        )
        difference = output - targets
        error_sum = error_sum + 0.5 * jnp.sum(row_keep * difference * difference)
        weight_parts, vector_parts, grad_hidden = backward(
            row_keep * difference, hidden, lengths, latents, vectors, clips, kept_values
        )
        if weight_sums is None:
            weight_sums = list(weight_parts)
        else:
            weight_sums = [running + added for running, added in zip(weight_sums, weight_parts)]
        vector_sums = [running + added for running, added in zip(vector_sums, vector_parts)]
        outputs_all.append(output.astype(jnp.bfloat16).reshape(seq_count, local_rows, width_all))
        grads_all.append(grad_hidden.reshape(seq_count, local_rows, width_all))
    weight_sums = (
        lax.psum_scatter(
            weight_sums[0].astype(jnp.bfloat16), "grp", scatter_dimension=0, tiled=True
        ).astype(jnp.float32),
        lax.psum_scatter(
            weight_sums[1].astype(jnp.bfloat16), "grp", scatter_dimension=0, tiled=True
        ).astype(jnp.float32),
        lax.psum_scatter(
            weight_sums[2].astype(jnp.bfloat16), "grp", scatter_dimension=0, tiled=True
        ).astype(jnp.float32),
        lax.psum_scatter(
            weight_sums[3].astype(jnp.bfloat16), "grp", scatter_dimension=0, tiled=True
        ).astype(jnp.float32),
        lax.psum_scatter(
            weight_sums[4].astype(jnp.bfloat16), "grp", scatter_dimension=0, tiled=True
        ).astype(jnp.float32),
        lax.psum_scatter(
            weight_sums[5].astype(jnp.bfloat16), "grp", scatter_dimension=0, tiled=True
        ).astype(jnp.float32),
    )
    vector_shards = (
        lax.psum_scatter(
            vector_sums[0].astype(jnp.bfloat16), "grp", scatter_dimension=0, tiled=True
        ).astype(jnp.float32),
        lax.psum_scatter(
            vector_sums[1].astype(jnp.bfloat16), "grp", scatter_dimension=0, tiled=True
        ).astype(jnp.float32),
        lax.psum_scatter(
            vector_sums[2].astype(jnp.bfloat16), "grp", scatter_dimension=0, tiled=True
        ).astype(jnp.float32),
        lax.psum_scatter(
            vector_sums[3].astype(jnp.bfloat16), "grp", scatter_dimension=0, tiled=True
        ).astype(jnp.float32),
        lax.psum_scatter(
            vector_sums[4].astype(jnp.bfloat16), "grp", scatter_dimension=0, tiled=True
        ).astype(jnp.float32),
        lax.psum_scatter(
            vector_sums[5].astype(jnp.bfloat16), "grp", scatter_dimension=0, tiled=True
        ).astype(jnp.float32),
        lax.psum_scatter(
            vector_sums[6].astype(jnp.bfloat16), "grp", scatter_dimension=0, tiled=True
        ).astype(jnp.float32),
        lax.psum_scatter(
            vector_sums[7].astype(jnp.bfloat16), "grp", scatter_dimension=0, tiled=True
        ).astype(jnp.float32),
        lax.psum_scatter(
            vector_sums[8].astype(jnp.bfloat16), "grp", scatter_dimension=0, tiled=True
        ).astype(jnp.float32),
    )
    totals = (
        lax.psum(weight_sums[0].astype(jnp.bfloat16), "rep").astype(jnp.float32),
        lax.psum(weight_sums[1].astype(jnp.bfloat16), "rep").astype(jnp.float32),
        lax.psum(weight_sums[2].astype(jnp.bfloat16), "rep").astype(jnp.float32),
        lax.psum(weight_sums[3].astype(jnp.bfloat16), "rep").astype(jnp.float32),
        lax.psum(weight_sums[4].astype(jnp.bfloat16), "rep").astype(jnp.float32),
        lax.psum(weight_sums[5].astype(jnp.bfloat16), "rep").astype(jnp.float32),
        lax.psum(vector_shards[0].astype(jnp.bfloat16), "rep").astype(jnp.float32),
        lax.psum(vector_shards[1].astype(jnp.bfloat16), "rep").astype(jnp.float32),
        lax.psum(vector_shards[2].astype(jnp.bfloat16), "rep").astype(jnp.float32),
        lax.psum(vector_shards[3].astype(jnp.bfloat16), "rep").astype(jnp.float32),
        lax.psum(vector_shards[4].astype(jnp.bfloat16), "rep").astype(jnp.float32),
        lax.psum(vector_shards[5].astype(jnp.bfloat16), "rep").astype(jnp.float32),
        lax.psum(vector_shards[6].astype(jnp.bfloat16), "rep").astype(jnp.float32),
        lax.psum(vector_shards[7].astype(jnp.bfloat16), "rep").astype(jnp.float32),
        lax.psum(vector_shards[8].astype(jnp.bfloat16), "rep").astype(jnp.float32),
    )
    error_all = lax.psum(error_sum, ("rep", "grp"))
    entries = (
        micro_count
        * seq_count
        * lax.axis_size("rep")
        * local_rows
        * lax.axis_size("grp")
        * width_all
    )
    distill_loss = error_all / entries
    return (
        jnp.stack(outputs_all),
        distill_loss,
        jnp.stack(grads_all),
        totals[0],
        totals[1],
        totals[2],
        totals[3],
        totals[4],
        totals[5],
        totals[6],
        totals[7],
        totals[8],
        totals[9],
        totals[10],
        totals[11],
        totals[12],
        totals[13],
        totals[14],
    )


F32 = jnp.float32
BF16 = jnp.bfloat16
ANY = pl.BlockSpec(memory_space=pl.ANY)
VM = pl.BlockSpec(memory_space=pltpu.VMEM)
SM = pl.BlockSpec(memory_space=pltpu.SMEM)
VMEM_LIMIT = 60 * 1024 * 1024

I_CORE, I_REP, I_Z, I_LEN, I_RING = 0, 1, 2, 3, 4


def z_ring(line):
    return list(range(0, line, 2)) + list(range(1, line, 2))[::-1]


def dims(a, b, ca, cb):
    return lax.dot_general(a, b, (((ca,), (cb,)), ((), ())), preferred_element_type=F32)


def params(**kw):
    return pltpu.CompilerParams(vmem_limit_bytes=VMEM_LIMIT, **kw)


def cost(flops, nbytes, trans=0):
    return pl.CostEstimate(flops=int(flops), bytes_accessed=int(nbytes), transcendentals=int(trans))


def wait_all(ref, sem):
    pltpu.make_async_copy(ref, ref, sem).wait()


def binary_rows(latent):
    level = jnp.mean(jnp.abs(latent), axis=1, keepdims=True)
    return jnp.where(latent > 0, level, jnp.where(latent < 0, -level, 0.0)).astype(BF16)


def pack_kernel(
    info, hid, lq, lk, lv, lo, lu, ld, tq, tk, tv, to, tu, td, qkv, own, mine, keep, send
):
    core, rep = info[I_CORE], info[I_REP]
    keep[...] = hid[core]
    send[...] = hid[1 - core]
    for slot, ref in enumerate((lq, lk, lv)):
        qkv[0, slot] = binary_rows(ref[...])
    for slot, ref in enumerate((tq, tk, tv)):
        qkv[1, slot] = ref[...]
    rows, width = lq.shape
    quarter = own.shape[0]
    half = rows // 2

    def fill(base, up, down):
        for r in range(quarter):
            own[r, base : base + rows] = up[r * rows : (r + 1) * rows]
            own[r, base + rows : base + 2 * rows] = down[:, r * width : (r + 1) * width]

    fill(0, binary_rows(lu[...]), binary_rows(ld[...]))
    fill(2 * rows, tu, td)
    student_out = binary_rows(lo[...])
    for h in range(2):
        own[h, 4 * rows :] = student_out[h * half : (h + 1) * half]
        own[2 + h, 4 * rows :] = to[h * half : (h + 1) * half]
    mine[...] = own[rep]


def pack(info, hid, latents, tutors):
    rows, width = latents[0].shape
    piece = 4 * rows + rows // 2
    half = hid.shape[1:]
    return pl.pallas_call(
        pack_kernel,
        out_shape=(
            jax.ShapeDtypeStruct((2, 3, rows, width), BF16),
            jax.ShapeDtypeStruct((4, piece, width), BF16),
            jax.ShapeDtypeStruct((piece, width), BF16),
            jax.ShapeDtypeStruct(half, BF16),
            jax.ShapeDtypeStruct(half, BF16),
        ),
        in_specs=[SM] + [VM] * 13,
        out_specs=(VM,) * 5,
        compiler_params=params(),
        cost_estimate=cost(4e6, 12e6),
        name="pack",
    )(info, hid, *latents, *tutors)


def load_tokens(info, xs, pieces, sem):
    core = info[I_CORE]
    for k, piece in enumerate(pieces):
        for j in range(2):
            spot = jnp.where(j == 0, core, 1 - core)
            pltpu.make_async_copy(piece.at[j], xs.at[info[I_RING + k], spot], sem).start()


def load_rows(info, ws, own, sib, sem):
    core = info[I_CORE]
    for slot in range(3):
        pltpu.make_async_copy(own.at[slot], ws.at[slot, core], sem).start()
        pltpu.make_async_copy(sib.at[slot], ws.at[slot, 1 - core], sem).start()


def attend_kernel(student, info, *refs):
    pieces, refs = refs[:4], refs[4:]
    own, sib, bq, bv, clip = refs[:5]
    refs = refs[5:]
    if student:
        out, qkv_out, lse_out, ctx_out, xs, ws, qs, ks, vt, ct, sems = refs
    else:
        out, xs, ws, qs, ks, vt, ct, sems = refs
    load_tokens(info, xs, pieces, sems.at[0])
    load_rows(info, ws, own, sib, sems.at[1])
    line, _, half, width = xs.shape
    block = 2 * half
    feats = qs.shape[1]
    total = qs.shape[0]
    heads = feats // DH
    place = info[I_Z]
    length = info[I_LEN]
    bq_row, bv_row = bq[place], bv[place]
    wait_all(xs, sems.at[0])
    wait_all(ws, sems.at[1])

    def project(b, carry):
        rows = pl.ds(pl.multiple_of(b * block, block), block)
        x = xs[b].reshape(block, width)
        if student:
            lim = clip[...]
            x = jnp.clip(x.astype(F32), -lim, lim).astype(BF16)
        q = (dims(x, ws[0].reshape(feats, width), 1, 1) + bq_row).astype(BF16)
        k = dims(x, ws[1].reshape(feats, width), 1, 1).astype(BF16)
        v = (dims(x, ws[2].reshape(feats, width), 1, 1) + bv_row).astype(BF16)
        q = q * jnp.asarray(DH ** (-0.5), BF16)
        qs[rows] = q
        ks[rows] = k
        vt[:, rows] = v.astype(F32).T.astype(BF16)
        if student:
            qkv_out[0, rows] = q
            qkv_out[1, rows] = k
            qkv_out[2, rows] = v
        return carry

    lax.fori_loop(0, line, project, 0)
    fill = jnp.where(
        lax.broadcasted_iota(jnp.int32, (total, 1), 0) < length, 0.0, NEG_FILL
    ).astype(F32)
    lane_head = lax.broadcasted_iota(jnp.int32, (1, feats), 1) // DH

    def mix(b, carry):
        rows = pl.ds(pl.multiple_of(b * block, block), block)
        q = qs[rows]
        for h in range(heads):
            q_h = jnp.where(lane_head == h, q, jnp.zeros_like(q))
            scores = dims(ks[...], q_h, 1, 1) + fill
            top = jnp.max(scores, axis=0, keepdims=True)
            weight = jnp.exp(scores - top)
            mass = jnp.sum(weight, axis=0, keepdims=True)
            head = slice(h * DH, (h + 1) * DH)
            mixed = dims(vt[head], weight.astype(BF16), 1, 0) * (1.0 / mass)
            ct[head, rows] = mixed
            if student:
                lse_out[h : h + 1, rows] = top + jnp.log(mass)
        return carry

    lax.fori_loop(0, line, mix, 0)
    for b in range(line):
        out[b] = ct[:, b * block : (b + 1) * block].T.astype(BF16)
    if student:
        ctx_out[...] = ct[...]


def attend(info, pieces, own, sib, bq, bv, clip, student):
    _, half, width = pieces[0].shape
    line = len(pieces)
    total = line * 2 * half
    rows = own.shape[1]
    feats = 2 * rows
    outs = [jax.ShapeDtypeStruct((line, 2 * half, feats), BF16)]
    if student:
        outs += [
            jax.ShapeDtypeStruct((3, total, feats), BF16),
            jax.ShapeDtypeStruct((8, total), F32),
            jax.ShapeDtypeStruct((feats, total), F32),
        ]
    return pl.pallas_call(
        functools.partial(attend_kernel, student),
        out_shape=tuple(outs),
        in_specs=[SM] + [ANY] * 6 + [VM] * 3,
        out_specs=(VM,) * len(outs),
        scratch_shapes=[
            pltpu.VMEM((line, 2, half, width), BF16),
            pltpu.VMEM((3, 2, rows, width), BF16),
            pltpu.VMEM((total, feats), BF16),
            pltpu.VMEM((total, feats), BF16),
            pltpu.VMEM((feats, total), BF16),
            pltpu.VMEM((feats, total), F32),
            pltpu.SemaphoreType.DMA((2,)),
        ],
        compiler_params=params(),
        cost_estimate=cost(6e9, 4e6, 3e6),
        name="attend_student" if student else "attend_tutor",
    )(info, *pieces, own, sib, bq, bv, clip)


def attend_back_kernel(info, *refs):
    pieces, refs = refs[:4], refs[4:]
    (own, sib, clip, qkv, lse, ctx, dctx, part0, part1, part2, part3, keep, send) = refs[:13]
    (xs, ws, kt, dct, dq, dk, dv, sems) = refs[13:]
    parts = (part0, part1, part2, part3)
    load_tokens(info, xs, pieces, sems.at[0])
    load_rows(info, ws, own, sib, sems.at[1])
    line, _, half, width = xs.shape
    block = 2 * half
    total, feats = dk.shape
    heads = feats // DH
    core = info[I_CORE]
    length = info[I_LEN]
    lim = clip[...]
    for b in range(line):
        cols = slice(b * block, (b + 1) * block)
        kt[:, cols] = qkv[1, cols].astype(F32).T.astype(BF16)
        dct[:, cols] = dctx[b].astype(F32).T
    dk[...] = jnp.zeros_like(dk)
    dv[...] = jnp.zeros_like(dv)
    fill = jnp.where(
        lax.broadcasted_iota(jnp.int32, (total, 1), 0) < length, 0.0, NEG_FILL
    ).astype(F32)
    lane_head = lax.broadcasted_iota(jnp.int32, (1, feats), 1) // DH

    def body(b, carry):
        rows = pl.ds(pl.multiple_of(b * block, block), block)
        q = qkv[0, rows]
        g = dctx[b]
        dk_add = dv_add = None
        for h in range(heads):
            head = slice(h * DH, (h + 1) * DH)
            q_h = jnp.where(lane_head == h, q, jnp.zeros_like(q))
            g_h = jnp.where(lane_head == h, g, jnp.zeros_like(g))
            delta = jnp.sum(dct[head, rows] * ctx[head, rows], axis=0, keepdims=True)
            probs = jnp.exp(dims(qkv[1], q_h, 1, 1) + fill - lse[h : h + 1, rows])
            dprobs = dims(qkv[2], g_h, 1, 1)
            dscores = (probs * (dprobs - delta)).astype(BF16)
            dv_h = dims(probs.astype(BF16), g_h, 1, 0)
            dk_h = dims(dscores, q_h, 1, 0)
            dk_add = dk_h if dk_add is None else dk_add + dk_h
            dv_add = dv_h if dv_add is None else dv_add + dv_h
            dq[head, rows] = dims(kt[head], dscores, 1, 0) * (DH ** (-0.5))
        dk[...] += dk_add
        dv[...] += dv_add
        return carry

    lax.fori_loop(0, line, body, 0)
    wait_all(xs, sems.at[0])
    wait_all(ws, sems.at[1])
    dq_t = dq[...].astype(BF16)
    dq_low = dq_t.astype(F32).T.astype(BF16)
    dk_low = dk[...].astype(BF16)
    dv_low = dv[...].astype(BF16)
    dk_t = dk_low.astype(F32).T.astype(BF16)
    dv_t = dv_low.astype(F32).T.astype(BF16)
    qkv_flat = [ws[slot].reshape(feats, width) for slot in range(3)]
    for k in range(line):
        spot = info[I_RING + k]
        rows = pl.ds(pl.multiple_of(spot * block, block), block)
        dk_rows = dk[rows].astype(BF16)
        dv_rows = dv[rows].astype(BF16)
        dq_rows = dq[:, rows].T.astype(BF16)
        parts[k][...] = (
            dims(dq_rows, qkv_flat[0], 1, 0)
            + dims(dk_rows, qkv_flat[1], 1, 0)
            + dims(dv_rows, qkv_flat[2], 1, 0)
        ).astype(BF16)
    grads = []
    for low_t in (dq_t, dk_t, dv_t):
        acc = None
        for b in range(line):
            x = jnp.clip(xs[b].reshape(block, width).astype(F32), -lim, lim).astype(BF16)
            one = dims(low_t[:, b * block : (b + 1) * block], x, 1, 0)
            acc = one if acc is None else acc + one
        grads.append(acc)
    rows = feats // 2
    bias_q = jnp.sum(dq_low.astype(F32), axis=0, keepdims=True)
    bias_v = jnp.sum(dv_low.astype(F32), axis=0, keepdims=True)
    for rel, ref in ((0, keep), (1, send)):
        for c in range(2):

            @pl.when((core if rel == 0 else 1 - core) == c)
            def _():
                for slot, grad in enumerate(grads):
                    ref[slot * rows : (slot + 1) * rows] = grad[c * rows : (c + 1) * rows].astype(
                        ref.dtype
                    )
                tail = jnp.concatenate(
                    [
                        bias_q[:, c * rows : (c + 1) * rows],
                        bias_v[:, c * rows : (c + 1) * rows],
                        jnp.zeros((1, width - 2 * rows), F32),
                    ],
                    axis=1,
                )
                ref[3 * rows :] = jnp.broadcast_to(tail, (16, width)).astype(ref.dtype)


def attend_back(info, pieces, own, sib, clip, qkv, lse, ctx, dctx):
    _, half, width = pieces[0].shape
    line = len(pieces)
    total = line * 2 * half
    rows = own.shape[1]
    feats = 2 * rows
    part = jax.ShapeDtypeStruct((2 * half, width), BF16)
    grad = jax.ShapeDtypeStruct((3 * rows + 16, width), BF16)
    return pl.pallas_call(
        attend_back_kernel,
        out_shape=(part,) * 4 + (grad, grad),
        in_specs=[SM] + [ANY] * 6 + [VM] * 5,
        out_specs=(VM,) * 6,
        scratch_shapes=[
            pltpu.VMEM((line, 2, half, width), BF16),
            pltpu.VMEM((3, 2, rows, width), BF16),
            pltpu.VMEM((feats, total), BF16),
            pltpu.VMEM((feats, total), F32),
            pltpu.VMEM((feats, total), F32),
            pltpu.VMEM((total, feats), F32),
            pltpu.VMEM((total, feats), F32),
            pltpu.SemaphoreType.DMA((2,)),
        ],
        compiler_params=params(),
        cost_estimate=cost(12e9, 6e6, 3e6),
        name="attend_back",
    )(info, *pieces, own, sib, clip, qkv, lse, ctx, dctx)


V_OUT, V_DOWN, V_G1, V_S1, V_G2, V_S2, V_UP = 0, 1, 2, 3, 4, 5, 6
S_OUT, S_DOWN, S_G1, S_S1, S_G2, S_S2, S_UP, S_ERR = 0, 1, 2, 3, 4, 5, 6, 10
PAD = 32


def norm_parts(v):
    centre = v - jnp.mean(v, axis=-1, keepdims=True)
    inv = lax.rsqrt(jnp.mean(centre * centre, axis=-1, keepdims=True) + NORM_EPS)
    return centre * inv, inv


def norm_back(dnormed, normed, inv):
    return inv * (
        dnormed
        - jnp.mean(dnormed, axis=-1, keepdims=True)
        - normed * jnp.mean(dnormed * normed, axis=-1, keepdims=True)
    )


def turned(v):
    return v.T.astype(BF16)


def middle_kernel(info, own, sib, *refs):
    chunks, refs = refs[:30], refs[30:]
    (x_own, ctx_s, ctx_t, vecs) = refs[:4]
    (out_keep, out_send, dfirst_keep, dctx_out, sums) = refs[4:9]
    grads = refs[9:17]
    (w_up, w_dn, w_out, gate_pre, lower, gup, gdn, base, aim, acc, sems) = refs[17:]
    core, rep, place, length = info[I_CORE], info[I_REP], info[I_Z], info[I_LEN]
    _, groups, quarters, rows, width = w_up.shape
    tokens = ctx_s.shape[1]
    line = groups // 2
    hidden = groups * rows
    half = rows // 2

    def place_piece(src, first, last, r, g):
        fields = (
            (0, rows, lambda: w_up.at[0, g, r], 0),
            (rows, 2 * rows, lambda: w_dn.at[0, r, g], 1),
            (2 * rows, 3 * rows, lambda: w_up.at[1, g, r], 2),
            (3 * rows, 4 * rows, lambda: w_dn.at[1, r, g], 3),
            (4 * rows, 4 * rows + half, lambda: w_out.at[r // 2, g, lax.rem(r, 2)], 4),
        )
        for lo, hi, dst, sem in fields:
            if first <= lo and hi <= last:
                pltpu.make_async_copy(
                    src.at[pl.ds(lo - first, hi - lo)], dst(), sems.at[sem]
                ).start()

    piece = 4 * rows + half
    for rel, ref in ((0, own), (1, sib)):
        member = 2 * place + (core if rel == 0 else 1 - core)
        for r in range(quarters):
            place_piece(ref.at[r], 0, piece, r, member)
    for k in range(1, line):
        for rel in range(2):
            member = 2 * info[I_RING + k] + (core if rel == 0 else 1 - core)
            mine, from_x, from_y, far_a, far_b = chunks[((k - 1) * 2 + rel) * 5 :][:5]
            place_piece(mine, 0, piece, rep, member)
            place_piece(from_x, 0, piece, rep ^ 1, member)
            place_piece(from_y, 0, piece, rep ^ 2, member)
            place_piece(far_a, 0, 2 * rows, rep ^ 3, member)
            place_piece(far_b, 2 * rows, piece, rep ^ 3, member)

    wait_all(w_out, sems.at[4])
    x_low = jnp.concatenate(
        [x_own[jnp.where(core == j, 0, 1)] for j in range(2)], axis=0
    ).astype(F32)

    def row(net, which):
        return vecs[net, which]

    def context_of(ref):
        return jnp.concatenate([ref[zb] for zb in range(line)], axis=1)

    def upper(net, ctx):
        first = (
            x_low + dims(ctx, w_out[net].reshape(width, width), 1, 1) + row(net, V_OUT)
        )
        normed, inv = norm_parts(first)
        return normed, inv, normed * row(net, V_G1) + row(net, V_S1)

    def lower_half(net, upper_in, keep):
        acc[...] = jnp.zeros_like(acc)

        def step(r, carry):
            gate = (
                dims(upper_in, w_up[net, pl.ds(2 * r, 2)].reshape(hidden, width), 1, 1)
                + vecs[net, V_UP + r]
            )
            low = gelu_exact(gate).astype(BF16)
            if keep:
                gate_pre[r] = gate
                lower[r] = low
            acc[...] += dims(low, w_dn[net, r].reshape(width, hidden), 1, 1)
            return carry

        lax.fori_loop(0, quarters, step, 0)
        return acc[...]

    ctx_tutor = context_of(ctx_t)
    _, _, first_norm = upper(1, ctx_tutor)
    ctx_low = context_of(ctx_s)
    normed_one, inv_one, first_norm_s = upper(0, ctx_low)
    base[...] = first_norm_s
    wait_all(w_up.at[1], sems.at[2])
    wait_all(w_dn.at[1], sems.at[3])
    second = first_norm + lower_half(1, first_norm.astype(BF16), False) + row(1, V_DOWN)
    normed, _ = norm_parts(second)
    aim[...] = normed * row(1, V_G2) + row(1, V_S2)

    wait_all(w_up.at[0], sems.at[0])
    wait_all(w_dn.at[0], sems.at[1])
    upper_in = first_norm_s.astype(BF16)
    second = base[...] + lower_half(0, upper_in, True) + row(0, V_DOWN)
    normed_two, inv_two = norm_parts(second)
    output = normed_two * row(0, V_G2) + row(0, V_S2)
    aim[...] = output - aim[...]
    acc[...] = output

    def part_of(ref, j):
        return ref[pl.ds(pl.multiple_of(j * (tokens // 2), tokens // 2), tokens // 2)]

    out_keep[...] = part_of(acc, core).astype(BF16)
    out_send[...] = part_of(acc, 1 - core).astype(BF16)
    where = place * tokens + lax.broadcasted_iota(jnp.int32, (tokens, 1), 0)
    kept = jnp.where(where < length, 1.0, 0.0).astype(F32)
    dout = kept * aim[...]
    sums[...] = jnp.zeros_like(sums)
    error = 0.5 * jnp.sum(dout * dout)
    sums[S_ERR] = jnp.full((1, width), error, F32)
    sums[S_G2] = jnp.sum(dout * normed_two, axis=0, keepdims=True)
    sums[S_S2] = jnp.sum(dout, axis=0, keepdims=True)
    dsecond = norm_back(dout * row(0, V_G2), normed_two, inv_two)
    sums[S_DOWN] = jnp.sum(dsecond, axis=0, keepdims=True)
    g_down = dsecond.astype(BF16)
    g_down_t = turned(dsecond)
    acc[...] = dsecond

    def back(r, carry):
        low = lower[r]
        gdn[r, :, 0:rows] = dims(g_down_t, low, 1, 0).astype(BF16).reshape(groups, rows, hidden)
        dlower = dims(g_down, w_dn[0, r].reshape(width, hidden), 1, 0)
        gate = gate_pre[r]
        slope = 0.5 * (1.0 + lax.erf(gate * 0.7071067811865476)) + gate * (
            0.3989422804014327 * jnp.exp(-0.5 * gate * gate)
        )
        dgate = dlower * slope
        sums[S_UP + r] = jnp.sum(dgate, axis=0, keepdims=True)
        gup_r = dims(turned(dgate), upper_in, 1, 0).astype(BF16)
        gup[pl.ds(2 * r, 2)] = gup_r.reshape(2, quarters, rows, width)
        acc[...] += dims(
            dgate.astype(BF16), w_up[0, pl.ds(2 * r, 2)].reshape(hidden, width), 1, 0
        )
        return carry

    lax.fori_loop(0, quarters, back, 0)
    dfirst = acc[...]
    sums[S_G1] = jnp.sum(dfirst * normed_one, axis=0, keepdims=True)
    sums[S_S1] = jnp.sum(dfirst, axis=0, keepdims=True)
    dsum = norm_back(dfirst * row(0, V_G1), normed_one, inv_one)
    sums[S_OUT] = jnp.sum(dsum, axis=0, keepdims=True)
    dfirst_keep[...] = dsum
    g_out = dsum.astype(BF16)
    dctx = dims(g_out, w_out[0].reshape(width, width), 1, 0).astype(BF16)
    feats = width // line
    for zb in range(line):
        dctx_out[zb] = dctx[:, zb * feats : (zb + 1) * feats]
    gout = dims(turned(dsum), ctx_low, 1, 0).reshape(groups, quarters, rows // quarters, width)
    slim = rows // quarters
    for r in range(quarters):
        for g in range(groups):
            gdn[r, g, rows : rows + slim] = gout[g, r].astype(BF16)
            gdn[r, g, rows + slim :] = jnp.zeros((PAD - slim, width), BF16)

    for rel in range(2):
        a_keep, a_send, b_keep, b_send = grads[rel * 4 : rel * 4 + 4]
        for far in range(4):
            r = rep ^ far
            for k in range(line):
                g = 2 * info[I_RING + k] + (core if rel == 0 else 1 - core)
                a_ref = a_send if far & 1 else a_keep
                b_ref = b_send if far & 2 else b_keep
                pltpu.make_async_copy(
                    gup.at[g, r], a_ref.at[far >> 1, k], sems.at[5 + rel * 4 + (far & 1)]
                ).start()
                pltpu.make_async_copy(
                    gdn.at[r, g], b_ref.at[far & 1, k], sems.at[7 + rel * 4 + (far >> 1)]
                ).start()
    for rel in range(2):
        for slot in range(4):
            ref = grads[rel * 4 + slot]
            wait_all(ref, sems.at[5 + rel * 4 + slot])


def middle(info, own, sib, chunks, x_own, ctx_s, ctx_t, vecs):
    line, tokens, feats = ctx_s.shape
    width = line * feats
    quarters = own.shape[0]
    groups = 2 * line
    rows = width // groups
    half = (tokens // 2, width)
    a_shape = jax.ShapeDtypeStruct((2, line, rows, width), BF16)
    b_shape = jax.ShapeDtypeStruct((2, line, rows + PAD, width), BF16)
    outs = (
        jax.ShapeDtypeStruct(half, BF16),
        jax.ShapeDtypeStruct(half, BF16),
        jax.ShapeDtypeStruct((tokens, width), F32),
        jax.ShapeDtypeStruct((line, tokens, feats), BF16),
        jax.ShapeDtypeStruct((16, 1, width), F32),
    ) + (a_shape, a_shape, b_shape, b_shape) * 2
    return pl.pallas_call(
        middle_kernel,
        out_shape=outs,
        in_specs=[SM] + [ANY] * 32 + [VM] * 4,
        out_specs=(VM,) * 5 + (ANY,) * 8,
        scratch_shapes=[
            pltpu.VMEM((2, groups, quarters, rows, width), BF16),
            pltpu.VMEM((2, quarters, groups, rows, width), BF16),
            pltpu.VMEM((2, groups, 2, rows // 2, width), BF16),
            pltpu.VMEM((quarters, tokens, width), F32),
            pltpu.VMEM((quarters, tokens, width), BF16),
            pltpu.VMEM((groups, quarters, rows, width), BF16),
            pltpu.VMEM((quarters, groups, rows + PAD, width), BF16),
            pltpu.VMEM((tokens, width), F32),
            pltpu.VMEM((tokens, width), F32),
            pltpu.VMEM((tokens, width), F32),
            pltpu.SemaphoreType.DMA((13,)),
        ],
        compiler_params=params(),
        cost_estimate=cost(15e9, 30e6, 4e6),
        name="middle",
    )(info, own, sib, *chunks, x_own, ctx_s, ctx_t, vecs)


def finish_kernel(info, *refs):
    pieces, refs = refs[:4], refs[4:]
    grad_qkv, up, down, out, gq, gk, gv, scr, sem = refs
    rep = info[I_REP]
    for far, ref in enumerate(pieces):
        pltpu.make_async_copy(ref, scr.at[rep ^ far], sem.at[0]).start()
    rows, width = gq.shape
    for slot, ref in enumerate((gq, gk, gv)):
        ref[...] = grad_qkv[slot * rows : (slot + 1) * rows].astype(F32)
    wait_all(scr, sem.at[0])
    slim = rows // len(pieces)
    for r in range(len(pieces)):
        up[r * rows : (r + 1) * rows] = scr[r, 0:rows].astype(F32)
        down[:, r * width : (r + 1) * width] = scr[r, rows : 2 * rows].astype(F32)
        out[r * slim : (r + 1) * slim] = scr[r, 2 * rows : 2 * rows + PAD].astype(F32)[:slim]


def finish(info, pieces, grad_qkv):
    high, width = pieces[0].shape
    rows = (high - PAD) // 2
    small = jax.ShapeDtypeStruct((rows, width), F32)
    return pl.pallas_call(
        finish_kernel,
        out_shape=(
            jax.ShapeDtypeStruct((4 * rows, width), F32),
            jax.ShapeDtypeStruct((rows, 4 * width), F32),
            small,
            small,
            small,
            small,
        ),
        in_specs=[SM] + [ANY] * 4 + [VM],
        out_specs=(VM,) * 6,
        scratch_shapes=[
            pltpu.VMEM((4, high, width), BF16),
            pltpu.SemaphoreType.DMA((1,)),
        ],
        compiler_params=params(),
        cost_estimate=cost(1e6, 8e6),
        name="finish",
    )(info, *pieces, grad_qkv)


def add_low(*terms):
    total = terms[0].astype(F32)
    for term in terms[1:]:
        total = total + term.astype(F32)
    return total.astype(BF16)


def line_shards(line, *args):
    hidden_in, seq_lengths = args[0], args[1]
    latents, vectors, clip_input = args[2:8], args[8:17], args[17]
    tutors = args[18:24]
    tutor_biases, tutor_inner, tutor_gains, tutor_shifts = args[24:28]
    micro_count, _, local_rows, width = hidden_in.shape
    rep, grp = lax.axis_index("rep"), lax.axis_index("grp")
    place, core = grp // 2, lax.rem(grp, 2)
    ring = z_ring(line)
    behind = [[ring[(ring.index(z) - k) % line] for k in range(line)] for z in range(line)]

    def over_z(x, pairs):
        return lax.ppermute(x, "grp", [(2 * a + c, 2 * b + c) for a, b in pairs for c in range(2)])

    def next_z(x):
        return over_z(x, [(ring[i], ring[(i + 1) % line]) for i in range(line)])

    def swap(x):
        return lax.ppermute(x, "grp", [(g, g ^ 1) for g in range(2 * line)])

    def to_rep(x, bit):
        return lax.ppermute(x, "rep", [(i, i ^ bit) for i in range(4)])

    def to_tokens(x):
        groups = [[2 * z + c for z in range(line)] for c in range(2)]
        return lax.all_to_all(x, "grp", 0, 0, axis_index_groups=groups, tiled=True)

    length = seq_lengths[core, 0]
    info = jnp.concatenate(
        [
            jnp.stack([core, rep, place, length]).astype(jnp.int32),
            jnp.asarray(behind, jnp.int32)[place],
        ]
    )
    clip = clip_input.reshape(1, width)
    qkv_own, own, piece, keep, send = pack(info, hidden_in[:, 0], latents, tutors)
    x_own = jnp.stack([keep, swap(send)])
    qkv_sib = swap(qkv_own)
    sib = swap(own)
    tokens_in = [x_own]
    for _ in range(line - 1):
        tokens_in.append(next_z(tokens_in[-1]))

    rows = latents[0].shape[0]
    chunks = []
    for _ in range(line - 1):
        piece = next_z(piece)
        from_x, from_y = to_rep(piece, 1), to_rep(piece, 2)
        far_a = to_rep(from_x[: 2 * rows], 2)
        far_b = to_rep(from_y[2 * rows :], 1)
        got = [piece, from_x, from_y, far_a, far_b]
        chunks += got + [swap(one) for one in got]

    def heads_row(vector):
        return vector.reshape(line, 1, width // line)

    ctx_s, qkv, lse, ctx = attend(
        info,
        tokens_in,
        qkv_own[0],
        qkv_sib[0],
        heads_row(vectors[0]),
        heads_row(vectors[1]),
        clip,
        True,
    )
    (ctx_t,) = attend(
        info,
        tokens_in,
        qkv_own[1],
        qkv_sib[1],
        heads_row(tutor_biases[0]),
        heads_row(tutor_biases[1]),
        clip,
        False,
    )
    ctx_s, ctx_t = to_tokens(ctx_s), to_tokens(ctx_t)
    vecs = jnp.concatenate(
        [
            vectors[2],
            vectors[4],
            vectors[5],
            vectors[6],
            vectors[7],
            vectors[8],
            vectors[3],
            tutor_biases[2],
            tutor_biases[3],
            tutor_gains[0],
            tutor_shifts[0],
            tutor_gains[1],
            tutor_shifts[1],
            tutor_inner,
        ]
    ).reshape(2, 10, 1, width)
    (
        out_keep,
        out_send,
        dfirst,
        dctx,
        sums,
        a_keep,
        a_send,
        b_keep,
        b_send,
        a_keep_sib,
        a_send_sib,
        b_keep_sib,
        b_send_sib,
    ) = middle(info, own, sib, chunks, x_own, ctx_s, ctx_t, vecs)

    def by_micro(kept, got):
        return jnp.where(
            core == 0, jnp.stack([kept, got]), jnp.stack([got, kept])
        )[:, None]

    dctx = to_tokens(dctx)
    a_out = add_low(a_send, swap(a_send_sib))
    b_out = add_low(b_send, swap(b_send_sib))
    a_keep_sib, b_keep_sib = swap(a_keep_sib), swap(b_keep_sib)
    a_in, b_in = to_rep(a_out, 1), to_rep(b_out, 2)
    a_next = to_rep(add_low(a_keep[1], a_keep_sib[1], a_in[1]), 2)
    b_next = to_rep(add_low(b_keep[1], b_keep_sib[1], b_in[1]), 1)
    both = jnp.concatenate(
        [
            add_low(a_keep[0], a_keep_sib[0], a_in[0], a_next),
            add_low(b_keep[0], b_keep_sib[0], b_in[0], b_next),
        ],
        axis=1,
    )
    layer_out = by_micro(out_keep, swap(out_send))

    part0, part1, part2, part3, gqkv, gqkv_sib = attend_back(
        info, tokens_in, qkv_own[0], qkv_sib[0], clip, qkv, lse, ctx, dctx
    )
    moving = next_z(part1)
    moving = next_z(add_low(moving, part2))
    moving = next_z(add_low(moving, part3))
    grads = next_z(both[1])
    grads = next_z(add_low(grads, both[2]))
    grads = next_z(add_low(grads, both[3]))
    grads = add_low(grads, both[0])
    quarter = [grads, to_rep(grads, 1), to_rep(grads, 2), to_rep(grads, 3)]

    gqkv = add_low(gqkv, swap(gqkv_sib))
    gqkv = add_low(gqkv, to_rep(gqkv, 1))
    gqkv = add_low(gqkv, to_rep(gqkv, 2))
    grad_up, grad_down, grad_out, grad_q, grad_k, grad_v = finish(info, quarter, gqkv)

    total = sums.reshape(16, width)
    total = total + swap(total)
    total = total + to_rep(total, 1)
    total = total + to_rep(total, 2)
    bit = 1
    while bit < line:
        total = total + over_z(total, [(z, z ^ bit) for z in range(line)])
        bit *= 2
    own_cols = lax.dynamic_slice_in_dim(total.reshape(16, 2 * line, rows), grp, 1, 1)[:, 0]
    own_up = lax.dynamic_slice_in_dim(
        total[S_UP : S_UP + 4].reshape(2 * line, 4 * rows), grp, 1, 0
    )[0]
    entries = micro_count * 4 * 2 * line * local_rows * width
    loss = total[S_ERR, 0] / entries

    order = jnp.stack([jnp.where(core == 0, 0, 1), jnp.where(core == 0, 1, 0)])
    hidden_tokens = x_own[order].reshape(2 * local_rows, width).astype(F32)
    dxin = moving.astype(F32) + part0.astype(F32)
    grad_input = dfirst + jnp.where(jnp.abs(hidden_tokens) < clip, dxin, 0.0)
    halves = grad_input.reshape(2, local_rows, width)
    grad_input = by_micro(
        jnp.where(core == 0, halves[0], halves[1]),
        swap(jnp.where(core == 0, halves[1], halves[0])),
    )
    bias = gqkv[3 * rows].astype(F32)
    return (
        layer_out,
        loss,
        grad_input,
        grad_q,
        grad_k,
        grad_v,
        grad_out,
        grad_up,
        grad_down,
        bias[:rows],
        bias[rows : 2 * rows],
        own_cols[S_OUT],
        own_up,
        own_cols[S_DOWN],
        own_cols[S_G1],
        own_cols[S_S1],
        own_cols[S_G2],
        own_cols[S_S2],
    )


def fits_line(mesh, args):
    line = mesh.shape["grp"] // 2
    micro_count, seq_count, total, width = args[0].shape
    hidden = args[6].shape[0]
    return (
        mesh.shape["rep"] == 4
        and line == 4
        and H % line == 0
        and micro_count == 2
        and seq_count == mesh.shape["rep"]
        and total == 8 * 128
        and hidden == 4 * width
    )


def solution(mesh):
    def mapped(body):
        return jax.shard_map(
        body,
        mesh=mesh,
        in_specs=(
            P(None, "rep", "grp", None),
            P(None, "rep"),
            P("grp", None),
            P("grp", None),
            P("grp", None),
            P("grp", None),
            P("grp", None),
            P("grp", None),
            P(),
            P(),
            P(),
            P(),
            P(),
            P(),
            P(),
            P(),
            P(),
            P(),
            P("grp", None),
            P("grp", None),
            P("grp", None),
            P("grp", None),
            P("grp", None),
            P("grp", None),
            P(),
            P(),
            P(),
            P(),
        ),
        out_specs=(
            P(None, "rep", "grp", None),
            P(),
            P(None, "rep", "grp", None),
            P("grp", None),
            P("grp", None),
            P("grp", None),
            P("grp", None),
            P("grp", None),
            P("grp", None),
            P("grp"),
            P("grp"),
            P("grp"),
            P("grp"),
            P("grp"),
            P("grp"),
            P("grp"),
            P("grp"),
            P("grp"),
        ),
        check_vma=False,
    )

    def step(*args):
        if fits_line(mesh, args):
            line = mesh.shape["grp"] // 2
            return mapped(functools.partial(line_shards, line))(*args)
        return mapped(shards)(*args)

    return step
```

```python
import functools

import jax
import jax.numpy as jnp
from jax import lax
from jax.experimental import pallas as pl
from jax.experimental.pallas import tpu as pltpu
from jax.sharding import PartitionSpec as P

H = 12
DH = 64


NEG_FILL = -1e30
NORM_EPS = 1e-05


def layer_norm(tensor, gain_row, shift_row):
    centre = tensor - jnp.mean(tensor, axis=-1, keepdims=True)
    spread = jnp.mean(centre * centre, axis=-1, keepdims=True)
    return centre * lax.rsqrt(spread + NORM_EPS) * gain_row + shift_row


def gelu_exact(tensor):
    return 0.5 * tensor * (1.0 + lax.erf(tensor * 0.7071067811865476))


def times_rows(operand, weight):
    return lax.dot_general(
        operand, weight, (((1,), (1,)), ((), ())), preferred_element_type=jnp.float32
    )


def binarize(latent_rows):
    magnitude = jnp.mean(jnp.abs(latent_rows), axis=1, keepdims=True)
    return (magnitude * jnp.sign(latent_rows)).astype(jnp.bfloat16)


def student_project(operand, latent):
    return times_rows(
        operand,
        binarize(
            lax.all_gather(latent.astype(jnp.bfloat16), "grp", axis=0, tiled=True).astype(
                jnp.float32
            )
        ),
    )


def teacher_project(operand, weight):
    return times_rows(operand, lax.all_gather(weight, "grp", axis=0, tiled=True))


def add_columns(grads_low, weight_rows):
    return jnp.dot(grads_low, weight_rows, preferred_element_type=jnp.float32)


def student_back(grads_low, latent):
    return add_columns(
        grads_low,
        binarize(
            lax.all_gather(latent.astype(jnp.bfloat16), "grp", axis=0, tiled=True).astype(
                jnp.float32
            )
        ),
    )


def weight_grad(grads_low, operand):
    return lax.dot_general(
        grads_low, operand, (((0,), (0,)), ((), ())), preferred_element_type=jnp.float32
    )


def head_scores(queries, keys):
    seq_count, query_rows = (queries.shape[0], queries.shape[1])
    key_rows = keys.shape[1]
    query_heads = queries.reshape(seq_count, query_rows, H, DH)
    key_heads = keys.reshape(seq_count, key_rows, H, DH)
    return jnp.einsum(
        "schd,snhd->shcn", query_heads, key_heads, preferred_element_type=jnp.float32
    ) * DH ** (-0.5)


def key_mask(lengths, first_row, key_rows):
    positions = first_row + jnp.arange(key_rows, dtype=jnp.int32)
    return (positions[None, :] < lengths[:, None])[:, None, None, :]


def in_blocks(block_step, state_in, pieces):
    total_rows = pieces[0].shape[1]
    block_rows = 512

    def scan_step(running, block_index):
        offset = block_index * block_rows
        sliced = tuple(
            (lax.dynamic_slice_in_dim(member, offset, block_rows, 1) for member in pieces)
        )
        return (block_step(running, sliced, offset), None)

    state_out, unused = lax.scan(
        scan_step, state_in, jnp.arange(total_rows // block_rows, dtype=jnp.int32)
    )
    return state_out


def attention_forward(queries, keys, values, lengths):
    seq_count, query_rows, width_all = queries.shape
    stat_shape = (seq_count, H, query_rows)

    def stat_step(state_in, pieces, first_row):
        row_top, row_sum = state_in
        key_part = pieces[0]
        scores = jnp.where(
            key_mask(lengths, first_row, key_part.shape[1]),
            head_scores(queries, key_part),
            NEG_FILL,
        )
        new_top = jnp.maximum(row_top, jnp.max(scores, axis=3))
        row_sum = row_sum * jnp.exp(row_top - new_top) + jnp.sum(
            jnp.exp(scores - new_top[..., None]), axis=3
        )
        return (new_top, row_sum)

    stat_init = (jnp.full(stat_shape, NEG_FILL, jnp.float32), jnp.zeros(stat_shape, jnp.float32))
    row_top, row_sum = in_blocks(
        stat_step, stat_init, (lax.all_gather(keys, "grp", axis=1, tiled=True),)
    )
    log_total = row_top + jnp.log(row_sum)
    head_shape = (seq_count, query_rows, H, DH)

    def mix_step(state_in, pieces, first_row):
        key_part, value_part = pieces
        key_rows = key_part.shape[1]
        scores = jnp.where(
            key_mask(lengths, first_row, key_rows), head_scores(queries, key_part), NEG_FILL
        )
        softmax_w = jnp.exp(scores - log_total[..., None])
        value_heads = value_part.reshape(seq_count, key_rows, H, DH)
        return state_in + jnp.einsum(
            "shcn,snhd->schd",
            softmax_w.astype(jnp.bfloat16),
            value_heads,
            preferred_element_type=jnp.float32,
        )

    context_heads = in_blocks(
        mix_step,
        jnp.zeros(head_shape, jnp.float32),
        (
            lax.all_gather(keys, "grp", axis=1, tiled=True),
            lax.all_gather(values, "grp", axis=1, tiled=True),
        ),
    )
    return (context_heads, log_total)


def query_grads(queries, keys, values, lengths, log_total, delta_heads, dcontext):
    seq_count, query_rows, width_all = queries.shape
    dcontext_heads = dcontext.reshape(seq_count, query_rows, H, DH)

    def query_grad_step(running, pieces, first_row):
        key_part, value_part = pieces
        key_rows = key_part.shape[1]
        scores = jnp.where(
            key_mask(lengths, first_row, key_rows), head_scores(queries, key_part), NEG_FILL
        )
        softmax_w = jnp.exp(scores - log_total[..., None])
        value_heads = value_part.reshape(seq_count, key_rows, H, DH)
        key_heads = key_part.reshape(seq_count, key_rows, H, DH)
        dweights = jnp.einsum(
            "schd,snhd->shcn", dcontext_heads, value_heads, preferred_element_type=jnp.float32
        )
        dscores = (softmax_w * (dweights - delta_heads[..., None])).astype(jnp.bfloat16)
        return running + jnp.einsum(
            "shcn,snhd->schd", dscores, key_heads, preferred_element_type=jnp.float32
        )

    zero_heads = jnp.zeros((seq_count, query_rows, H, DH), jnp.float32)
    folded = in_blocks(
        query_grad_step,
        zero_heads,
        (
            lax.all_gather(keys, "grp", axis=1, tiled=True),
            lax.all_gather(values, "grp", axis=1, tiled=True),
        ),
    )
    return (folded * DH ** (-0.5)).reshape(seq_count, query_rows, width_all)


def key_grads(queries, keys, values, lengths, log_rows, delta_rows, dcontext):
    seq_count, key_rows, width_all = keys.shape
    log_all, delta_all = (
        lax.all_gather(log_rows, "grp", axis=1, tiled=True),
        lax.all_gather(delta_rows, "grp", axis=1, tiled=True),
    )
    own_mask = key_mask(lengths, lax.axis_index("grp") * key_rows, key_rows)
    value_heads = values.reshape(seq_count, key_rows, H, DH)

    def key_grad_step(running, pieces, first_row):
        query_part, dcontext_part = pieces
        query_count = query_part.shape[1]
        log_part = jnp.transpose(
            lax.dynamic_slice_in_dim(log_all, first_row, query_count, 1), (0, 2, 1)
        )
        delta_part = jnp.transpose(
            lax.dynamic_slice_in_dim(delta_all, first_row, query_count, 1), (0, 2, 1)
        )
        scores = jnp.where(own_mask, head_scores(query_part, keys), NEG_FILL)
        softmax_w = jnp.exp(scores - log_part[..., None])
        dcontext_heads = dcontext_part.reshape(seq_count, query_count, H, DH)
        query_heads = query_part.reshape(seq_count, query_count, H, DH)
        dweights = jnp.einsum(
            "schd,snhd->shcn", dcontext_heads, value_heads, preferred_element_type=jnp.float32
        )
        dscores = (softmax_w * (dweights - delta_part[..., None])).astype(jnp.bfloat16)
        dkey_sum = running[0] + jnp.einsum(
            "shcn,schd->snhd", dscores, query_heads, preferred_element_type=jnp.float32
        )
        dvalue_sum = running[1] + jnp.einsum(
            "shcn,schd->snhd",
            softmax_w.astype(jnp.bfloat16),
            dcontext_heads,
            preferred_element_type=jnp.float32,
        )
        return (dkey_sum, dvalue_sum)

    zero_heads = jnp.zeros((seq_count, key_rows, H, DH), jnp.float32)
    dkey_sum, dvalue_sum = in_blocks(
        key_grad_step,
        (zero_heads, zero_heads),
        (
            lax.all_gather(queries, "grp", axis=1, tiled=True),
            lax.all_gather(dcontext, "grp", axis=1, tiled=True),
        ),
    )
    return (
        (dkey_sum * DH ** (-0.5)).reshape(seq_count, key_rows, width_all),
        dvalue_sum.reshape(seq_count, key_rows, width_all),
    )


def forward(hidden, lengths, project, vectors, clips):
    b_query, b_value, b_out, b_up, b_down, gain_one, shift_one, gain_two, shift_two = vectors
    seq_count = lengths.shape[0]
    query_rows = hidden.shape[0] // seq_count
    width_all = hidden.shape[1]
    entering = hidden if clips is None else jnp.clip(hidden, -clips[0], clips[0])
    inputs = entering.astype(jnp.bfloat16)
    queries = (
        (project(inputs, 0) + b_query)
        .astype(jnp.bfloat16)
        .reshape(seq_count, query_rows, width_all)
    )
    keys = project(inputs, 1).astype(jnp.bfloat16).reshape(seq_count, query_rows, width_all)
    values = (
        (project(inputs, 2) + b_value)
        .astype(jnp.bfloat16)
        .reshape(seq_count, query_rows, width_all)
    )
    context_heads, log_total = attention_forward(queries, keys, values, lengths)
    context_low = context_heads.reshape(hidden.shape).astype(jnp.bfloat16)
    first_sum = hidden + project(context_low, 3) + b_out
    first_norm = layer_norm(first_sum, gain_one, shift_one)
    upper_in = first_norm.astype(jnp.bfloat16)
    gate_pre = project(upper_in, 4) + b_up
    lower_in = gelu_exact(gate_pre).astype(jnp.bfloat16)
    second_sum = first_norm + project(lower_in, 5) + b_down
    output = layer_norm(second_sum, gain_two, shift_two)
    kept_values = (
        inputs,
        queries,
        keys,
        values,
        context_heads,
        log_total,
        context_low,
        first_sum,
        first_norm,
        upper_in,
        gate_pre,
        lower_in,
        second_sum,
    )
    return (output, kept_values)


def backward(grad_output, hidden, lengths, latents, vectors, clips, kept_values):
    (
        inputs,
        queries,
        keys,
        values,
        context_heads,
        log_total,
        context_low,
        first_sum,
        first_norm,
        upper_in,
        gate_pre,
        lower_in,
        second_sum,
    ) = kept_values
    w_query, w_key, w_value, w_out, w_up, w_down = latents
    gain_one, shift_one, gain_two, shift_two = (vectors[5], vectors[6], vectors[7], vectors[8])
    seq_count, query_rows, width_all = queries.shape
    unused, pull_two = jax.vjp(layer_norm, second_sum, gain_two, shift_two)
    dsecond, dgain_two, dshift_two = pull_two(grad_output)
    dsecond_low = dsecond.astype(jnp.bfloat16)
    grad_down = weight_grad(dsecond_low, lower_in)
    dlower = student_back(dsecond_low, w_down)
    unused, pull_gate = jax.vjp(gelu_exact, gate_pre)
    dgate = pull_gate(dlower)[0]
    dgate_low = dgate.astype(jnp.bfloat16)
    grad_up = weight_grad(dgate_low, upper_in)
    dupper = student_back(dgate_low, w_up)
    dfirst = dsecond + dupper
    unused, pull_one = jax.vjp(layer_norm, first_sum, gain_one, shift_one)
    dfirst_sum, dgain_one, dshift_one = pull_one(dfirst)
    dbranch_low = dfirst_sum.astype(jnp.bfloat16)
    grad_out = weight_grad(dbranch_low, context_low)
    dcontext = (
        student_back(dbranch_low, w_out)
        .astype(jnp.bfloat16)
        .reshape(seq_count, query_rows, width_all)
    )
    delta_rows = jnp.sum(
        dcontext.reshape(seq_count, query_rows, H, DH).astype(jnp.float32) * context_heads, axis=3
    )
    dqueries = query_grads(
        queries, keys, values, lengths, log_total, jnp.transpose(delta_rows, (0, 2, 1)), dcontext
    )
    dkeys, dvalues = key_grads(
        queries, keys, values, lengths, jnp.transpose(log_total, (0, 2, 1)), delta_rows, dcontext
    )
    all_rows = seq_count * query_rows
    dqueries_low = dqueries.reshape(all_rows, width_all).astype(jnp.bfloat16)
    dkeys_low = dkeys.reshape(all_rows, width_all).astype(jnp.bfloat16)
    dvalues_low = dvalues.reshape(all_rows, width_all).astype(jnp.bfloat16)
    grad_query = weight_grad(dqueries_low, inputs)
    grad_key = weight_grad(dkeys_low, inputs)
    grad_value = weight_grad(dvalues_low, inputs)
    dinputs = (
        student_back(dqueries_low, w_query)
        + student_back(dkeys_low, w_key)
        + student_back(dvalues_low, w_value)
    )
    unused, pull_input = jax.vjp(lambda tensor: jnp.clip(tensor, -clips[0], clips[0]), hidden)
    grad_hidden = dfirst_sum + pull_input(dinputs)[0]
    weight_parts = (grad_query, grad_key, grad_value, grad_out, grad_up, grad_down)
    vector_parts = (
        jnp.sum(dqueries_low.astype(jnp.float32), axis=0),
        jnp.sum(dvalues_low.astype(jnp.float32), axis=0),
        jnp.sum(dfirst_sum, axis=0),
        jnp.sum(dgate, axis=0),
        jnp.sum(dsecond, axis=0),
        dgain_one,
        dshift_one,
        dgain_two,
        dshift_two,
    )
    return (weight_parts, vector_parts, grad_hidden)


def shards(
    hidden_in,
    seq_lengths,
    latent_query,
    latent_key,
    latent_value,
    latent_out,
    latent_up,
    latent_down,
    bias_query,
    bias_value,
    bias_out,
    bias_up,
    bias_down,
    gain_first,
    shift_first,
    gain_second,
    shift_second,
    clip_input,
    teacher_query,
    teacher_key,
    teacher_value,
    teacher_out,
    teacher_up,
    teacher_down,
    teacher_biases,
    teacher_inner,
    teacher_gains,
    teacher_shifts,
):
    latents = (latent_query, latent_key, latent_value, latent_out, latent_up, latent_down)
    tutors = (teacher_query, teacher_key, teacher_value, teacher_out, teacher_up, teacher_down)
    vectors = (
        bias_query,
        bias_value,
        bias_out,
        bias_up,
        bias_down,
        gain_first,
        shift_first,
        gain_second,
        shift_second,
    )
    tutor_vectors = (
        teacher_biases[0],
        teacher_biases[1],
        teacher_biases[2],
        teacher_inner,
        teacher_biases[3],
        teacher_gains[0],
        teacher_shifts[0],
        teacher_gains[1],
        teacher_shifts[1],
    )
    clips = (clip_input,)
    micro_count, seq_count, local_rows, width_all = hidden_in.shape
    positions = lax.axis_index("grp") * local_rows + jnp.arange(local_rows, dtype=jnp.int32)

    def student_weight(operand, slot_index):
        return student_project(operand, latents[slot_index])

    def tutor_weight(operand, slot_index):
        return teacher_project(operand, tutors[slot_index])

    weight_sums = None
    vector_sums = [jnp.zeros(vector.shape, jnp.float32) for vector in vectors]
    error_sum = jnp.zeros((), jnp.float32)
    outputs_all = []
    grads_all = []
    for micro_index in range(micro_count):
        hidden = (
            hidden_in[micro_index].astype(jnp.float32).reshape(seq_count * local_rows, width_all)
        )
        lengths = seq_lengths[micro_index]
        targets, unused = forward(hidden, lengths, tutor_weight, tutor_vectors, None)
        output, kept_values = forward(hidden, lengths, student_weight, vectors, clips)
        row_keep = (
            (positions[None, :] < lengths[:, None])
            .astype(jnp.float32)
            .reshape(seq_count * local_rows, 1)
        )
        difference = output - targets
        error_sum = error_sum + 0.5 * jnp.sum(row_keep * difference * difference)
        weight_parts, vector_parts, grad_hidden = backward(
            row_keep * difference, hidden, lengths, latents, vectors, clips, kept_values
        )
        if weight_sums is None:
            weight_sums = list(weight_parts)
        else:
            weight_sums = [running + added for running, added in zip(weight_sums, weight_parts)]
        vector_sums = [running + added for running, added in zip(vector_sums, vector_parts)]
        outputs_all.append(output.astype(jnp.bfloat16).reshape(seq_count, local_rows, width_all))
        grads_all.append(grad_hidden.reshape(seq_count, local_rows, width_all))
    weight_sums = (
        lax.psum_scatter(
            weight_sums[0].astype(jnp.bfloat16), "grp", scatter_dimension=0, tiled=True
        ).astype(jnp.float32),
        lax.psum_scatter(
            weight_sums[1].astype(jnp.bfloat16), "grp", scatter_dimension=0, tiled=True
        ).astype(jnp.float32),
        lax.psum_scatter(
            weight_sums[2].astype(jnp.bfloat16), "grp", scatter_dimension=0, tiled=True
        ).astype(jnp.float32),
        lax.psum_scatter(
            weight_sums[3].astype(jnp.bfloat16), "grp", scatter_dimension=0, tiled=True
        ).astype(jnp.float32),
        lax.psum_scatter(
            weight_sums[4].astype(jnp.bfloat16), "grp", scatter_dimension=0, tiled=True
        ).astype(jnp.float32),
        lax.psum_scatter(
            weight_sums[5].astype(jnp.bfloat16), "grp", scatter_dimension=0, tiled=True
        ).astype(jnp.float32),
    )
    vector_shards = (
        lax.psum_scatter(
            vector_sums[0].astype(jnp.bfloat16), "grp", scatter_dimension=0, tiled=True
        ).astype(jnp.float32),
        lax.psum_scatter(
            vector_sums[1].astype(jnp.bfloat16), "grp", scatter_dimension=0, tiled=True
        ).astype(jnp.float32),
        lax.psum_scatter(
            vector_sums[2].astype(jnp.bfloat16), "grp", scatter_dimension=0, tiled=True
        ).astype(jnp.float32),
        lax.psum_scatter(
            vector_sums[3].astype(jnp.bfloat16), "grp", scatter_dimension=0, tiled=True
        ).astype(jnp.float32),
        lax.psum_scatter(
            vector_sums[4].astype(jnp.bfloat16), "grp", scatter_dimension=0, tiled=True
        ).astype(jnp.float32),
        lax.psum_scatter(
            vector_sums[5].astype(jnp.bfloat16), "grp", scatter_dimension=0, tiled=True
        ).astype(jnp.float32),
        lax.psum_scatter(
            vector_sums[6].astype(jnp.bfloat16), "grp", scatter_dimension=0, tiled=True
        ).astype(jnp.float32),
        lax.psum_scatter(
            vector_sums[7].astype(jnp.bfloat16), "grp", scatter_dimension=0, tiled=True
        ).astype(jnp.float32),
        lax.psum_scatter(
            vector_sums[8].astype(jnp.bfloat16), "grp", scatter_dimension=0, tiled=True
        ).astype(jnp.float32),
    )
    totals = (
        lax.psum(weight_sums[0].astype(jnp.bfloat16), "rep").astype(jnp.float32),
        lax.psum(weight_sums[1].astype(jnp.bfloat16), "rep").astype(jnp.float32),
        lax.psum(weight_sums[2].astype(jnp.bfloat16), "rep").astype(jnp.float32),
        lax.psum(weight_sums[3].astype(jnp.bfloat16), "rep").astype(jnp.float32),
        lax.psum(weight_sums[4].astype(jnp.bfloat16), "rep").astype(jnp.float32),
        lax.psum(weight_sums[5].astype(jnp.bfloat16), "rep").astype(jnp.float32),
        lax.psum(vector_shards[0].astype(jnp.bfloat16), "rep").astype(jnp.float32),
        lax.psum(vector_shards[1].astype(jnp.bfloat16), "rep").astype(jnp.float32),
        lax.psum(vector_shards[2].astype(jnp.bfloat16), "rep").astype(jnp.float32),
        lax.psum(vector_shards[3].astype(jnp.bfloat16), "rep").astype(jnp.float32),
        lax.psum(vector_shards[4].astype(jnp.bfloat16), "rep").astype(jnp.float32),
        lax.psum(vector_shards[5].astype(jnp.bfloat16), "rep").astype(jnp.float32),
        lax.psum(vector_shards[6].astype(jnp.bfloat16), "rep").astype(jnp.float32),
        lax.psum(vector_shards[7].astype(jnp.bfloat16), "rep").astype(jnp.float32),
        lax.psum(vector_shards[8].astype(jnp.bfloat16), "rep").astype(jnp.float32),
    )
    error_all = lax.psum(error_sum, ("rep", "grp"))
    entries = (
        micro_count
        * seq_count
        * lax.axis_size("rep")
        * local_rows
        * lax.axis_size("grp")
        * width_all
    )
    distill_loss = error_all / entries
    return (
        jnp.stack(outputs_all),
        distill_loss,
        jnp.stack(grads_all),
        totals[0],
        totals[1],
        totals[2],
        totals[3],
        totals[4],
        totals[5],
        totals[6],
        totals[7],
        totals[8],
        totals[9],
        totals[10],
        totals[11],
        totals[12],
        totals[13],
        totals[14],
    )


F32 = jnp.float32
BF16 = jnp.bfloat16
ANY = pl.BlockSpec(memory_space=pl.ANY)
VM = pl.BlockSpec(memory_space=pltpu.VMEM)
SM = pl.BlockSpec(memory_space=pltpu.SMEM)
VMEM_LIMIT = 60 * 1024 * 1024

I_CORE, I_REP, I_Z, I_LEN, I_RING = 0, 1, 2, 3, 4


def z_ring(line):
    return list(range(0, line, 2)) + list(range(1, line, 2))[::-1]


def dims(a, b, ca, cb):
    return lax.dot_general(a, b, (((ca,), (cb,)), ((), ())), preferred_element_type=F32)


def params(**kw):
    return pltpu.CompilerParams(vmem_limit_bytes=VMEM_LIMIT, **kw)


def cost(flops, nbytes, trans=0):
    return pl.CostEstimate(flops=int(flops), bytes_accessed=int(nbytes), transcendentals=int(trans))


def wait_all(ref, sem):
    pltpu.make_async_copy(ref, ref, sem).wait()


def binary_rows(latent):
    level = jnp.mean(jnp.abs(latent), axis=1, keepdims=True)
    return jnp.where(latent > 0, level, jnp.where(latent < 0, -level, 0.0)).astype(BF16)


def pack_kernel(info, lq, lk, lv, lo, lu, ld, tq, tk, tv, to, tu, td, qkv, own, mine):
    rep = info[I_REP]
    for slot, ref in enumerate((lq, lk, lv)):
        qkv[0, slot] = binary_rows(ref[...])
    for slot, ref in enumerate((tq, tk, tv)):
        qkv[1, slot] = ref[...]
    rows, width = lq.shape
    quarter = own.shape[0]
    half = rows // 2

    def fill(base, up, down):
        for r in range(quarter):
            own[r, base : base + rows] = up[r * rows : (r + 1) * rows]
            own[r, base + rows : base + 2 * rows] = down[:, r * width : (r + 1) * width]

    fill(0, binary_rows(lu[...]), binary_rows(ld[...]))
    fill(2 * rows, tu, td)
    student_out = binary_rows(lo[...])
    for h in range(2):
        own[h, 4 * rows :] = student_out[h * half : (h + 1) * half]
        own[2 + h, 4 * rows :] = to[h * half : (h + 1) * half]
    mine[...] = own[rep]


def pack(info, latents, tutors):
    rows, width = latents[0].shape
    piece = 4 * rows + rows // 2
    return pl.pallas_call(
        pack_kernel,
        out_shape=(
            jax.ShapeDtypeStruct((2, 3, rows, width), BF16),
            jax.ShapeDtypeStruct((4, piece, width), BF16),
            jax.ShapeDtypeStruct((piece, width), BF16),
        ),
        in_specs=[SM] + [VM] * 12,
        out_specs=(VM,) * 3,
        compiler_params=params(),
        cost_estimate=cost(4e6, 12e6),
        name="pack",
    )(info, *latents, *tutors)


def table_kernel(*refs):
    heads_bias, vecs = refs[13:]
    line, _, feats = heads_bias.shape[2:]
    width = line * feats

    def flat(ref):
        return ref[...].reshape(1, ref.shape[0])

    bq, bv, bo, bu, bd, g1, s1, g2, s2 = [flat(ref) for ref in refs[:9]]
    biases, inner, gains, shifts = refs[9:13]
    for net, pair in enumerate(((bq, bv), (biases[0:1], biases[1:2]))):
        for slot, row in enumerate(pair):
            for z in range(line):
                heads_bias[net, slot, z] = row[:, z * feats : (z + 1) * feats]
    rows = (
        (bo, bd, g1, s1, g2, s2),
        (biases[2:3], biases[3:4], gains[0:1], shifts[0:1], gains[1:2], shifts[1:2]),
    )
    for net, up in enumerate((bu, flat(inner))):
        for slot, row in enumerate(rows[net]):
            vecs[net, slot] = row
        for r in range(4):
            vecs[net, V_UP + r] = up[:, r * width : (r + 1) * width]


def table(vectors, tutor_vectors, line):
    width = vectors[0].shape[0]
    return pl.pallas_call(
        table_kernel,
        out_shape=(
            jax.ShapeDtypeStruct((2, 2, line, 1, width // line), F32),
            jax.ShapeDtypeStruct((2, 10, 1, width), F32),
        ),
        in_specs=[VM] * 13,
        out_specs=(VM,) * 2,
        compiler_params=params(),
        cost_estimate=cost(1e5, 2e5),
        name="table",
    )(*vectors, *tutor_vectors)


def load_tokens(info, xs, pieces, sem):
    core = info[I_CORE]
    for k, piece in enumerate(pieces):
        for j in range(2):
            spot = jnp.where(j == 0, core, 1 - core)
            pltpu.make_async_copy(piece.at[j], xs.at[info[I_RING + k], spot], sem).start()


def load_rows(info, ws, own, sib, net, sem):
    core = info[I_CORE]
    for slot in range(3):
        pltpu.make_async_copy(own.at[net, slot], ws.at[slot, core], sem).start()
        pltpu.make_async_copy(sib.at[net, slot], ws.at[slot, 1 - core], sem).start()


def attend_kernel(student, info, *refs):
    pieces, refs = refs[:4], refs[4:]
    own, sib, heads_bias, clip = refs[:4]
    refs = refs[4:]
    net = 0 if student else 1
    if student:
        out, qkv_out, lse_out, ctx_out, xs, ws, qs, ks, vt, ct, low, sems = refs
    else:
        _, out, xs, ws, qs, ks, vt, ct, low, sems = refs
    load_tokens(info, xs, pieces, sems.at[0])
    load_rows(info, ws, own, sib, net, sems.at[1])
    line, _, half, width = xs.shape
    block = 2 * half
    feats = qs.shape[1]
    total = qs.shape[0]
    heads = feats // DH
    place = info[I_Z]
    length = info[I_LEN]
    bq_row, bv_row = heads_bias[net, 0, place], heads_bias[net, 1, place]
    wait_all(xs, sems.at[0])
    wait_all(ws, sems.at[1])

    def project(b, carry):
        rows = pl.ds(pl.multiple_of(b * block, block), block)
        x = xs[b].reshape(block, width)
        if student:
            lim = clip[...]
            x = jnp.clip(x.astype(F32), -lim, lim).astype(BF16)
        q = (dims(x, ws[0].reshape(feats, width), 1, 1) + bq_row).astype(BF16)
        k = dims(x, ws[1].reshape(feats, width), 1, 1).astype(BF16)
        v = (dims(x, ws[2].reshape(feats, width), 1, 1) + bv_row).astype(BF16)
        q = q * jnp.asarray(DH ** (-0.5), BF16)
        qs[rows] = q
        ks[rows] = k
        vt[:, rows] = v.astype(F32).T.astype(BF16)
        if student:
            qkv_out[0, rows] = q
            qkv_out[1, rows] = k
            qkv_out[2, rows] = v
        return carry

    lax.fori_loop(0, line, project, 0)
    fill = jnp.where(
        lax.broadcasted_iota(jnp.int32, (total, 1), 0) < length, 0.0, NEG_FILL
    ).astype(F32)
    lane_head = lax.broadcasted_iota(jnp.int32, (1, feats), 1) // DH

    def mix(b, carry):
        rows = pl.ds(pl.multiple_of(b * block, block), block)
        q = qs[rows]
        for h in range(heads):
            q_h = jnp.where(lane_head == h, q, jnp.zeros_like(q))
            scores = dims(ks[...], q_h, 1, 1) + fill
            top = jnp.max(scores, axis=0, keepdims=True)
            weight = jnp.exp(scores - top)
            mass = jnp.sum(weight, axis=0, keepdims=True)
            head = slice(h * DH, (h + 1) * DH)
            mixed = dims(vt[head], weight.astype(BF16), 1, 0) * (1.0 / mass)
            ct[head, rows] = mixed
            if student:
                lse_out[h : h + 1, rows] = top + jnp.log(mass)
        return carry

    lax.fori_loop(0, line, mix, 0)
    for b in range(line):
        low[b] = ct[:, b * block : (b + 1) * block].astype(BF16)
        pltpu.make_async_copy(low.at[b], out.at[b, net], sems.at[2 + b]).start()
    if student:
        ctx_out[...] = ct[...]
    for b in range(line):
        pltpu.make_async_copy(low.at[b], out.at[b, net], sems.at[2 + b]).wait()


def attend(info, pieces, own, sib, heads_bias, clip, both=None):
    _, half, width = pieces[0].shape
    line = len(pieces)
    total = line * 2 * half
    rows = own.shape[2]
    feats = 2 * rows
    student = both is None
    outs = [jax.ShapeDtypeStruct((line, 2, feats, 2 * half), BF16)]
    if student:
        outs += [
            jax.ShapeDtypeStruct((3, total, feats), BF16),
            jax.ShapeDtypeStruct((8, total), F32),
            jax.ShapeDtypeStruct((feats, total), F32),
        ]
    return pl.pallas_call(
        functools.partial(attend_kernel, student),
        out_shape=tuple(outs),
        in_specs=[SM] + [ANY] * 6 + [VM] * 2 + ([] if student else [ANY]),
        out_specs=(ANY,) + (VM,) * (len(outs) - 1),
        scratch_shapes=[
            pltpu.VMEM((line, 2, half, width), BF16),
            pltpu.VMEM((3, 2, rows, width), BF16),
            pltpu.VMEM((total, feats), BF16),
            pltpu.VMEM((total, feats), BF16),
            pltpu.VMEM((feats, total), BF16),
            pltpu.VMEM((feats, total), F32),
            pltpu.VMEM((line, feats, 2 * half), BF16),
            pltpu.SemaphoreType.DMA((2 + line,)),
        ],
        input_output_aliases={} if student else {9: 0},
        compiler_params=params(),
        cost_estimate=cost(6e9, 4e6, 3e6),
        name="attend_student" if student else "attend_tutor",
    )(info, *pieces, own, sib, heads_bias, clip, *([] if student else [both]))


def attend_back_kernel(info, *refs):
    pieces, refs = refs[:4], refs[4:]
    (own, sib, clip, qkv, lse, ctx, dctx, part0, part1, part2, part3, keep, send) = refs[:13]
    (xs, ws, kt, dct, dq, dk, dv, sems) = refs[13:]
    parts = (part0, part1, part2, part3)
    load_tokens(info, xs, pieces, sems.at[0])
    load_rows(info, ws, own, sib, 0, sems.at[1])
    line, _, half, width = xs.shape
    block = 2 * half
    total, feats = dk.shape
    heads = feats // DH
    core = info[I_CORE]
    length = info[I_LEN]
    lim = clip[...]
    for b in range(line):
        cols = slice(b * block, (b + 1) * block)
        kt[:, cols] = qkv[1, cols].astype(F32).T.astype(BF16)
        dct[:, cols] = dctx[b].astype(F32)
    dk[...] = jnp.zeros_like(dk)
    dv[...] = jnp.zeros_like(dv)
    fill = jnp.where(
        lax.broadcasted_iota(jnp.int32, (total, 1), 0) < length, 0.0, NEG_FILL
    ).astype(F32)
    lane_head = lax.broadcasted_iota(jnp.int32, (1, feats), 1) // DH
    row_head = lax.broadcasted_iota(jnp.int32, (feats, 1), 0) // DH

    def body(b, carry):
        rows = pl.ds(pl.multiple_of(b * block, block), block)
        q = qkv[0, rows]
        g = dctx[b]
        dk_add = dv_add = None
        for h in range(heads):
            head = slice(h * DH, (h + 1) * DH)
            q_h = jnp.where(lane_head == h, q, jnp.zeros_like(q))
            g_h = jnp.where(row_head == h, g, jnp.zeros_like(g))
            delta = jnp.sum(dct[head, rows] * ctx[head, rows], axis=0, keepdims=True)
            probs = jnp.exp(dims(qkv[1], q_h, 1, 1) + fill - lse[h : h + 1, rows])
            dprobs = dims(qkv[2], g_h, 1, 0)
            dscores = (probs * (dprobs - delta)).astype(BF16)
            dv_h = dims(probs.astype(BF16), g_h, 1, 1)
            dk_h = dims(dscores, q_h, 1, 0)
            dk_add = dk_h if dk_add is None else dk_add + dk_h
            dv_add = dv_h if dv_add is None else dv_add + dv_h
            dq[head, rows] = dims(kt[head], dscores, 1, 0) * (DH ** (-0.5))
        dk[...] += dk_add
        dv[...] += dv_add
        return carry

    lax.fori_loop(0, line, body, 0)
    wait_all(xs, sems.at[0])
    wait_all(ws, sems.at[1])
    dq_t = dq[...].astype(BF16)
    dq_low = dq_t.astype(F32).T.astype(BF16)
    dk_low = dk[...].astype(BF16)
    dv_low = dv[...].astype(BF16)
    dk_t = dk_low.astype(F32).T.astype(BF16)
    dv_t = dv_low.astype(F32).T.astype(BF16)
    qkv_flat = [ws[slot].reshape(feats, width) for slot in range(3)]
    for k in range(line):
        spot = info[I_RING + k]
        rows = pl.ds(pl.multiple_of(spot * block, block), block)
        dk_rows = dk[rows].astype(BF16)
        dv_rows = dv[rows].astype(BF16)
        dq_rows = dq[:, rows].T.astype(BF16)
        parts[k][...] = (
            dims(dq_rows, qkv_flat[0], 1, 0)
            + dims(dk_rows, qkv_flat[1], 1, 0)
            + dims(dv_rows, qkv_flat[2], 1, 0)
        ).astype(BF16)
    grads = []
    for low_t in (dq_t, dk_t, dv_t):
        acc = None
        for b in range(line):
            x = jnp.clip(xs[b].reshape(block, width).astype(F32), -lim, lim).astype(BF16)
            one = dims(low_t[:, b * block : (b + 1) * block], x, 1, 0)
            acc = one if acc is None else acc + one
        grads.append(acc)
    rows = feats // 2
    bias_q = jnp.sum(dq_low.astype(F32), axis=0, keepdims=True)
    bias_v = jnp.sum(dv_low.astype(F32), axis=0, keepdims=True)
    for rel, ref in ((0, keep), (1, send)):
        for c in range(2):

            @pl.when((core if rel == 0 else 1 - core) == c)
            def _():
                for slot, grad in enumerate(grads):
                    ref[slot * rows : (slot + 1) * rows] = grad[c * rows : (c + 1) * rows].astype(
                        ref.dtype
                    )
                tail = jnp.concatenate(
                    [
                        bias_q[:, c * rows : (c + 1) * rows],
                        bias_v[:, c * rows : (c + 1) * rows],
                        jnp.zeros((1, width - 2 * rows), F32),
                    ],
                    axis=1,
                )
                ref[3 * rows :] = jnp.broadcast_to(tail, (16, width)).astype(ref.dtype)


def attend_back(info, pieces, own, sib, clip, qkv, lse, ctx, dctx):
    _, half, width = pieces[0].shape
    line = len(pieces)
    total = line * 2 * half
    rows = own.shape[2]
    feats = 2 * rows
    part = jax.ShapeDtypeStruct((2 * half, width), BF16)
    grad = jax.ShapeDtypeStruct((3 * rows + 16, width), BF16)
    return pl.pallas_call(
        attend_back_kernel,
        out_shape=(part,) * 4 + (grad, grad),
        in_specs=[SM] + [ANY] * 6 + [VM] * 5,
        out_specs=(VM,) * 6,
        scratch_shapes=[
            pltpu.VMEM((line, 2, half, width), BF16),
            pltpu.VMEM((3, 2, rows, width), BF16),
            pltpu.VMEM((feats, total), BF16),
            pltpu.VMEM((feats, total), F32),
            pltpu.VMEM((feats, total), F32),
            pltpu.VMEM((total, feats), F32),
            pltpu.VMEM((total, feats), F32),
            pltpu.SemaphoreType.DMA((2,)),
        ],
        compiler_params=params(),
        cost_estimate=cost(12e9, 6e6, 3e6),
        name="attend_back",
    )(info, *pieces, own, sib, clip, qkv, lse, ctx, dctx)


V_OUT, V_DOWN, V_G1, V_S1, V_G2, V_S2, V_UP = 0, 1, 2, 3, 4, 5, 6
S_OUT, S_DOWN, S_G1, S_S1, S_G2, S_S2, S_UP = 0, 1, 2, 3, 4, 5, 6
PAD = 16


def norm_parts(v):
    centre = v - jnp.mean(v, axis=-1, keepdims=True)
    inv = lax.rsqrt(jnp.mean(centre * centre, axis=-1, keepdims=True) + NORM_EPS)
    return centre * inv, inv


def norm_back(dnormed, normed, inv):
    return inv * (
        dnormed
        - jnp.mean(dnormed, axis=-1, keepdims=True)
        - normed * jnp.mean(dnormed * normed, axis=-1, keepdims=True)
    )


def turned(v):
    return v.T.astype(BF16)


def middle_kernel(info, own, sib, *refs):
    chunks, refs = refs[:26], refs[26:]
    (x_own, ctx, vecs) = refs[:3]
    (out_keep, out_send, dfirst_keep, dctx_out) = refs[3:7]
    grads = refs[7:15]
    (w_up, w_dn, w_out, gate_pre, lower, gup, gdn, sums, base, aim, acc, sems) = refs[15:]
    core, rep, place, length = info[I_CORE], info[I_REP], info[I_Z], info[I_LEN]
    _, groups, quarters, rows, width = w_up.shape
    tokens = ctx.shape[3]
    line = groups // 2
    hidden = groups * rows
    half = rows // 2

    def place_piece(src, first, last, r, g):
        fields = (
            (0, rows, lambda: w_up.at[0, g, r], 0),
            (rows, 2 * rows, lambda: w_dn.at[0, r, g], 1),
            (2 * rows, 3 * rows, lambda: w_up.at[1, g, r], 2),
            (3 * rows, 4 * rows, lambda: w_dn.at[1, r, g], 3),
            (4 * rows, 4 * rows + half, lambda: w_out.at[r // 2, g, lax.rem(r, 2)], 4),
        )
        for lo, hi, dst, sem in fields:
            if first <= lo and hi <= last:
                pltpu.make_async_copy(
                    src.at[pl.ds(lo - first, hi - lo)], dst(), sems.at[sem]
                ).start()

    piece = 4 * rows + half
    for rel, ref in ((0, own), (1, sib)):
        member = 2 * place + (core if rel == 0 else 1 - core)
        for r in range(quarters):
            place_piece(ref.at[r], 0, piece, r, member)
    for k in range(1, line):
        for rel in range(2):
            member = 2 * info[I_RING + k] + (core if rel == 0 else 1 - core)
            got = chunks[(k - 1) * 8 + rel * (4 if k < line - 1 else 5) :]
            for far in range(3):
                place_piece(got[far], 0, piece, rep ^ far, member)
            if k < line - 1:
                place_piece(got[3], 0, piece, rep ^ 3, member)
            else:
                place_piece(got[3], 0, 2 * rows, rep ^ 3, member)
                place_piece(got[4], 2 * rows, piece, rep ^ 3, member)

    wait_all(w_out, sems.at[4])
    x_low = jnp.concatenate(
        [x_own[jnp.where(core == j, 0, 1)] for j in range(2)], axis=0
    ).astype(F32)

    def row(net, which):
        return vecs[net, which]

    def context_of(net):
        flat = jnp.concatenate([ctx[zb, net] for zb in range(line)], axis=0)
        return flat, flat.astype(F32).T.astype(BF16)

    def upper(net, ctx):
        first = (
            x_low + dims(ctx, w_out[net].reshape(width, width), 1, 1) + row(net, V_OUT)
        )
        normed, inv = norm_parts(first)
        return normed, inv, normed * row(net, V_G1) + row(net, V_S1)

    def lower_half(net, upper_in, keep):
        acc[...] = jnp.zeros_like(acc)

        def step(r, carry):
            gate = (
                dims(upper_in, w_up[net, pl.ds(2 * r, 2)].reshape(hidden, width), 1, 1)
                + vecs[net, V_UP + r]
            )
            low = gelu_exact(gate).astype(BF16)
            if keep:
                gate_pre[r] = gate
                lower[r] = low
            acc[...] += dims(low, w_dn[net, r].reshape(width, hidden), 1, 1)
            return carry

        lax.fori_loop(0, quarters, step, 0)
        return acc[...]

    _, ctx_tutor = context_of(1)
    _, _, first_norm = upper(1, ctx_tutor)
    ctx_flat, ctx_low = context_of(0)
    normed_one, inv_one, first_norm_s = upper(0, ctx_low)
    base[...] = first_norm_s
    wait_all(w_up.at[1], sems.at[2])
    wait_all(w_dn.at[1], sems.at[3])
    second = first_norm + lower_half(1, first_norm.astype(BF16), False) + row(1, V_DOWN)
    normed, _ = norm_parts(second)
    aim[...] = normed * row(1, V_G2) + row(1, V_S2)

    wait_all(w_up.at[0], sems.at[0])
    wait_all(w_dn.at[0], sems.at[1])
    upper_in = first_norm_s.astype(BF16)
    second = base[...] + lower_half(0, upper_in, True) + row(0, V_DOWN)
    normed_two, inv_two = norm_parts(second)
    output = normed_two * row(0, V_G2) + row(0, V_S2)
    aim[...] = output - aim[...]
    acc[...] = output

    def part_of(ref, j):
        return ref[pl.ds(pl.multiple_of(j * (tokens // 2), tokens // 2), tokens // 2)]

    out_keep[...] = part_of(acc, core).astype(BF16)
    out_send[...] = part_of(acc, 1 - core).astype(BF16)
    where = place * tokens + lax.broadcasted_iota(jnp.int32, (tokens, 1), 0)
    kept = jnp.where(where < length, 1.0, 0.0).astype(F32)
    dout = kept * aim[...]
    sums[...] = jnp.zeros_like(sums)
    error = 0.5 * jnp.sum(dout * dout)
    sums[S_G2] = jnp.sum(dout * normed_two, axis=0, keepdims=True)
    sums[S_S2] = jnp.sum(dout, axis=0, keepdims=True)
    dsecond = norm_back(dout * row(0, V_G2), normed_two, inv_two)
    sums[S_DOWN] = jnp.sum(dsecond, axis=0, keepdims=True)
    g_down = dsecond.astype(BF16)
    g_down_t = turned(dsecond)
    acc[...] = dsecond

    def back(r, carry):
        low = lower[r]
        gdn[r, :, 0:rows] = dims(g_down_t, low, 1, 0).astype(BF16).reshape(groups, rows, hidden)
        dlower = dims(g_down, w_dn[0, r].reshape(width, hidden), 1, 0)
        gate = gate_pre[r]
        slope = 0.5 * (1.0 + lax.erf(gate * 0.7071067811865476)) + gate * (
            0.3989422804014327 * jnp.exp(-0.5 * gate * gate)
        )
        dgate = dlower * slope
        sums[S_UP + r] = jnp.sum(dgate, axis=0, keepdims=True)
        gup_r = dims(turned(dgate), upper_in, 1, 0).astype(BF16)
        gup[pl.ds(2 * r, 2), :, 0:rows] = gup_r.reshape(2, quarters, rows, width)
        acc[...] += dims(
            dgate.astype(BF16), w_up[0, pl.ds(2 * r, 2)].reshape(hidden, width), 1, 0
        )
        return carry

    lax.fori_loop(0, quarters, back, 0)
    dfirst = acc[...]
    sums[S_G1] = jnp.sum(dfirst * normed_one, axis=0, keepdims=True)
    sums[S_S1] = jnp.sum(dfirst, axis=0, keepdims=True)
    dsum = norm_back(dfirst * row(0, V_G1), normed_one, inv_one)
    sums[S_OUT] = jnp.sum(dsum, axis=0, keepdims=True)
    dfirst_keep[...] = dsum
    g_out = dsum.astype(BF16)
    dctx = turned(dims(g_out, w_out[0].reshape(width, width), 1, 0))
    dctx_out[...] = dctx.reshape(dctx_out.shape)
    gout = dims(turned(dsum), ctx_flat, 1, 1).reshape(groups, quarters, rows // quarters, width)
    number = rep * groups + 2 * place + core
    high = error.astype(BF16).astype(F32)
    middle_part = (error - high).astype(BF16).astype(F32)
    lane = lax.broadcasted_iota(jnp.int32, (1, width), 1)
    digits = jnp.zeros((1, width), F32)
    for slot, digit in enumerate((high, middle_part, error - high - middle_part)):
        digits = jnp.where(lane == 3 * number + slot, digit, digits)
    ups = jnp.concatenate([sums[S_UP + r] for r in range(quarters)], axis=1)
    slim = rows // quarters
    for g in range(groups):
        own_rows = [sums[which][:, g * rows : (g + 1) * rows] for which in range(6)]
        vectors = jnp.concatenate(
            [
                jnp.concatenate(own_rows, axis=0),
                jnp.zeros((6, width - rows), F32),
            ],
            axis=1,
        )
        inner = jnp.concatenate(
            [
                ups[:, g * 4 * rows : (g + 1) * 4 * rows],
                jnp.zeros((1, width - 4 * rows), F32),
            ],
            axis=1,
        )
        tail = jnp.concatenate([vectors, inner, digits], axis=0)
        for r in range(quarters):
            gup[g, r, rows:] = gout[g, r, :PAD].astype(BF16)
            gdn[r, g, rows:] = jnp.concatenate([gout[g, r, PAD:slim], tail], axis=0).astype(BF16)

    for rel in range(2):
        a_keep, a_send, b_keep, b_send = grads[rel * 4 : rel * 4 + 4]
        for far in range(4):
            r = rep ^ far
            for k in range(line):
                g = 2 * info[I_RING + k] + (core if rel == 0 else 1 - core)
                a_ref = a_send if far & 1 else a_keep
                b_ref = b_send if far & 2 else b_keep
                pltpu.make_async_copy(
                    gup.at[g, r], a_ref.at[far >> 1, k], sems.at[5 + rel * 4 + (far & 1)]
                ).start()
                pltpu.make_async_copy(
                    gdn.at[r, g], b_ref.at[far & 1, k], sems.at[7 + rel * 4 + (far >> 1)]
                ).start()
    for rel in range(2):
        for slot in range(4):
            ref = grads[rel * 4 + slot]
            wait_all(ref, sems.at[5 + rel * 4 + slot])


def middle(info, own, sib, chunks, x_own, ctx, vecs):
    line, _, feats, tokens = ctx.shape
    width = line * feats
    quarters = own.shape[0]
    groups = 2 * line
    rows = width // groups
    half = (tokens // 2, width)
    part = jax.ShapeDtypeStruct((2, line, rows + PAD, width), BF16)
    outs = (
        jax.ShapeDtypeStruct(half, BF16),
        jax.ShapeDtypeStruct(half, BF16),
        jax.ShapeDtypeStruct((tokens, width), F32),
        jax.ShapeDtypeStruct((line, feats, tokens), BF16),
    ) + (part,) * 8
    return pl.pallas_call(
        middle_kernel,
        out_shape=outs,
        in_specs=[SM] + [ANY] * 28 + [VM] * 3,
        out_specs=(VM,) * 4 + (ANY,) * 8,
        scratch_shapes=[
            pltpu.VMEM((2, groups, quarters, rows, width), BF16),
            pltpu.VMEM((2, quarters, groups, rows, width), BF16),
            pltpu.VMEM((2, groups, 2, rows // 2, width), BF16),
            pltpu.VMEM((quarters, tokens, width), F32),
            pltpu.VMEM((quarters, tokens, width), BF16),
            pltpu.VMEM((groups, quarters, rows + PAD, width), BF16),
            pltpu.VMEM((quarters, groups, rows + PAD, width), BF16),
            pltpu.VMEM((S_UP + quarters, 1, width), F32),
            pltpu.VMEM((tokens, width), F32),
            pltpu.VMEM((tokens, width), F32),
            pltpu.VMEM((tokens, width), F32),
            pltpu.SemaphoreType.DMA((13,)),
        ],
        compiler_params=params(),
        cost_estimate=cost(15e9, 30e6, 4e6),
        name="middle",
    )(info, own, sib, *chunks, x_own, ctx, vecs)


def finish_kernel(entries, info, *refs):
    pieces, refs = refs[:4], refs[4:]
    grad_qkv, up, down, out, gq, gk, gv, loss, bq, bv, bu = refs[:11]
    others, scr, sem = refs[11:17], refs[17], refs[18]
    rep = info[I_REP]
    for far, ref in enumerate(pieces):
        pltpu.make_async_copy(ref, scr.at[rep ^ far], sem.at[0]).start()
    rows, width = gq.shape
    for slot, ref in enumerate((gq, gk, gv)):
        ref[...] = grad_qkv[slot * rows : (slot + 1) * rows].astype(F32)
    bias = grad_qkv[3 * rows :].astype(F32)
    bq[...] = bias[0, :rows]
    bv[...] = bias[0, rows : 2 * rows]
    wait_all(scr, sem.at[0])
    slim = rows // len(pieces)
    high = rows + PAD
    for r in range(len(pieces)):
        up[r * rows : (r + 1) * rows] = scr[r, 0:rows].astype(F32)
        down[:, r * width : (r + 1) * width] = scr[r, high : high + rows].astype(F32)
        out[r * slim : r * slim + PAD] = scr[r, rows:high].astype(F32)
        last = scr[r, high + rows :].astype(F32)
        out[r * slim + PAD : (r + 1) * slim] = last[: slim - PAD]
        if r == 0:
            tail = last[slim - PAD :]
            for slot, ref in enumerate(others):
                ref[...] = tail[slot, :rows]
            bu[...] = tail[S_UP, : 4 * rows]
            loss[...] = jnp.full((1, 1), jnp.sum(tail[S_UP + 1 : S_UP + 2]) / entries, F32)


def finish(info, pieces, grad_qkv, entries):
    high, width = pieces[0].shape
    rows = high // 2 - PAD
    small = jax.ShapeDtypeStruct((rows, width), F32)
    vector = jax.ShapeDtypeStruct((rows,), F32)
    return pl.pallas_call(
        functools.partial(finish_kernel, entries),
        out_shape=(
            jax.ShapeDtypeStruct((4 * rows, width), F32),
            jax.ShapeDtypeStruct((rows, 4 * width), F32),
            small,
            small,
            small,
            small,
            jax.ShapeDtypeStruct((1, 1), F32),
            vector,
            vector,
            jax.ShapeDtypeStruct((4 * rows,), F32),
        )
        + (vector,) * 6,
        in_specs=[SM] + [ANY] * 4 + [VM],
        out_specs=(VM,) * 16,
        scratch_shapes=[
            pltpu.VMEM((4, high, width), BF16),
            pltpu.SemaphoreType.DMA((1,)),
        ],
        compiler_params=params(),
        cost_estimate=cost(1e6, 8e6),
        name="finish",
    )(info, *pieces, grad_qkv)


def add_low(*terms):
    total = terms[0].astype(F32)
    for term in terms[1:]:
        total = total + term.astype(F32)
    return total.astype(BF16)


def after(value, *others):
    return lax.optimization_barrier((value,) + others)[0]


def line_shards(line, *args):
    hidden_in, seq_lengths = args[0], args[1]
    latents, vectors, clip_input = args[2:8], args[8:17], args[17]
    tutors, tutor_vectors = args[18:24], args[24:28]
    micro_count, _, local_rows, width = hidden_in.shape
    rows = latents[0].shape[0]
    rep, grp = lax.axis_index("rep"), lax.axis_index("grp")
    core = lax.rem(grp, 2)
    ring = z_ring(line)

    def over_z(x, pairs):
        return lax.ppermute(x, "grp", [(2 * a + c, 2 * b + c) for a, b in pairs for c in range(2)])

    def next_z(x):
        return over_z(x, [(ring[i], ring[(i + 1) % line]) for i in range(line)])

    def swap(x):
        return lax.ppermute(x, "grp", [(g, g ^ 1) for g in range(2 * line)])

    def to_rep(x, bit):
        return lax.ppermute(x, "rep", [(i, i ^ bit) for i in range(4)])

    def to_tokens(x):
        groups = [[2 * z + c for z in range(line)] for c in range(2)]
        return lax.all_to_all(x, "grp", 0, 0, axis_index_groups=groups, tiled=True)

    scalars = [
        [g % 2, 0, g // 2, 0] + [ring[(ring.index(g // 2) - k) % line] for k in range(line)]
        for g in range(2 * line)
    ]
    lane = jnp.arange(4 + line, dtype=jnp.int32)
    info = jnp.sum(
        jnp.where(jnp.arange(2 * line)[:, None] == grp, jnp.asarray(scalars, jnp.int32), 0), axis=0
    )
    length = jnp.where(core == 0, seq_lengths[0, 0], seq_lengths[1, 0])
    info = jnp.where(lane == I_REP, rep, jnp.where(lane == I_LEN, length, info)).astype(jnp.int32)
    clip = clip_input.reshape(1, width)
    tokens = hidden_in[:, 0]
    keep = jnp.where(core == 0, tokens[0], tokens[1])
    swapped = swap(jnp.where(core == 0, tokens[1], tokens[0]))
    x_own = jnp.stack([keep, swapped])
    x_1 = next_z(x_own)
    qkv_own, own, piece = pack(after(info, x_own), latents, tutors)
    heads_bias, vecs = table(vectors, tutor_vectors, line)

    def to_sides(value):
        return [value, to_rep(value, 1), to_rep(value, 2)]

    piece_1 = next_z(piece)
    qkv_sib = swap(qkv_own)
    sib = swap(own)
    x_2 = next_z(after(x_1, sib, qkv_sib))
    x_3 = next_z(after(x_2, piece_1))
    piece_2 = next_z(piece_1)
    got_1 = to_sides(piece_1)
    tokens_in = [x_own, x_1, x_2, x_3]
    mixed, qkv, lse, ctx = attend(info, tokens_in, qkv_own, qkv_sib, heads_bias, clip)
    mixed = after(mixed, *got_1, piece_2)
    piece_2 = after(piece_2, mixed)
    piece_3 = next_z(piece_2)
    got_2 = to_sides(piece_2)
    got_1.append(to_rep(after(got_1[1], mixed), 2))
    (mixed,) = attend(info, tokens_in, qkv_own, qkv_sib, heads_bias, clip, mixed)
    got_2.append(to_rep(after(got_2[2], mixed), 1))
    got_3 = to_sides(after(piece_3, mixed))
    mixed = to_tokens(mixed)
    got_3.append(to_rep(after(got_3[1][: 2 * rows], mixed), 2))
    got_3.append(to_rep(after(got_3[2][2 * rows :], mixed), 1))
    chunks = []
    for got in (got_1, got_2, got_3):
        chunks += got + [swap(after(one, got_3[0])) for one in got]
    (
        out_keep,
        out_send,
        dfirst,
        dctx,
        a_keep,
        a_send,
        b_keep,
        b_send,
        a_keep_sib,
        a_send_sib,
        b_keep_sib,
        b_send_sib,
    ) = middle(info, own, sib, chunks, x_own, mixed, vecs)

    def by_micro(kept, got):
        return jnp.where(core == 0, jnp.stack([kept, got]), jnp.stack([got, kept]))[:, None]

    dctx = to_tokens(dctx)
    a_out = add_low(a_send, swap(a_send_sib))
    b_out = add_low(b_send, swap(b_send_sib))
    a_in, b_in = to_rep(a_out, 1), to_rep(b_out, 2)
    a_keep_sib, b_keep_sib = swap(a_keep_sib), swap(b_keep_sib)
    part0, part1, part2, part3, gqkv, gqkv_sib = attend_back(
        info, tokens_in, qkv_own, qkv_sib, clip, qkv, lse, ctx, after(dctx, a_out, b_out)
    )
    moving_1 = next_z(part1)
    gqkv_sib = swap(gqkv_sib)
    a_next = to_rep(add_low(a_keep[1], a_keep_sib[1], after(a_in, part1)[1]), 2)
    b_next = to_rep(add_low(b_keep[1], b_keep_sib[1], after(b_in, part1)[1]), 1)
    moving_2 = next_z(after(add_low(moving_1, part2), a_in, b_in))
    both = jnp.concatenate(
        [
            add_low(a_keep[0], a_keep_sib[0], a_in[0], a_next),
            add_low(b_keep[0], b_keep_sib[0], b_in[0], b_next),
        ],
        axis=1,
    )
    moving_3 = next_z(add_low(moving_2, part3))
    grads_1 = next_z(both[1])
    layer_out = by_micro(out_keep, swap(after(out_send, moving_2)))
    gqkv = add_low(gqkv, gqkv_sib)
    gqkv = add_low(gqkv, to_rep(after(gqkv, moving_2), 1))
    grads_2 = next_z(after(add_low(grads_1, both[2]), gqkv))
    gqkv = add_low(gqkv, to_rep(gqkv, 2))
    grads_3 = next_z(after(add_low(grads_2, both[3]), gqkv))
    grads = add_low(grads_3, both[0])
    quarter = to_sides(grads) + [to_rep(grads, 3)]
    entries = micro_count * 4 * 2 * line * local_rows * width
    ends = finish(info, quarter, gqkv, entries)
    grad_up, grad_down, grad_out, grad_q, grad_k, grad_v, loss, bq, bv, bu = ends[:10]
    bo, bd, g1, s1, g2, s2 = ends[10:]

    hidden_tokens = jnp.where(core == 0, x_own, x_own[::-1])
    hidden_tokens = hidden_tokens.reshape(2 * local_rows, width).astype(F32)
    dxin = moving_3.astype(F32) + part0.astype(F32)
    grad_input = dfirst + jnp.where(jnp.abs(hidden_tokens) < clip, dxin, 0.0)
    halves = grad_input.reshape(2, local_rows, width)
    grad_input = by_micro(
        jnp.where(core == 0, halves[0], halves[1]),
        swap(jnp.where(core == 0, halves[1], halves[0])),
    )
    return (
        layer_out,
        loss.reshape(()),
        grad_input,
        grad_q,
        grad_k,
        grad_v,
        grad_out,
        grad_up,
        grad_down,
        bq,
        bv,
        bo,
        bu,
        bd,
        g1,
        s1,
        g2,
        s2,
    )


def fits_line(mesh, args):
    line = mesh.shape["grp"] // 2
    micro_count, seq_count, total, width = args[0].shape
    hidden = args[6].shape[0]
    return (
        mesh.shape["rep"] == 4
        and line == 4
        and H % line == 0
        and micro_count == 2
        and seq_count == mesh.shape["rep"]
        and total == 8 * 128
        and hidden == 4 * width
    )


def solution(mesh):
    def mapped(body):
        return jax.shard_map(
        body,
        mesh=mesh,
        in_specs=(
            P(None, "rep", "grp", None),
            P(None, "rep"),
            P("grp", None),
            P("grp", None),
            P("grp", None),
            P("grp", None),
            P("grp", None),
            P("grp", None),
            P(),
            P(),
            P(),
            P(),
            P(),
            P(),
            P(),
            P(),
            P(),
            P(),
            P("grp", None),
            P("grp", None),
            P("grp", None),
            P("grp", None),
            P("grp", None),
            P("grp", None),
            P(),
            P(),
            P(),
            P(),
        ),
        out_specs=(
            P(None, "rep", "grp", None),
            P(),
            P(None, "rep", "grp", None),
            P("grp", None),
            P("grp", None),
            P("grp", None),
            P("grp", None),
            P("grp", None),
            P("grp", None),
            P("grp"),
            P("grp"),
            P("grp"),
            P("grp"),
            P("grp"),
            P("grp"),
            P("grp"),
            P("grp"),
            P("grp"),
        ),
        check_vma=False,
    )

    def step(*args):
        if fits_line(mesh, args):
            line = mesh.shape["grp"] // 2
            return mapped(functools.partial(line_shards, line))(*args)
        return mapped(shards)(*args)

    return step
```

```python
import functools

import jax
import jax.numpy as jnp
from jax import lax
from jax.experimental import pallas as pl
from jax.experimental.pallas import tpu as pltpu
from jax.sharding import PartitionSpec as P

H = 12
DH = 64


NEG_FILL = -1e30
NORM_EPS = 1e-05


def layer_norm(tensor, gain_row, shift_row):
    centre = tensor - jnp.mean(tensor, axis=-1, keepdims=True)
    spread = jnp.mean(centre * centre, axis=-1, keepdims=True)
    return centre * lax.rsqrt(spread + NORM_EPS) * gain_row + shift_row


def gelu_exact(tensor):
    return 0.5 * tensor * (1.0 + lax.erf(tensor * 0.7071067811865476))


def times_rows(operand, weight):
    return lax.dot_general(
        operand, weight, (((1,), (1,)), ((), ())), preferred_element_type=jnp.float32
    )


def binarize(latent_rows):
    magnitude = jnp.mean(jnp.abs(latent_rows), axis=1, keepdims=True)
    return (magnitude * jnp.sign(latent_rows)).astype(jnp.bfloat16)


def student_project(operand, latent):
    return times_rows(
        operand,
        binarize(
            lax.all_gather(latent.astype(jnp.bfloat16), "grp", axis=0, tiled=True).astype(
                jnp.float32
            )
        ),
    )


def teacher_project(operand, weight):
    return times_rows(operand, lax.all_gather(weight, "grp", axis=0, tiled=True))


def add_columns(grads_low, weight_rows):
    return jnp.dot(grads_low, weight_rows, preferred_element_type=jnp.float32)


def student_back(grads_low, latent):
    return add_columns(
        grads_low,
        binarize(
            lax.all_gather(latent.astype(jnp.bfloat16), "grp", axis=0, tiled=True).astype(
                jnp.float32
            )
        ),
    )


def weight_grad(grads_low, operand):
    return lax.dot_general(
        grads_low, operand, (((0,), (0,)), ((), ())), preferred_element_type=jnp.float32
    )


def head_scores(queries, keys):
    seq_count, query_rows = (queries.shape[0], queries.shape[1])
    key_rows = keys.shape[1]
    query_heads = queries.reshape(seq_count, query_rows, H, DH)
    key_heads = keys.reshape(seq_count, key_rows, H, DH)
    return jnp.einsum(
        "schd,snhd->shcn", query_heads, key_heads, preferred_element_type=jnp.float32
    ) * DH ** (-0.5)


def key_mask(lengths, first_row, key_rows):
    positions = first_row + jnp.arange(key_rows, dtype=jnp.int32)
    return (positions[None, :] < lengths[:, None])[:, None, None, :]


def in_blocks(block_step, state_in, pieces):
    total_rows = pieces[0].shape[1]
    block_rows = 512

    def scan_step(running, block_index):
        offset = block_index * block_rows
        sliced = tuple(
            (lax.dynamic_slice_in_dim(member, offset, block_rows, 1) for member in pieces)
        )
        return (block_step(running, sliced, offset), None)

    state_out, unused = lax.scan(
        scan_step, state_in, jnp.arange(total_rows // block_rows, dtype=jnp.int32)
    )
    return state_out


def attention_forward(queries, keys, values, lengths):
    seq_count, query_rows, width_all = queries.shape
    stat_shape = (seq_count, H, query_rows)

    def stat_step(state_in, pieces, first_row):
        row_top, row_sum = state_in
        key_part = pieces[0]
        scores = jnp.where(
            key_mask(lengths, first_row, key_part.shape[1]),
            head_scores(queries, key_part),
            NEG_FILL,
        )
        new_top = jnp.maximum(row_top, jnp.max(scores, axis=3))
        row_sum = row_sum * jnp.exp(row_top - new_top) + jnp.sum(
            jnp.exp(scores - new_top[..., None]), axis=3
        )
        return (new_top, row_sum)

    stat_init = (jnp.full(stat_shape, NEG_FILL, jnp.float32), jnp.zeros(stat_shape, jnp.float32))
    row_top, row_sum = in_blocks(
        stat_step, stat_init, (lax.all_gather(keys, "grp", axis=1, tiled=True),)
    )
    log_total = row_top + jnp.log(row_sum)
    head_shape = (seq_count, query_rows, H, DH)

    def mix_step(state_in, pieces, first_row):
        key_part, value_part = pieces
        key_rows = key_part.shape[1]
        scores = jnp.where(
            key_mask(lengths, first_row, key_rows), head_scores(queries, key_part), NEG_FILL
        )
        softmax_w = jnp.exp(scores - log_total[..., None])
        value_heads = value_part.reshape(seq_count, key_rows, H, DH)
        return state_in + jnp.einsum(
            "shcn,snhd->schd",
            softmax_w.astype(jnp.bfloat16),
            value_heads,
            preferred_element_type=jnp.float32,
        )

    context_heads = in_blocks(
        mix_step,
        jnp.zeros(head_shape, jnp.float32),
        (
            lax.all_gather(keys, "grp", axis=1, tiled=True),
            lax.all_gather(values, "grp", axis=1, tiled=True),
        ),
    )
    return (context_heads, log_total)


def query_grads(queries, keys, values, lengths, log_total, delta_heads, dcontext):
    seq_count, query_rows, width_all = queries.shape
    dcontext_heads = dcontext.reshape(seq_count, query_rows, H, DH)

    def query_grad_step(running, pieces, first_row):
        key_part, value_part = pieces
        key_rows = key_part.shape[1]
        scores = jnp.where(
            key_mask(lengths, first_row, key_rows), head_scores(queries, key_part), NEG_FILL
        )
        softmax_w = jnp.exp(scores - log_total[..., None])
        value_heads = value_part.reshape(seq_count, key_rows, H, DH)
        key_heads = key_part.reshape(seq_count, key_rows, H, DH)
        dweights = jnp.einsum(
            "schd,snhd->shcn", dcontext_heads, value_heads, preferred_element_type=jnp.float32
        )
        dscores = (softmax_w * (dweights - delta_heads[..., None])).astype(jnp.bfloat16)
        return running + jnp.einsum(
            "shcn,snhd->schd", dscores, key_heads, preferred_element_type=jnp.float32
        )

    zero_heads = jnp.zeros((seq_count, query_rows, H, DH), jnp.float32)
    folded = in_blocks(
        query_grad_step,
        zero_heads,
        (
            lax.all_gather(keys, "grp", axis=1, tiled=True),
            lax.all_gather(values, "grp", axis=1, tiled=True),
        ),
    )
    return (folded * DH ** (-0.5)).reshape(seq_count, query_rows, width_all)


def key_grads(queries, keys, values, lengths, log_rows, delta_rows, dcontext):
    seq_count, key_rows, width_all = keys.shape
    log_all, delta_all = (
        lax.all_gather(log_rows, "grp", axis=1, tiled=True),
        lax.all_gather(delta_rows, "grp", axis=1, tiled=True),
    )
    own_mask = key_mask(lengths, lax.axis_index("grp") * key_rows, key_rows)
    value_heads = values.reshape(seq_count, key_rows, H, DH)

    def key_grad_step(running, pieces, first_row):
        query_part, dcontext_part = pieces
        query_count = query_part.shape[1]
        log_part = jnp.transpose(
            lax.dynamic_slice_in_dim(log_all, first_row, query_count, 1), (0, 2, 1)
        )
        delta_part = jnp.transpose(
            lax.dynamic_slice_in_dim(delta_all, first_row, query_count, 1), (0, 2, 1)
        )
        scores = jnp.where(own_mask, head_scores(query_part, keys), NEG_FILL)
        softmax_w = jnp.exp(scores - log_part[..., None])
        dcontext_heads = dcontext_part.reshape(seq_count, query_count, H, DH)
        query_heads = query_part.reshape(seq_count, query_count, H, DH)
        dweights = jnp.einsum(
            "schd,snhd->shcn", dcontext_heads, value_heads, preferred_element_type=jnp.float32
        )
        dscores = (softmax_w * (dweights - delta_part[..., None])).astype(jnp.bfloat16)
        dkey_sum = running[0] + jnp.einsum(
            "shcn,schd->snhd", dscores, query_heads, preferred_element_type=jnp.float32
        )
        dvalue_sum = running[1] + jnp.einsum(
            "shcn,schd->snhd",
            softmax_w.astype(jnp.bfloat16),
            dcontext_heads,
            preferred_element_type=jnp.float32,
        )
        return (dkey_sum, dvalue_sum)

    zero_heads = jnp.zeros((seq_count, key_rows, H, DH), jnp.float32)
    dkey_sum, dvalue_sum = in_blocks(
        key_grad_step,
        (zero_heads, zero_heads),
        (
            lax.all_gather(queries, "grp", axis=1, tiled=True),
            lax.all_gather(dcontext, "grp", axis=1, tiled=True),
        ),
    )
    return (
        (dkey_sum * DH ** (-0.5)).reshape(seq_count, key_rows, width_all),
        dvalue_sum.reshape(seq_count, key_rows, width_all),
    )


def forward(hidden, lengths, project, vectors, clips):
    b_query, b_value, b_out, b_up, b_down, gain_one, shift_one, gain_two, shift_two = vectors
    seq_count = lengths.shape[0]
    query_rows = hidden.shape[0] // seq_count
    width_all = hidden.shape[1]
    entering = hidden if clips is None else jnp.clip(hidden, -clips[0], clips[0])
    inputs = entering.astype(jnp.bfloat16)
    queries = (
        (project(inputs, 0) + b_query)
        .astype(jnp.bfloat16)
        .reshape(seq_count, query_rows, width_all)
    )
    keys = project(inputs, 1).astype(jnp.bfloat16).reshape(seq_count, query_rows, width_all)
    values = (
        (project(inputs, 2) + b_value)
        .astype(jnp.bfloat16)
        .reshape(seq_count, query_rows, width_all)
    )
    context_heads, log_total = attention_forward(queries, keys, values, lengths)
    context_low = context_heads.reshape(hidden.shape).astype(jnp.bfloat16)
    first_sum = hidden + project(context_low, 3) + b_out
    first_norm = layer_norm(first_sum, gain_one, shift_one)
    upper_in = first_norm.astype(jnp.bfloat16)
    gate_pre = project(upper_in, 4) + b_up
    lower_in = gelu_exact(gate_pre).astype(jnp.bfloat16)
    second_sum = first_norm + project(lower_in, 5) + b_down
    output = layer_norm(second_sum, gain_two, shift_two)
    kept_values = (
        inputs,
        queries,
        keys,
        values,
        context_heads,
        log_total,
        context_low,
        first_sum,
        first_norm,
        upper_in,
        gate_pre,
        lower_in,
        second_sum,
    )
    return (output, kept_values)


def backward(grad_output, hidden, lengths, latents, vectors, clips, kept_values):
    (
        inputs,
        queries,
        keys,
        values,
        context_heads,
        log_total,
        context_low,
        first_sum,
        first_norm,
        upper_in,
        gate_pre,
        lower_in,
        second_sum,
    ) = kept_values
    w_query, w_key, w_value, w_out, w_up, w_down = latents
    gain_one, shift_one, gain_two, shift_two = (vectors[5], vectors[6], vectors[7], vectors[8])
    seq_count, query_rows, width_all = queries.shape
    unused, pull_two = jax.vjp(layer_norm, second_sum, gain_two, shift_two)
    dsecond, dgain_two, dshift_two = pull_two(grad_output)
    dsecond_low = dsecond.astype(jnp.bfloat16)
    grad_down = weight_grad(dsecond_low, lower_in)
    dlower = student_back(dsecond_low, w_down)
    unused, pull_gate = jax.vjp(gelu_exact, gate_pre)
    dgate = pull_gate(dlower)[0]
    dgate_low = dgate.astype(jnp.bfloat16)
    grad_up = weight_grad(dgate_low, upper_in)
    dupper = student_back(dgate_low, w_up)
    dfirst = dsecond + dupper
    unused, pull_one = jax.vjp(layer_norm, first_sum, gain_one, shift_one)
    dfirst_sum, dgain_one, dshift_one = pull_one(dfirst)
    dbranch_low = dfirst_sum.astype(jnp.bfloat16)
    grad_out = weight_grad(dbranch_low, context_low)
    dcontext = (
        student_back(dbranch_low, w_out)
        .astype(jnp.bfloat16)
        .reshape(seq_count, query_rows, width_all)
    )
    delta_rows = jnp.sum(
        dcontext.reshape(seq_count, query_rows, H, DH).astype(jnp.float32) * context_heads, axis=3
    )
    dqueries = query_grads(
        queries, keys, values, lengths, log_total, jnp.transpose(delta_rows, (0, 2, 1)), dcontext
    )
    dkeys, dvalues = key_grads(
        queries, keys, values, lengths, jnp.transpose(log_total, (0, 2, 1)), delta_rows, dcontext
    )
    all_rows = seq_count * query_rows
    dqueries_low = dqueries.reshape(all_rows, width_all).astype(jnp.bfloat16)
    dkeys_low = dkeys.reshape(all_rows, width_all).astype(jnp.bfloat16)
    dvalues_low = dvalues.reshape(all_rows, width_all).astype(jnp.bfloat16)
    grad_query = weight_grad(dqueries_low, inputs)
    grad_key = weight_grad(dkeys_low, inputs)
    grad_value = weight_grad(dvalues_low, inputs)
    dinputs = (
        student_back(dqueries_low, w_query)
        + student_back(dkeys_low, w_key)
        + student_back(dvalues_low, w_value)
    )
    unused, pull_input = jax.vjp(lambda tensor: jnp.clip(tensor, -clips[0], clips[0]), hidden)
    grad_hidden = dfirst_sum + pull_input(dinputs)[0]
    weight_parts = (grad_query, grad_key, grad_value, grad_out, grad_up, grad_down)
    vector_parts = (
        jnp.sum(dqueries_low.astype(jnp.float32), axis=0),
        jnp.sum(dvalues_low.astype(jnp.float32), axis=0),
        jnp.sum(dfirst_sum, axis=0),
        jnp.sum(dgate, axis=0),
        jnp.sum(dsecond, axis=0),
        dgain_one,
        dshift_one,
        dgain_two,
        dshift_two,
    )
    return (weight_parts, vector_parts, grad_hidden)


def shards(
    hidden_in,
    seq_lengths,
    latent_query,
    latent_key,
    latent_value,
    latent_out,
    latent_up,
    latent_down,
    bias_query,
    bias_value,
    bias_out,
    bias_up,
    bias_down,
    gain_first,
    shift_first,
    gain_second,
    shift_second,
    clip_input,
    teacher_query,
    teacher_key,
    teacher_value,
    teacher_out,
    teacher_up,
    teacher_down,
    teacher_biases,
    teacher_inner,
    teacher_gains,
    teacher_shifts,
):
    latents = (latent_query, latent_key, latent_value, latent_out, latent_up, latent_down)
    tutors = (teacher_query, teacher_key, teacher_value, teacher_out, teacher_up, teacher_down)
    vectors = (
        bias_query,
        bias_value,
        bias_out,
        bias_up,
        bias_down,
        gain_first,
        shift_first,
        gain_second,
        shift_second,
    )
    tutor_vectors = (
        teacher_biases[0],
        teacher_biases[1],
        teacher_biases[2],
        teacher_inner,
        teacher_biases[3],
        teacher_gains[0],
        teacher_shifts[0],
        teacher_gains[1],
        teacher_shifts[1],
    )
    clips = (clip_input,)
    micro_count, seq_count, local_rows, width_all = hidden_in.shape
    positions = lax.axis_index("grp") * local_rows + jnp.arange(local_rows, dtype=jnp.int32)

    def student_weight(operand, slot_index):
        return student_project(operand, latents[slot_index])

    def tutor_weight(operand, slot_index):
        return teacher_project(operand, tutors[slot_index])

    weight_sums = None
    vector_sums = [jnp.zeros(vector.shape, jnp.float32) for vector in vectors]
    error_sum = jnp.zeros((), jnp.float32)
    outputs_all = []
    grads_all = []
    for micro_index in range(micro_count):
        hidden = (
            hidden_in[micro_index].astype(jnp.float32).reshape(seq_count * local_rows, width_all)
        )
        lengths = seq_lengths[micro_index]
        targets, unused = forward(hidden, lengths, tutor_weight, tutor_vectors, None)
        output, kept_values = forward(hidden, lengths, student_weight, vectors, clips)
        row_keep = (
            (positions[None, :] < lengths[:, None])
            .astype(jnp.float32)
            .reshape(seq_count * local_rows, 1)
        )
        difference = output - targets
        error_sum = error_sum + 0.5 * jnp.sum(row_keep * difference * difference)
        weight_parts, vector_parts, grad_hidden = backward(
            row_keep * difference, hidden, lengths, latents, vectors, clips, kept_values
        )
        if weight_sums is None:
            weight_sums = list(weight_parts)
        else:
            weight_sums = [running + added for running, added in zip(weight_sums, weight_parts)]
        vector_sums = [running + added for running, added in zip(vector_sums, vector_parts)]
        outputs_all.append(output.astype(jnp.bfloat16).reshape(seq_count, local_rows, width_all))
        grads_all.append(grad_hidden.reshape(seq_count, local_rows, width_all))
    weight_sums = (
        lax.psum_scatter(
            weight_sums[0].astype(jnp.bfloat16), "grp", scatter_dimension=0, tiled=True
        ).astype(jnp.float32),
        lax.psum_scatter(
            weight_sums[1].astype(jnp.bfloat16), "grp", scatter_dimension=0, tiled=True
        ).astype(jnp.float32),
        lax.psum_scatter(
            weight_sums[2].astype(jnp.bfloat16), "grp", scatter_dimension=0, tiled=True
        ).astype(jnp.float32),
        lax.psum_scatter(
            weight_sums[3].astype(jnp.bfloat16), "grp", scatter_dimension=0, tiled=True
        ).astype(jnp.float32),
        lax.psum_scatter(
            weight_sums[4].astype(jnp.bfloat16), "grp", scatter_dimension=0, tiled=True
        ).astype(jnp.float32),
        lax.psum_scatter(
            weight_sums[5].astype(jnp.bfloat16), "grp", scatter_dimension=0, tiled=True
        ).astype(jnp.float32),
    )
    vector_shards = (
        lax.psum_scatter(
            vector_sums[0].astype(jnp.bfloat16), "grp", scatter_dimension=0, tiled=True
        ).astype(jnp.float32),
        lax.psum_scatter(
            vector_sums[1].astype(jnp.bfloat16), "grp", scatter_dimension=0, tiled=True
        ).astype(jnp.float32),
        lax.psum_scatter(
            vector_sums[2].astype(jnp.bfloat16), "grp", scatter_dimension=0, tiled=True
        ).astype(jnp.float32),
        lax.psum_scatter(
            vector_sums[3].astype(jnp.bfloat16), "grp", scatter_dimension=0, tiled=True
        ).astype(jnp.float32),
        lax.psum_scatter(
            vector_sums[4].astype(jnp.bfloat16), "grp", scatter_dimension=0, tiled=True
        ).astype(jnp.float32),
        lax.psum_scatter(
            vector_sums[5].astype(jnp.bfloat16), "grp", scatter_dimension=0, tiled=True
        ).astype(jnp.float32),
        lax.psum_scatter(
            vector_sums[6].astype(jnp.bfloat16), "grp", scatter_dimension=0, tiled=True
        ).astype(jnp.float32),
        lax.psum_scatter(
            vector_sums[7].astype(jnp.bfloat16), "grp", scatter_dimension=0, tiled=True
        ).astype(jnp.float32),
        lax.psum_scatter(
            vector_sums[8].astype(jnp.bfloat16), "grp", scatter_dimension=0, tiled=True
        ).astype(jnp.float32),
    )
    totals = (
        lax.psum(weight_sums[0].astype(jnp.bfloat16), "rep").astype(jnp.float32),
        lax.psum(weight_sums[1].astype(jnp.bfloat16), "rep").astype(jnp.float32),
        lax.psum(weight_sums[2].astype(jnp.bfloat16), "rep").astype(jnp.float32),
        lax.psum(weight_sums[3].astype(jnp.bfloat16), "rep").astype(jnp.float32),
        lax.psum(weight_sums[4].astype(jnp.bfloat16), "rep").astype(jnp.float32),
        lax.psum(weight_sums[5].astype(jnp.bfloat16), "rep").astype(jnp.float32),
        lax.psum(vector_shards[0].astype(jnp.bfloat16), "rep").astype(jnp.float32),
        lax.psum(vector_shards[1].astype(jnp.bfloat16), "rep").astype(jnp.float32),
        lax.psum(vector_shards[2].astype(jnp.bfloat16), "rep").astype(jnp.float32),
        lax.psum(vector_shards[3].astype(jnp.bfloat16), "rep").astype(jnp.float32),
        lax.psum(vector_shards[4].astype(jnp.bfloat16), "rep").astype(jnp.float32),
        lax.psum(vector_shards[5].astype(jnp.bfloat16), "rep").astype(jnp.float32),
        lax.psum(vector_shards[6].astype(jnp.bfloat16), "rep").astype(jnp.float32),
        lax.psum(vector_shards[7].astype(jnp.bfloat16), "rep").astype(jnp.float32),
        lax.psum(vector_shards[8].astype(jnp.bfloat16), "rep").astype(jnp.float32),
    )
    error_all = lax.psum(error_sum, ("rep", "grp"))
    entries = (
        micro_count
        * seq_count
        * lax.axis_size("rep")
        * local_rows
        * lax.axis_size("grp")
        * width_all
    )
    distill_loss = error_all / entries
    return (
        jnp.stack(outputs_all),
        distill_loss,
        jnp.stack(grads_all),
        totals[0],
        totals[1],
        totals[2],
        totals[3],
        totals[4],
        totals[5],
        totals[6],
        totals[7],
        totals[8],
        totals[9],
        totals[10],
        totals[11],
        totals[12],
        totals[13],
        totals[14],
    )


F32 = jnp.float32
BF16 = jnp.bfloat16
ANY = pl.BlockSpec(memory_space=pl.ANY)
VM = pl.BlockSpec(memory_space=pltpu.VMEM)
SM = pl.BlockSpec(memory_space=pltpu.SMEM)
VMEM_LIMIT = 60 * 1024 * 1024

I_CORE, I_REP, I_Z, I_LEN, I_RING = 0, 1, 2, 3, 4


def z_ring(line):
    return list(range(0, line, 2)) + list(range(1, line, 2))[::-1]


def dims(a, b, ca, cb):
    return lax.dot_general(a, b, (((ca,), (cb,)), ((), ())), preferred_element_type=F32)


def params(**kw):
    return pltpu.CompilerParams(vmem_limit_bytes=VMEM_LIMIT, **kw)


def cost(flops, nbytes, trans=0):
    return pl.CostEstimate(flops=int(flops), bytes_accessed=int(nbytes), transcendentals=int(trans))


def wait_all(ref, sem):
    pltpu.make_async_copy(ref, ref, sem).wait()


def binary_rows(latent):
    level = jnp.mean(jnp.abs(latent), axis=1, keepdims=True)
    return jnp.where(latent > 0, level, jnp.where(latent < 0, -level, 0.0)).astype(BF16)


def pack_kernel(info, lq, lk, lv, lo, lu, ld, tq, tk, tv, to, tu, td, qkv, own, mine):
    rep = info[I_REP]
    for slot, ref in enumerate((lq, lk, lv)):
        qkv[0, slot] = binary_rows(ref[...])
    for slot, ref in enumerate((tq, tk, tv)):
        qkv[1, slot] = ref[...]
    rows, width = lq.shape
    quarter = own.shape[0]
    half = rows // 2

    def fill(base, up, down):
        for r in range(quarter):
            own[r, base : base + rows] = up[r * rows : (r + 1) * rows]
            own[r, base + rows : base + 2 * rows] = down[:, r * width : (r + 1) * width]

    fill(0, binary_rows(lu[...]), binary_rows(ld[...]))
    fill(2 * rows, tu, td)
    student_out = binary_rows(lo[...])
    for h in range(2):
        own[h, 4 * rows :] = student_out[h * half : (h + 1) * half]
        own[2 + h, 4 * rows :] = to[h * half : (h + 1) * half]
    mine[...] = own[rep]


def pack(info, latents, tutors):
    rows, width = latents[0].shape
    piece = 4 * rows + rows // 2
    return pl.pallas_call(
        pack_kernel,
        out_shape=(
            jax.ShapeDtypeStruct((2, 3, rows, width), BF16),
            jax.ShapeDtypeStruct((4, piece, width), BF16),
            jax.ShapeDtypeStruct((piece, width), BF16),
        ),
        in_specs=[SM] + [VM] * 12,
        out_specs=(VM,) * 3,
        compiler_params=params(),
        cost_estimate=cost(4e6, 12e6),
        name="pack",
    )(info, *latents, *tutors)


def table_kernel(*refs):
    heads_bias, vecs = refs[13:]
    line, _, feats = heads_bias.shape[2:]
    width = line * feats

    def flat(ref):
        return ref[...].reshape(1, ref.shape[0])

    bq, bv, bo, bu, bd, g1, s1, g2, s2 = [flat(ref) for ref in refs[:9]]
    biases, inner, gains, shifts = refs[9:13]
    for net, pair in enumerate(((bq, bv), (biases[0:1], biases[1:2]))):
        for slot, row in enumerate(pair):
            for z in range(line):
                heads_bias[net, slot, z] = row[:, z * feats : (z + 1) * feats]
    rows = (
        (bo, bd, g1, s1, g2, s2),
        (biases[2:3], biases[3:4], gains[0:1], shifts[0:1], gains[1:2], shifts[1:2]),
    )
    for net, up in enumerate((bu, flat(inner))):
        for slot, row in enumerate(rows[net]):
            vecs[net, slot] = row
        for r in range(4):
            vecs[net, V_UP + r] = up[:, r * width : (r + 1) * width]


def table(vectors, tutor_vectors, line):
    width = vectors[0].shape[0]
    return pl.pallas_call(
        table_kernel,
        out_shape=(
            jax.ShapeDtypeStruct((2, 2, line, 1, width // line), F32),
            jax.ShapeDtypeStruct((2, 10, 1, width), F32),
        ),
        in_specs=[VM] * 13,
        out_specs=(VM,) * 2,
        compiler_params=params(),
        cost_estimate=cost(1e5, 2e5),
        name="table",
    )(*vectors, *tutor_vectors)


def load_tokens(info, xs, pieces, sem):
    core = info[I_CORE]
    for k, piece in enumerate(pieces):
        for j in range(2):
            spot = jnp.where(j == 0, core, 1 - core)
            pltpu.make_async_copy(piece.at[j], xs.at[info[I_RING + k], spot], sem).start()


def load_rows(info, ws, own, sib, net, sem):
    core = info[I_CORE]
    for slot in range(3):
        pltpu.make_async_copy(own.at[net, slot], ws.at[slot, core], sem).start()
        pltpu.make_async_copy(sib.at[net, slot], ws.at[slot, 1 - core], sem).start()


def attend_kernel(student, info, *refs):
    pieces, refs = refs[:4], refs[4:]
    own, sib, heads_bias, clip = refs[:4]
    refs = refs[4:]
    net = 0 if student else 1
    if student:
        out, qkv_out, lse_out, ctx_out, xs, ws, qs, ks, vt, ct, low, sems = refs
    else:
        _, out, xs, ws, qs, ks, vt, ct, low, sems = refs
    load_tokens(info, xs, pieces, sems.at[0])
    load_rows(info, ws, own, sib, net, sems.at[1])
    line, _, half, width = xs.shape
    block = 2 * half
    feats = qs.shape[1]
    total = qs.shape[0]
    heads = feats // DH
    place = info[I_Z]
    length = info[I_LEN]
    bq_row, bv_row = heads_bias[net, 0, place], heads_bias[net, 1, place]
    wait_all(xs, sems.at[0])
    wait_all(ws, sems.at[1])

    def project(b, carry):
        rows = pl.ds(pl.multiple_of(b * block, block), block)
        x = xs[b].reshape(block, width)
        if student:
            lim = clip[...]
            x = jnp.clip(x.astype(F32), -lim, lim).astype(BF16)
        q = (dims(x, ws[0].reshape(feats, width), 1, 1) + bq_row).astype(BF16)
        k = dims(x, ws[1].reshape(feats, width), 1, 1).astype(BF16)
        v = (dims(x, ws[2].reshape(feats, width), 1, 1) + bv_row).astype(BF16)
        q = q * jnp.asarray(DH ** (-0.5), BF16)
        qs[rows] = q
        ks[rows] = k
        vt[:, rows] = v.astype(F32).T.astype(BF16)
        if student:
            qkv_out[0, rows] = q
            qkv_out[1, rows] = k
            qkv_out[2, rows] = v
        return carry

    lax.fori_loop(0, line, project, 0, unroll=True)
    fill = jnp.where(
        lax.broadcasted_iota(jnp.int32, (total, 1), 0) < length, 0.0, NEG_FILL
    ).astype(F32)
    lane_head = lax.broadcasted_iota(jnp.int32, (1, feats), 1) // DH

    def mix(b, carry):
        rows = pl.ds(pl.multiple_of(b * block, block), block)
        q = qs[rows]
        for h in range(heads):
            q_h = jnp.where(lane_head == h, q, jnp.zeros_like(q))
            scores = dims(ks[...], q_h, 1, 1) + fill
            top = jnp.max(scores, axis=0, keepdims=True)
            weight = jnp.exp(scores - top)
            mass = jnp.sum(weight, axis=0, keepdims=True)
            head = slice(h * DH, (h + 1) * DH)
            mixed = dims(vt[head], weight.astype(BF16), 1, 0) * (1.0 / mass)
            ct[head, rows] = mixed
            if student:
                lse_out[h : h + 1, rows] = top + jnp.log(mass)
        return carry

    lax.fori_loop(0, line, mix, 0)
    for b in range(line):
        low[b] = ct[:, b * block : (b + 1) * block].astype(BF16)
        pltpu.make_async_copy(low.at[b], out.at[b, net], sems.at[2 + b]).start()
    if student:
        ctx_out[...] = ct[...]
    for b in range(line):
        pltpu.make_async_copy(low.at[b], out.at[b, net], sems.at[2 + b]).wait()


def attend(info, pieces, own, sib, heads_bias, clip, both=None):
    _, half, width = pieces[0].shape
    line = len(pieces)
    total = line * 2 * half
    rows = own.shape[2]
    feats = 2 * rows
    student = both is None
    outs = [jax.ShapeDtypeStruct((line, 2, feats, 2 * half), BF16)]
    if student:
        outs += [
            jax.ShapeDtypeStruct((3, total, feats), BF16),
            jax.ShapeDtypeStruct((8, total), F32),
            jax.ShapeDtypeStruct((feats, total), F32),
        ]
    return pl.pallas_call(
        functools.partial(attend_kernel, student),
        out_shape=tuple(outs),
        in_specs=[SM] + [ANY] * 6 + [VM] * 2 + ([] if student else [ANY]),
        out_specs=(ANY,) + (VM,) * (len(outs) - 1),
        scratch_shapes=[
            pltpu.VMEM((line, 2, half, width), BF16),
            pltpu.VMEM((3, 2, rows, width), BF16),
            pltpu.VMEM((total, feats), BF16),
            pltpu.VMEM((total, feats), BF16),
            pltpu.VMEM((feats, total), BF16),
            pltpu.VMEM((feats, total), F32),
            pltpu.VMEM((line, feats, 2 * half), BF16),
            pltpu.SemaphoreType.DMA((2 + line,)),
        ],
        input_output_aliases={} if student else {9: 0},
        compiler_params=params(),
        cost_estimate=cost(6e9, 4e6, 3e6),
        name="attend_student" if student else "attend_tutor",
    )(info, *pieces, own, sib, heads_bias, clip, *([] if student else [both]))


def attend_back_kernel(info, *refs):
    pieces, refs = refs[:4], refs[4:]
    (own, sib, clip, qkv, lse, ctx, dctx, part0, part1, part2, part3, keep, send) = refs[:13]
    (xs, ws, kt, dct, dq, dk, dv, sems) = refs[13:]
    parts = (part0, part1, part2, part3)
    load_tokens(info, xs, pieces, sems.at[0])
    load_rows(info, ws, own, sib, 0, sems.at[1])
    line, _, half, width = xs.shape
    block = 2 * half
    total, feats = dk.shape
    heads = feats // DH
    core = info[I_CORE]
    length = info[I_LEN]
    lim = clip[...]
    for b in range(line):
        cols = slice(b * block, (b + 1) * block)
        kt[:, cols] = qkv[1, cols].astype(F32).T.astype(BF16)
        dct[:, cols] = dctx[b].astype(F32)
    dk[...] = jnp.zeros_like(dk)
    dv[...] = jnp.zeros_like(dv)
    fill = jnp.where(
        lax.broadcasted_iota(jnp.int32, (total, 1), 0) < length, 0.0, NEG_FILL
    ).astype(F32)
    lane_head = lax.broadcasted_iota(jnp.int32, (1, feats), 1) // DH
    row_head = lax.broadcasted_iota(jnp.int32, (feats, 1), 0) // DH

    def body(b, carry):
        rows = pl.ds(pl.multiple_of(b * block, block), block)
        q = qkv[0, rows]
        g = dctx[b]
        dk_add = dv_add = None
        for h in range(heads):
            head = slice(h * DH, (h + 1) * DH)
            q_h = jnp.where(lane_head == h, q, jnp.zeros_like(q))
            g_h = jnp.where(row_head == h, g, jnp.zeros_like(g))
            delta = jnp.sum(dct[head, rows] * ctx[head, rows], axis=0, keepdims=True)
            probs = jnp.exp(dims(qkv[1], q_h, 1, 1) + fill - lse[h : h + 1, rows])
            dprobs = dims(qkv[2], g_h, 1, 0)
            dscores = (probs * (dprobs - delta)).astype(BF16)
            dv_h = dims(probs.astype(BF16), g_h, 1, 1)
            dk_h = dims(dscores, q_h, 1, 0)
            dk_add = dk_h if dk_add is None else dk_add + dk_h
            dv_add = dv_h if dv_add is None else dv_add + dv_h
            dq[head, rows] = dims(kt[head], dscores, 1, 0) * (DH ** (-0.5))
        dk[...] += dk_add
        dv[...] += dv_add
        return carry

    lax.fori_loop(0, line, body, 0)
    wait_all(xs, sems.at[0])
    wait_all(ws, sems.at[1])
    dq_t = dq[...].astype(BF16)
    dq_low = dq_t.astype(F32).T.astype(BF16)
    dk_low = dk[...].astype(BF16)
    dv_low = dv[...].astype(BF16)
    dk_t = dk_low.astype(F32).T.astype(BF16)
    dv_t = dv_low.astype(F32).T.astype(BF16)
    qkv_flat = [ws[slot].reshape(feats, width) for slot in range(3)]
    for k in range(line):
        spot = info[I_RING + k]
        rows = pl.ds(pl.multiple_of(spot * block, block), block)
        dk_rows = dk[rows].astype(BF16)
        dv_rows = dv[rows].astype(BF16)
        dq_rows = dq[:, rows].T.astype(BF16)
        parts[k][...] = (
            dims(dq_rows, qkv_flat[0], 1, 0)
            + dims(dk_rows, qkv_flat[1], 1, 0)
            + dims(dv_rows, qkv_flat[2], 1, 0)
        ).astype(BF16)
    grads = []
    for low_t in (dq_t, dk_t, dv_t):
        acc = None
        for b in range(line):
            x = jnp.clip(xs[b].reshape(block, width).astype(F32), -lim, lim).astype(BF16)
            one = dims(low_t[:, b * block : (b + 1) * block], x, 1, 0)
            acc = one if acc is None else acc + one
        grads.append(acc)
    rows = feats // 2
    bias_q = jnp.sum(dq_low.astype(F32), axis=0, keepdims=True)
    bias_v = jnp.sum(dv_low.astype(F32), axis=0, keepdims=True)
    for rel, ref in ((0, keep), (1, send)):
        for c in range(2):

            @pl.when((core if rel == 0 else 1 - core) == c)
            def _():
                for slot, grad in enumerate(grads):
                    ref[slot * rows : (slot + 1) * rows] = grad[c * rows : (c + 1) * rows].astype(
                        ref.dtype
                    )
                tail = jnp.concatenate(
                    [
                        bias_q[:, c * rows : (c + 1) * rows],
                        bias_v[:, c * rows : (c + 1) * rows],
                        jnp.zeros((1, width - 2 * rows), F32),
                    ],
                    axis=1,
                )
                ref[3 * rows :] = jnp.broadcast_to(tail, (16, width)).astype(ref.dtype)


def attend_back(info, pieces, own, sib, clip, qkv, lse, ctx, dctx):
    _, half, width = pieces[0].shape
    line = len(pieces)
    total = line * 2 * half
    rows = own.shape[2]
    feats = 2 * rows
    part = jax.ShapeDtypeStruct((2 * half, width), BF16)
    grad = jax.ShapeDtypeStruct((3 * rows + 16, width), BF16)
    return pl.pallas_call(
        attend_back_kernel,
        out_shape=(part,) * 4 + (grad, grad),
        in_specs=[SM] + [ANY] * 6 + [VM] * 5,
        out_specs=(VM,) * 6,
        scratch_shapes=[
            pltpu.VMEM((line, 2, half, width), BF16),
            pltpu.VMEM((3, 2, rows, width), BF16),
            pltpu.VMEM((feats, total), BF16),
            pltpu.VMEM((feats, total), F32),
            pltpu.VMEM((feats, total), F32),
            pltpu.VMEM((total, feats), F32),
            pltpu.VMEM((total, feats), F32),
            pltpu.SemaphoreType.DMA((2,)),
        ],
        compiler_params=params(),
        cost_estimate=cost(12e9, 6e6, 3e6),
        name="attend_back",
    )(info, *pieces, own, sib, clip, qkv, lse, ctx, dctx)


V_OUT, V_DOWN, V_G1, V_S1, V_G2, V_S2, V_UP = 0, 1, 2, 3, 4, 5, 6
S_OUT, S_DOWN, S_G1, S_S1, S_G2, S_S2, S_UP = 0, 1, 2, 3, 4, 5, 6
PAD = 16


def norm_parts(v):
    centre = v - jnp.mean(v, axis=-1, keepdims=True)
    inv = lax.rsqrt(jnp.mean(centre * centre, axis=-1, keepdims=True) + NORM_EPS)
    return centre * inv, inv


def norm_back(dnormed, normed, inv):
    return inv * (
        dnormed
        - jnp.mean(dnormed, axis=-1, keepdims=True)
        - normed * jnp.mean(dnormed * normed, axis=-1, keepdims=True)
    )


def turned(v):
    return v.T.astype(BF16)


def middle_kernel(info, own, sib, *refs):
    chunks, refs = refs[:30], refs[30:]
    (x_own, ctx, vecs) = refs[:3]
    (out_keep, out_send, dfirst_keep, dctx_out) = refs[3:7]
    grads = refs[7:15]
    (weights, w_out, slopes, lower, gup, gdn, sums, base, aim, acc, sems) = refs[15:]
    core, rep, place, length = info[I_CORE], info[I_REP], info[I_Z], info[I_LEN]
    _, quarters, groups, pair, width = weights.shape
    rows = pair // 2
    tokens = ctx.shape[3]
    line = groups // 2
    hidden = groups * rows
    half = rows // 2

    piece = 2 * pair + half
    found = []
    for rel, ref in ((0, own), (1, sib)):
        member = 2 * place + (core if rel == 0 else 1 - core)
        found += [(ref.at[r], 0, piece, r, member) for r in range(quarters)]
    for k in range(1, line):
        for rel in range(2):
            member = 2 * info[I_RING + k] + (core if rel == 0 else 1 - core)
            got = chunks[((k - 1) * 2 + rel) * 5 :]
            found += [(got[far], 0, piece, rep ^ far, member) for far in range(3)]
            found.append((got[3], 0, pair, rep ^ 3, member))
            found.append((got[4], pair, piece, rep ^ 3, member))
    fields = (
        (2 * pair, piece, lambda r, g: w_out.at[r // 2, g, lax.rem(r, 2)], 2),
        (pair, 2 * pair, lambda r, g: weights.at[1, r, g], 1),
        (0, pair, lambda r, g: weights.at[0, r, g], 0),
    )
    for lo, hi, target, sem in fields:
        for src, first, last, r, g in found:
            if first <= lo and hi <= last:
                pltpu.make_async_copy(
                    src.at[pl.ds(lo - first, hi - lo)], target(r, g), sems.at[sem]
                ).start()

    def up_rows(net, r):
        return jnp.concatenate(
            [weights[net, q, 2 * r + g, 0:rows] for g in range(2) for q in range(quarters)], axis=0
        )

    def down_rows(net, r):
        return weights[net, r, :, rows:].reshape(width, hidden)

    wait_all(w_out, sems.at[2])
    x_low = jnp.concatenate(
        [x_own[jnp.where(core == j, 0, 1)] for j in range(2)], axis=0
    ).astype(F32)

    def row(net, which):
        return vecs[net, which]

    def context_of(net):
        flat = jnp.concatenate([ctx[zb, net] for zb in range(line)], axis=0)
        return flat, flat.astype(F32).T.astype(BF16)

    def upper(net, ctx):
        first = (
            x_low + dims(ctx, w_out[net].reshape(width, width), 1, 1) + row(net, V_OUT)
        )
        normed, inv = norm_parts(first)
        return normed, inv, normed * row(net, V_G1) + row(net, V_S1)

    def lower_half(net, upper_in, keep):
        acc[...] = jnp.zeros_like(acc)

        def step(r, carry):
            gate = (
                dims(upper_in, up_rows(net, r), 1, 1)
                + vecs[net, V_UP + r]
            )
            below = 0.5 * (1.0 + lax.erf(gate * 0.7071067811865476))
            low = (gate * below).astype(BF16)
            if keep:
                slopes[r] = below + gate * (0.3989422804014327 * jnp.exp(-0.5 * gate * gate))
                lower[r] = low
            acc[...] += dims(low, down_rows(net, r), 1, 1)
            return carry

        lax.fori_loop(0, quarters, step, 0, unroll=True)
        return acc[...]

    _, ctx_tutor = context_of(1)
    _, _, first_norm = upper(1, ctx_tutor)
    ctx_flat, ctx_low = context_of(0)
    normed_one, inv_one, first_norm_s = upper(0, ctx_low)
    base[...] = first_norm_s
    wait_all(weights.at[1], sems.at[1])
    second = first_norm + lower_half(1, first_norm.astype(BF16), False) + row(1, V_DOWN)
    normed, _ = norm_parts(second)
    aim[...] = normed * row(1, V_G2) + row(1, V_S2)

    wait_all(weights.at[0], sems.at[0])
    upper_in = first_norm_s.astype(BF16)
    second = base[...] + lower_half(0, upper_in, True) + row(0, V_DOWN)
    normed_two, inv_two = norm_parts(second)
    output = normed_two * row(0, V_G2) + row(0, V_S2)
    aim[...] = output - aim[...]
    acc[...] = output

    def part_of(ref, j):
        return ref[pl.ds(pl.multiple_of(j * (tokens // 2), tokens // 2), tokens // 2)]

    out_keep[...] = part_of(acc, core).astype(BF16)
    out_send[...] = part_of(acc, 1 - core).astype(BF16)
    where = place * tokens + lax.broadcasted_iota(jnp.int32, (tokens, 1), 0)
    kept = jnp.where(where < length, 1.0, 0.0).astype(F32)
    dout = kept * aim[...]
    sums[...] = jnp.zeros_like(sums)
    error = 0.5 * jnp.sum(dout * dout)
    sums[S_G2] = jnp.sum(dout * normed_two, axis=0, keepdims=True)
    sums[S_S2] = jnp.sum(dout, axis=0, keepdims=True)
    dsecond = norm_back(dout * row(0, V_G2), normed_two, inv_two)
    sums[S_DOWN] = jnp.sum(dsecond, axis=0, keepdims=True)
    g_down = dsecond.astype(BF16)
    g_down_t = turned(dsecond)
    acc[...] = dsecond

    def member_of(rel, z):
        return 2 * z + (core if rel == 0 else 1 - core)

    def send_up(rel, far, k, z, part):
        ref = grads[rel * 4 + (far & 1)].at[far >> 1, k, part]
        src = gup.at[member_of(rel, z), rep ^ far, part]
        pltpu.make_async_copy(src, ref, sems.at[3 + rel * 4 + (far & 1)]).start()

    def send_down(rel, high, low, k, z, r, part):
        ref = grads[rel * 4 + 2 + high].at[low, k, part]
        src = gdn.at[r, member_of(rel, z), part]
        pltpu.make_async_copy(src, ref, sems.at[5 + rel * 4 + high]).start()

    main, rest = pl.ds(0, rows), pl.ds(rows, PAD)

    def back(r, carry):
        low = lower[r]
        gdn[r, :, 0:rows] = dims(g_down_t, low, 1, 0).astype(BF16).reshape(groups, rows, hidden)
        dlower = dims(g_down, down_rows(0, r), 1, 0)
        dgate = dlower * slopes[r]
        sums[S_UP + r] = jnp.sum(dgate, axis=0, keepdims=True)
        gup_r = dims(turned(dgate), upper_in, 1, 0).astype(BF16)
        gup[pl.ds(2 * r, 2), :, 0:rows] = gup_r.reshape(2, quarters, rows, width)
        acc[...] += dims(dgate.astype(BF16), up_rows(0, r), 1, 0)
        hops = 0
        for k in range(1, line):
            hops = jnp.where(info[I_RING + k] == r, k, hops)
        far = r ^ rep
        for rel in range(2):
            for way in range(4):
                send_up(rel, way, hops, r, main)
            for high in range(2):

                @pl.when(far // 2 == high)
                def _():
                    for k in range(line):
                        send_down(rel, high, far & 1, k, info[I_RING + k], r, main)

        return carry

    lax.fori_loop(0, quarters, back, 0)
    dfirst = acc[...]
    sums[S_G1] = jnp.sum(dfirst * normed_one, axis=0, keepdims=True)
    sums[S_S1] = jnp.sum(dfirst, axis=0, keepdims=True)
    dsum = norm_back(dfirst * row(0, V_G1), normed_one, inv_one)
    sums[S_OUT] = jnp.sum(dsum, axis=0, keepdims=True)
    dfirst_keep[...] = dsum
    g_out = dsum.astype(BF16)
    dctx = turned(dims(g_out, w_out[0].reshape(width, width), 1, 0))
    dctx_out[...] = dctx.reshape(dctx_out.shape)
    gout = dims(turned(dsum), ctx_flat, 1, 1).reshape(groups, quarters, rows // quarters, width)
    number = rep * groups + 2 * place + core
    high = error.astype(BF16).astype(F32)
    middle_part = (error - high).astype(BF16).astype(F32)
    lane = lax.broadcasted_iota(jnp.int32, (1, width), 1)
    digits = jnp.zeros((1, width), F32)
    for slot, digit in enumerate((high, middle_part, error - high - middle_part)):
        digits = jnp.where(lane == 3 * number + slot, digit, digits)
    ups = jnp.concatenate([sums[S_UP + r] for r in range(quarters)], axis=1)
    slim = rows // quarters
    for g in range(groups):
        own_rows = [sums[which][:, g * rows : (g + 1) * rows] for which in range(6)]
        vectors = jnp.concatenate(
            [
                jnp.concatenate(own_rows, axis=0),
                jnp.zeros((6, width - rows), F32),
            ],
            axis=1,
        )
        inner = jnp.concatenate(
            [
                ups[:, g * 4 * rows : (g + 1) * 4 * rows],
                jnp.zeros((1, width - 4 * rows), F32),
            ],
            axis=1,
        )
        tail = jnp.concatenate([vectors, inner, digits], axis=0)
        for r in range(quarters):
            gup[g, r, rows:] = gout[g, r, :PAD].astype(BF16)
            gdn[r, g, rows:] = jnp.concatenate([gout[g, r, PAD:slim], tail], axis=0).astype(BF16)

    for rel in range(2):
        for far in range(4):
            for k in range(line):
                z = info[I_RING + k]
                send_up(rel, far, k, z, rest)
                send_down(rel, far >> 1, far & 1, k, z, rep ^ far, rest)
    for slot in range(8):
        wait_all(grads[slot], sems.at[3 + slot])


def middle(info, own, sib, chunks, x_own, ctx, vecs):
    line, _, feats, tokens = ctx.shape
    width = line * feats
    quarters = own.shape[0]
    groups = 2 * line
    rows = width // groups
    half = (tokens // 2, width)
    part = jax.ShapeDtypeStruct((2, line, rows + PAD, width), BF16)
    outs = (
        jax.ShapeDtypeStruct(half, BF16),
        jax.ShapeDtypeStruct(half, BF16),
        jax.ShapeDtypeStruct((tokens, width), F32),
        jax.ShapeDtypeStruct((line, feats, tokens), BF16),
    ) + (part,) * 8
    return pl.pallas_call(
        middle_kernel,
        out_shape=outs,
        in_specs=[SM] + [ANY] * 32 + [VM] * 3,
        out_specs=(VM,) * 4 + (ANY,) * 8,
        scratch_shapes=[
            pltpu.VMEM((2, quarters, groups, 2 * rows, width), BF16),
            pltpu.VMEM((2, groups, 2, rows // 2, width), BF16),
            pltpu.VMEM((quarters, tokens, width), F32),
            pltpu.VMEM((quarters, tokens, width), BF16),
            pltpu.VMEM((groups, quarters, rows + PAD, width), BF16),
            pltpu.VMEM((quarters, groups, rows + PAD, width), BF16),
            pltpu.VMEM((S_UP + quarters, 1, width), F32),
            pltpu.VMEM((tokens, width), F32),
            pltpu.VMEM((tokens, width), F32),
            pltpu.VMEM((tokens, width), F32),
            pltpu.SemaphoreType.DMA((11,)),
        ],
        compiler_params=params(),
        cost_estimate=cost(15e9, 30e6, 4e6),
        name="middle",
    )(info, own, sib, *chunks, x_own, ctx, vecs)


def finish_up_kernel(info, *refs):
    pieces, (up, out, scr, sem) = refs[:4], refs[4:]
    rep = info[I_REP]
    for far, ref in enumerate(pieces):
        pltpu.make_async_copy(ref, scr.at[rep ^ far], sem.at[0]).start()
    wait_all(scr, sem.at[0])
    rows = up.shape[0] // len(pieces)
    for r in range(len(pieces)):
        up[r * rows : (r + 1) * rows] = scr[r, 0:rows].astype(F32)
        out[r * PAD : (r + 1) * PAD] = scr[r, rows:].astype(F32)


def finish_up(info, pieces):
    high, width = pieces[0].shape
    rows = high - PAD
    return pl.pallas_call(
        finish_up_kernel,
        out_shape=(
            jax.ShapeDtypeStruct((4 * rows, width), F32),
            jax.ShapeDtypeStruct((4 * PAD, width), F32),
        ),
        in_specs=[SM] + [ANY] * 4,
        out_specs=(VM,) * 2,
        scratch_shapes=[
            pltpu.VMEM((4, high, width), BF16),
            pltpu.SemaphoreType.DMA((1,)),
        ],
        compiler_params=params(),
        cost_estimate=cost(1e6, 3e6),
        name="finish_up",
    )(info, *pieces)


def finish_heads_kernel(grad_qkv, gq, gk, gv, bq, bv):
    rows = gq.shape[0]
    for slot, ref in enumerate((gq, gk, gv)):
        ref[...] = grad_qkv[slot * rows : (slot + 1) * rows].astype(F32)
    bias = grad_qkv[3 * rows :].astype(F32)
    bq[...] = bias[0, :rows]
    bv[...] = bias[0, rows : 2 * rows]


def finish_heads(grad_qkv):
    high, width = grad_qkv.shape
    rows = (high - 16) // 3
    return pl.pallas_call(
        finish_heads_kernel,
        out_shape=(jax.ShapeDtypeStruct((rows, width), F32),) * 3
        + (jax.ShapeDtypeStruct((rows,), F32),) * 2,
        in_specs=[VM],
        out_specs=(VM,) * 5,
        compiler_params=params(),
        cost_estimate=cost(1e6, 2e6),
        name="finish_heads",
    )(grad_qkv)


def finish_kernel(entries, info, *refs):
    pieces, refs = refs[:4], refs[4:]
    firsts, down, out, loss, bu = refs[:5]
    others, scr, sem = refs[5:11], refs[11], refs[12]
    rep = info[I_REP]
    for far, ref in enumerate(pieces):
        pltpu.make_async_copy(ref, scr.at[rep ^ far], sem.at[0]).start()
    rows, width = out.shape
    slim = rows // len(pieces)
    for r in range(len(pieces)):
        out[r * slim : r * slim + PAD] = firsts[r * PAD : (r + 1) * PAD]
    wait_all(scr, sem.at[0])
    for r in range(len(pieces)):
        down[:, r * width : (r + 1) * width] = scr[r, 0:rows].astype(F32)
        last = scr[r, rows:].astype(F32)
        out[r * slim + PAD : (r + 1) * slim] = last[: slim - PAD]
        if r == 0:
            tail = last[slim - PAD :]
            for slot, ref in enumerate(others):
                ref[...] = tail[slot, :rows]
            bu[...] = tail[S_UP, : 4 * rows]
            loss[...] = jnp.full((1, 1), jnp.sum(tail[S_UP + 1 : S_UP + 2]) / entries, F32)


def finish(info, pieces, firsts, entries):
    high, width = pieces[0].shape
    rows = high - PAD
    vector = jax.ShapeDtypeStruct((rows,), F32)
    return pl.pallas_call(
        functools.partial(finish_kernel, entries),
        out_shape=(
            jax.ShapeDtypeStruct((rows, 4 * width), F32),
            jax.ShapeDtypeStruct((rows, width), F32),
            jax.ShapeDtypeStruct((1, 1), F32),
            jax.ShapeDtypeStruct((4 * rows,), F32),
        )
        + (vector,) * 6,
        in_specs=[SM] + [ANY] * 4 + [VM],
        out_specs=(VM,) * 10,
        scratch_shapes=[
            pltpu.VMEM((4, high, width), BF16),
            pltpu.SemaphoreType.DMA((1,)),
        ],
        compiler_params=params(),
        cost_estimate=cost(1e6, 4e6),
        name="finish",
    )(info, *pieces, firsts)


def add_low(*terms):
    total = terms[0].astype(F32)
    for term in terms[1:]:
        total = total + term.astype(F32)
    return total.astype(BF16)


def after(value, *others):
    return lax.optimization_barrier((value,) + others)[0]


def line_shards(line, *args):
    hidden_in, seq_lengths = args[0], args[1]
    latents, vectors, clip_input = args[2:8], args[8:17], args[17]
    tutors, tutor_vectors = args[18:24], args[24:28]
    micro_count, _, local_rows, width = hidden_in.shape
    rows = latents[0].shape[0]
    rep, grp = lax.axis_index("rep"), lax.axis_index("grp")
    core = lax.rem(grp, 2)
    ring = z_ring(line)

    def over_z(x, pairs):
        return lax.ppermute(x, "grp", [(2 * a + c, 2 * b + c) for a, b in pairs for c in range(2)])

    def next_z(x):
        return over_z(x, [(ring[i], ring[(i + 1) % line]) for i in range(line)])

    def swap(x):
        return lax.ppermute(x, "grp", [(g, g ^ 1) for g in range(2 * line)])

    def to_rep(x, bit):
        return lax.ppermute(x, "rep", [(i, i ^ bit) for i in range(4)])

    def to_tokens(x):
        groups = [[2 * z + c for z in range(line)] for c in range(2)]
        return lax.all_to_all(x, "grp", 0, 0, axis_index_groups=groups, tiled=True)

    scalars = [
        [g % 2, 0, g // 2, 0] + [ring[(ring.index(g // 2) - k) % line] for k in range(line)]
        for g in range(2 * line)
    ]
    lane = jnp.arange(4 + line, dtype=jnp.int32)
    info = jnp.sum(
        jnp.where(jnp.arange(2 * line)[:, None] == grp, jnp.asarray(scalars, jnp.int32), 0), axis=0
    )
    length = jnp.where(core == 0, seq_lengths[0, 0], seq_lengths[1, 0])
    info = jnp.where(lane == I_REP, rep, jnp.where(lane == I_LEN, length, info)).astype(jnp.int32)
    clip = clip_input.reshape(1, width)
    tokens = hidden_in[:, 0]
    keep = jnp.where(core == 0, tokens[0], tokens[1])
    swapped = swap(jnp.where(core == 0, tokens[1], tokens[0]))
    x_own = jnp.stack([keep, swapped])
    x_1 = next_z(x_own)
    qkv_own, own, piece = pack(info, latents, tutors)
    heads_bias, vecs = table(vectors, tutor_vectors, line)

    def to_sides(value):
        return [value, to_rep(value, 1), to_rep(value, 2)]

    def to_far(got, *ready):
        got.append(to_rep(after(got[1][: 2 * rows], *ready), 2))
        got.append(to_rep(after(got[2][2 * rows :], *ready), 1))

    piece_1 = next_z(piece)
    x_1 = next_z(after(x_own, piece))
    qkv_sib = swap(qkv_own)
    sib = swap(own)
    got_1 = to_sides(piece_1)
    x_2 = next_z(after(x_1, piece_1, qkv_sib))
    x_3 = next_z(after(x_2, sib, *got_1))
    piece_2 = next_z(after(piece_1, x_2))
    to_far(got_1, x_2)
    tokens_in = [x_own, x_1, x_2, x_3]
    mixed, qkv, lse, ctx = attend(info, tokens_in, qkv_own, qkv_sib, heads_bias, clip)
    mixed = after(mixed, piece_2, *got_1)
    piece_2 = after(piece_2, mixed)
    piece_3 = next_z(piece_2)
    got_2 = to_sides(piece_2)
    (mixed,) = attend(info, tokens_in, qkv_own, qkv_sib, heads_bias, clip, mixed)
    got_3 = to_sides(after(piece_3, mixed))
    mixed = to_tokens(mixed)
    to_far(got_3, got_3[1], got_3[2])
    to_far(got_2, got_3[1], got_3[2])
    chunks = []
    for got in (got_1, got_2, got_3):
        ready = mixed if got is got_3 else got_3[0]
        chunks += got
        chunks += [swap(after(one, got_3[0])) for one in got[:3]]
        chunks += [swap(after(far, ready)) for far in got[3:]]
    (
        out_keep,
        out_send,
        dfirst,
        dctx,
        a_keep,
        a_send,
        b_keep,
        b_send,
        a_keep_sib,
        a_send_sib,
        b_keep_sib,
        b_send_sib,
    ) = middle(info, own, sib, chunks, x_own, mixed, vecs)

    def by_micro(kept, got):
        return jnp.where(core == 0, jnp.stack([kept, got]), jnp.stack([got, kept]))[:, None]

    dctx = to_tokens(dctx)
    a_out = add_low(a_send, swap(a_send_sib))
    b_out = add_low(b_send, swap(b_send_sib))
    a_in, b_in = to_rep(a_out, 1), to_rep(b_out, 2)
    a_keep_sib, b_keep_sib = swap(a_keep_sib), swap(b_keep_sib)
    part0, part1, part2, part3, gqkv, gqkv_sib = attend_back(
        info, tokens_in, qkv_own, qkv_sib, clip, qkv, lse, ctx, after(dctx, a_out, b_out)
    )
    moving_1 = next_z(part1)
    gqkv_sib = swap(gqkv_sib)
    a_next = add_low(a_keep[1], a_keep_sib[1], after(a_in, part1)[1])
    b_next = add_low(b_keep[1], b_keep_sib[1], after(b_in, part1)[1])
    moving_2 = next_z(after(add_low(moving_1, part2), a_next, b_next))
    a_next, b_next = to_rep(a_next, 2), to_rep(b_next, 1)
    part_a = add_low(a_keep[0], a_keep_sib[0], a_in[0], a_next)
    part_b = add_low(b_keep[0], b_keep_sib[0], b_in[0], b_next)
    moving_3 = next_z(add_low(moving_2, part3))
    layer_out = by_micro(out_keep, swap(after(out_send, moving_2)))
    gqkv = add_low(gqkv, gqkv_sib)
    a_1, b_1 = next_z(part_a[1]), next_z(part_b[1])
    gqkv = add_low(gqkv, to_rep(after(gqkv, moving_2), 1))
    a_2, b_2 = next_z(add_low(a_1, part_a[2])), next_z(after(add_low(b_1, part_b[2]), gqkv))
    gqkv = add_low(gqkv, to_rep(gqkv, 2))
    a_3, b_3 = next_z(add_low(a_2, part_a[3])), next_z(after(add_low(b_2, part_b[3]), gqkv))
    grad_q, grad_k, grad_v, bq, bv = finish_heads(gqkv)
    a_all, b_all = add_low(a_3, part_a[0]), add_low(b_3, part_b[0])
    a_all = to_sides(a_all) + [to_rep(a_all, 3)]
    b_all = to_sides(b_all) + [to_rep(b_all, 3)]
    grad_up, firsts = finish_up(info, a_all)
    entries = micro_count * 4 * 2 * line * local_rows * width
    grad_down, grad_out, loss, bu, bo, bd, g1, s1, g2, s2 = finish(info, b_all, firsts, entries)

    hidden_tokens = jnp.where(core == 0, x_own, x_own[::-1])
    hidden_tokens = hidden_tokens.reshape(2 * local_rows, width).astype(F32)
    dxin = moving_3.astype(F32) + part0.astype(F32)
    grad_input = dfirst + jnp.where(jnp.abs(hidden_tokens) < clip, dxin, 0.0)
    halves = grad_input.reshape(2, local_rows, width)
    grad_input = by_micro(
        jnp.where(core == 0, halves[0], halves[1]),
        swap(jnp.where(core == 0, halves[1], halves[0])),
    )
    return (
        layer_out,
        loss.reshape(()),
        grad_input,
        grad_q,
        grad_k,
        grad_v,
        grad_out,
        grad_up,
        grad_down,
        bq,
        bv,
        bo,
        bu,
        bd,
        g1,
        s1,
        g2,
        s2,
    )


def fits_line(mesh, args):
    line = mesh.shape["grp"] // 2
    micro_count, seq_count, total, width = args[0].shape
    hidden = args[6].shape[0]
    return (
        mesh.shape["rep"] == 4
        and line == 4
        and H % line == 0
        and micro_count == 2
        and seq_count == mesh.shape["rep"]
        and total == 8 * 128
        and hidden == 4 * width
    )


def solution(mesh):
    def mapped(body):
        return jax.shard_map(
        body,
        mesh=mesh,
        in_specs=(
            P(None, "rep", "grp", None),
            P(None, "rep"),
            P("grp", None),
            P("grp", None),
            P("grp", None),
            P("grp", None),
            P("grp", None),
            P("grp", None),
            P(),
            P(),
            P(),
            P(),
            P(),
            P(),
            P(),
            P(),
            P(),
            P(),
            P("grp", None),
            P("grp", None),
            P("grp", None),
            P("grp", None),
            P("grp", None),
            P("grp", None),
            P(),
            P(),
            P(),
            P(),
        ),
        out_specs=(
            P(None, "rep", "grp", None),
            P(),
            P(None, "rep", "grp", None),
            P("grp", None),
            P("grp", None),
            P("grp", None),
            P("grp", None),
            P("grp", None),
            P("grp", None),
            P("grp"),
            P("grp"),
            P("grp"),
            P("grp"),
            P("grp"),
            P("grp"),
            P("grp"),
            P("grp"),
            P("grp"),
        ),
        check_vma=False,
    )

    def step(*args):
        if fits_line(mesh, args):
            line = mesh.shape["grp"] // 2
            return mapped(functools.partial(line_shards, line))(*args)
        return mapped(shards)(*args)

    return step
```

```python
import functools

import jax
import jax.numpy as jnp
from jax import lax
from jax.experimental import pallas as pl
from jax.experimental.pallas import tpu as pltpu
from jax.sharding import PartitionSpec as P

H = 12
DH = 64


NEG_FILL = -1e30
NORM_EPS = 1e-05


def layer_norm(tensor, gain_row, shift_row):
    centre = tensor - jnp.mean(tensor, axis=-1, keepdims=True)
    spread = jnp.mean(centre * centre, axis=-1, keepdims=True)
    return centre * lax.rsqrt(spread + NORM_EPS) * gain_row + shift_row


def gelu_exact(tensor):
    return 0.5 * tensor * (1.0 + lax.erf(tensor * 0.7071067811865476))


def times_rows(operand, weight):
    return lax.dot_general(
        operand, weight, (((1,), (1,)), ((), ())), preferred_element_type=jnp.float32
    )


def binarize(latent_rows):
    magnitude = jnp.mean(jnp.abs(latent_rows), axis=1, keepdims=True)
    return (magnitude * jnp.sign(latent_rows)).astype(jnp.bfloat16)


def student_project(operand, latent):
    return times_rows(
        operand,
        binarize(
            lax.all_gather(latent.astype(jnp.bfloat16), "grp", axis=0, tiled=True).astype(
                jnp.float32
            )
        ),
    )


def teacher_project(operand, weight):
    return times_rows(operand, lax.all_gather(weight, "grp", axis=0, tiled=True))


def add_columns(grads_low, weight_rows):
    return jnp.dot(grads_low, weight_rows, preferred_element_type=jnp.float32)


def student_back(grads_low, latent):
    return add_columns(
        grads_low,
        binarize(
            lax.all_gather(latent.astype(jnp.bfloat16), "grp", axis=0, tiled=True).astype(
                jnp.float32
            )
        ),
    )


def weight_grad(grads_low, operand):
    return lax.dot_general(
        grads_low, operand, (((0,), (0,)), ((), ())), preferred_element_type=jnp.float32
    )


def head_scores(queries, keys):
    seq_count, query_rows = (queries.shape[0], queries.shape[1])
    key_rows = keys.shape[1]
    query_heads = queries.reshape(seq_count, query_rows, H, DH)
    key_heads = keys.reshape(seq_count, key_rows, H, DH)
    return jnp.einsum(
        "schd,snhd->shcn", query_heads, key_heads, preferred_element_type=jnp.float32
    ) * DH ** (-0.5)


def key_mask(lengths, first_row, key_rows):
    positions = first_row + jnp.arange(key_rows, dtype=jnp.int32)
    return (positions[None, :] < lengths[:, None])[:, None, None, :]


def in_blocks(block_step, state_in, pieces):
    total_rows = pieces[0].shape[1]
    block_rows = 512

    def scan_step(running, block_index):
        offset = block_index * block_rows
        sliced = tuple(
            (lax.dynamic_slice_in_dim(member, offset, block_rows, 1) for member in pieces)
        )
        return (block_step(running, sliced, offset), None)

    state_out, unused = lax.scan(
        scan_step, state_in, jnp.arange(total_rows // block_rows, dtype=jnp.int32)
    )
    return state_out


def attention_forward(queries, keys, values, lengths):
    seq_count, query_rows, width_all = queries.shape
    stat_shape = (seq_count, H, query_rows)

    def stat_step(state_in, pieces, first_row):
        row_top, row_sum = state_in
        key_part = pieces[0]
        scores = jnp.where(
            key_mask(lengths, first_row, key_part.shape[1]),
            head_scores(queries, key_part),
            NEG_FILL,
        )
        new_top = jnp.maximum(row_top, jnp.max(scores, axis=3))
        row_sum = row_sum * jnp.exp(row_top - new_top) + jnp.sum(
            jnp.exp(scores - new_top[..., None]), axis=3
        )
        return (new_top, row_sum)

    stat_init = (jnp.full(stat_shape, NEG_FILL, jnp.float32), jnp.zeros(stat_shape, jnp.float32))
    row_top, row_sum = in_blocks(
        stat_step, stat_init, (lax.all_gather(keys, "grp", axis=1, tiled=True),)
    )
    log_total = row_top + jnp.log(row_sum)
    head_shape = (seq_count, query_rows, H, DH)

    def mix_step(state_in, pieces, first_row):
        key_part, value_part = pieces
        key_rows = key_part.shape[1]
        scores = jnp.where(
            key_mask(lengths, first_row, key_rows), head_scores(queries, key_part), NEG_FILL
        )
        softmax_w = jnp.exp(scores - log_total[..., None])
        value_heads = value_part.reshape(seq_count, key_rows, H, DH)
        return state_in + jnp.einsum(
            "shcn,snhd->schd",
            softmax_w.astype(jnp.bfloat16),
            value_heads,
            preferred_element_type=jnp.float32,
        )

    context_heads = in_blocks(
        mix_step,
        jnp.zeros(head_shape, jnp.float32),
        (
            lax.all_gather(keys, "grp", axis=1, tiled=True),
            lax.all_gather(values, "grp", axis=1, tiled=True),
        ),
    )
    return (context_heads, log_total)


def query_grads(queries, keys, values, lengths, log_total, delta_heads, dcontext):
    seq_count, query_rows, width_all = queries.shape
    dcontext_heads = dcontext.reshape(seq_count, query_rows, H, DH)

    def query_grad_step(running, pieces, first_row):
        key_part, value_part = pieces
        key_rows = key_part.shape[1]
        scores = jnp.where(
            key_mask(lengths, first_row, key_rows), head_scores(queries, key_part), NEG_FILL
        )
        softmax_w = jnp.exp(scores - log_total[..., None])
        value_heads = value_part.reshape(seq_count, key_rows, H, DH)
        key_heads = key_part.reshape(seq_count, key_rows, H, DH)
        dweights = jnp.einsum(
            "schd,snhd->shcn", dcontext_heads, value_heads, preferred_element_type=jnp.float32
        )
        dscores = (softmax_w * (dweights - delta_heads[..., None])).astype(jnp.bfloat16)
        return running + jnp.einsum(
            "shcn,snhd->schd", dscores, key_heads, preferred_element_type=jnp.float32
        )

    zero_heads = jnp.zeros((seq_count, query_rows, H, DH), jnp.float32)
    folded = in_blocks(
        query_grad_step,
        zero_heads,
        (
            lax.all_gather(keys, "grp", axis=1, tiled=True),
            lax.all_gather(values, "grp", axis=1, tiled=True),
        ),
    )
    return (folded * DH ** (-0.5)).reshape(seq_count, query_rows, width_all)


def key_grads(queries, keys, values, lengths, log_rows, delta_rows, dcontext):
    seq_count, key_rows, width_all = keys.shape
    log_all, delta_all = (
        lax.all_gather(log_rows, "grp", axis=1, tiled=True),
        lax.all_gather(delta_rows, "grp", axis=1, tiled=True),
    )
    own_mask = key_mask(lengths, lax.axis_index("grp") * key_rows, key_rows)
    value_heads = values.reshape(seq_count, key_rows, H, DH)

    def key_grad_step(running, pieces, first_row):
        query_part, dcontext_part = pieces
        query_count = query_part.shape[1]
        log_part = jnp.transpose(
            lax.dynamic_slice_in_dim(log_all, first_row, query_count, 1), (0, 2, 1)
        )
        delta_part = jnp.transpose(
            lax.dynamic_slice_in_dim(delta_all, first_row, query_count, 1), (0, 2, 1)
        )
        scores = jnp.where(own_mask, head_scores(query_part, keys), NEG_FILL)
        softmax_w = jnp.exp(scores - log_part[..., None])
        dcontext_heads = dcontext_part.reshape(seq_count, query_count, H, DH)
        query_heads = query_part.reshape(seq_count, query_count, H, DH)
        dweights = jnp.einsum(
            "schd,snhd->shcn", dcontext_heads, value_heads, preferred_element_type=jnp.float32
        )
        dscores = (softmax_w * (dweights - delta_part[..., None])).astype(jnp.bfloat16)
        dkey_sum = running[0] + jnp.einsum(
            "shcn,schd->snhd", dscores, query_heads, preferred_element_type=jnp.float32
        )
        dvalue_sum = running[1] + jnp.einsum(
            "shcn,schd->snhd",
            softmax_w.astype(jnp.bfloat16),
            dcontext_heads,
            preferred_element_type=jnp.float32,
        )
        return (dkey_sum, dvalue_sum)

    zero_heads = jnp.zeros((seq_count, key_rows, H, DH), jnp.float32)
    dkey_sum, dvalue_sum = in_blocks(
        key_grad_step,
        (zero_heads, zero_heads),
        (
            lax.all_gather(queries, "grp", axis=1, tiled=True),
            lax.all_gather(dcontext, "grp", axis=1, tiled=True),
        ),
    )
    return (
        (dkey_sum * DH ** (-0.5)).reshape(seq_count, key_rows, width_all),
        dvalue_sum.reshape(seq_count, key_rows, width_all),
    )


def forward(hidden, lengths, project, vectors, clips):
    b_query, b_value, b_out, b_up, b_down, gain_one, shift_one, gain_two, shift_two = vectors
    seq_count = lengths.shape[0]
    query_rows = hidden.shape[0] // seq_count
    width_all = hidden.shape[1]
    entering = hidden if clips is None else jnp.clip(hidden, -clips[0], clips[0])
    inputs = entering.astype(jnp.bfloat16)
    queries = (
        (project(inputs, 0) + b_query)
        .astype(jnp.bfloat16)
        .reshape(seq_count, query_rows, width_all)
    )
    keys = project(inputs, 1).astype(jnp.bfloat16).reshape(seq_count, query_rows, width_all)
    values = (
        (project(inputs, 2) + b_value)
        .astype(jnp.bfloat16)
        .reshape(seq_count, query_rows, width_all)
    )
    context_heads, log_total = attention_forward(queries, keys, values, lengths)
    context_low = context_heads.reshape(hidden.shape).astype(jnp.bfloat16)
    first_sum = hidden + project(context_low, 3) + b_out
    first_norm = layer_norm(first_sum, gain_one, shift_one)
    upper_in = first_norm.astype(jnp.bfloat16)
    gate_pre = project(upper_in, 4) + b_up
    lower_in = gelu_exact(gate_pre).astype(jnp.bfloat16)
    second_sum = first_norm + project(lower_in, 5) + b_down
    output = layer_norm(second_sum, gain_two, shift_two)
    kept_values = (
        inputs,
        queries,
        keys,
        values,
        context_heads,
        log_total,
        context_low,
        first_sum,
        first_norm,
        upper_in,
        gate_pre,
        lower_in,
        second_sum,
    )
    return (output, kept_values)


def backward(grad_output, hidden, lengths, latents, vectors, clips, kept_values):
    (
        inputs,
        queries,
        keys,
        values,
        context_heads,
        log_total,
        context_low,
        first_sum,
        first_norm,
        upper_in,
        gate_pre,
        lower_in,
        second_sum,
    ) = kept_values
    w_query, w_key, w_value, w_out, w_up, w_down = latents
    gain_one, shift_one, gain_two, shift_two = (vectors[5], vectors[6], vectors[7], vectors[8])
    seq_count, query_rows, width_all = queries.shape
    unused, pull_two = jax.vjp(layer_norm, second_sum, gain_two, shift_two)
    dsecond, dgain_two, dshift_two = pull_two(grad_output)
    dsecond_low = dsecond.astype(jnp.bfloat16)
    grad_down = weight_grad(dsecond_low, lower_in)
    dlower = student_back(dsecond_low, w_down)
    unused, pull_gate = jax.vjp(gelu_exact, gate_pre)
    dgate = pull_gate(dlower)[0]
    dgate_low = dgate.astype(jnp.bfloat16)
    grad_up = weight_grad(dgate_low, upper_in)
    dupper = student_back(dgate_low, w_up)
    dfirst = dsecond + dupper
    unused, pull_one = jax.vjp(layer_norm, first_sum, gain_one, shift_one)
    dfirst_sum, dgain_one, dshift_one = pull_one(dfirst)
    dbranch_low = dfirst_sum.astype(jnp.bfloat16)
    grad_out = weight_grad(dbranch_low, context_low)
    dcontext = (
        student_back(dbranch_low, w_out)
        .astype(jnp.bfloat16)
        .reshape(seq_count, query_rows, width_all)
    )
    delta_rows = jnp.sum(
        dcontext.reshape(seq_count, query_rows, H, DH).astype(jnp.float32) * context_heads, axis=3
    )
    dqueries = query_grads(
        queries, keys, values, lengths, log_total, jnp.transpose(delta_rows, (0, 2, 1)), dcontext
    )
    dkeys, dvalues = key_grads(
        queries, keys, values, lengths, jnp.transpose(log_total, (0, 2, 1)), delta_rows, dcontext
    )
    all_rows = seq_count * query_rows
    dqueries_low = dqueries.reshape(all_rows, width_all).astype(jnp.bfloat16)
    dkeys_low = dkeys.reshape(all_rows, width_all).astype(jnp.bfloat16)
    dvalues_low = dvalues.reshape(all_rows, width_all).astype(jnp.bfloat16)
    grad_query = weight_grad(dqueries_low, inputs)
    grad_key = weight_grad(dkeys_low, inputs)
    grad_value = weight_grad(dvalues_low, inputs)
    dinputs = (
        student_back(dqueries_low, w_query)
        + student_back(dkeys_low, w_key)
        + student_back(dvalues_low, w_value)
    )
    unused, pull_input = jax.vjp(lambda tensor: jnp.clip(tensor, -clips[0], clips[0]), hidden)
    grad_hidden = dfirst_sum + pull_input(dinputs)[0]
    weight_parts = (grad_query, grad_key, grad_value, grad_out, grad_up, grad_down)
    vector_parts = (
        jnp.sum(dqueries_low.astype(jnp.float32), axis=0),
        jnp.sum(dvalues_low.astype(jnp.float32), axis=0),
        jnp.sum(dfirst_sum, axis=0),
        jnp.sum(dgate, axis=0),
        jnp.sum(dsecond, axis=0),
        dgain_one,
        dshift_one,
        dgain_two,
        dshift_two,
    )
    return (weight_parts, vector_parts, grad_hidden)


def shards(
    hidden_in,
    seq_lengths,
    latent_query,
    latent_key,
    latent_value,
    latent_out,
    latent_up,
    latent_down,
    bias_query,
    bias_value,
    bias_out,
    bias_up,
    bias_down,
    gain_first,
    shift_first,
    gain_second,
    shift_second,
    clip_input,
    teacher_query,
    teacher_key,
    teacher_value,
    teacher_out,
    teacher_up,
    teacher_down,
    teacher_biases,
    teacher_inner,
    teacher_gains,
    teacher_shifts,
):
    latents = (latent_query, latent_key, latent_value, latent_out, latent_up, latent_down)
    tutors = (teacher_query, teacher_key, teacher_value, teacher_out, teacher_up, teacher_down)
    vectors = (
        bias_query,
        bias_value,
        bias_out,
        bias_up,
        bias_down,
        gain_first,
        shift_first,
        gain_second,
        shift_second,
    )
    tutor_vectors = (
        teacher_biases[0],
        teacher_biases[1],
        teacher_biases[2],
        teacher_inner,
        teacher_biases[3],
        teacher_gains[0],
        teacher_shifts[0],
        teacher_gains[1],
        teacher_shifts[1],
    )
    clips = (clip_input,)
    micro_count, seq_count, local_rows, width_all = hidden_in.shape
    positions = lax.axis_index("grp") * local_rows + jnp.arange(local_rows, dtype=jnp.int32)

    def student_weight(operand, slot_index):
        return student_project(operand, latents[slot_index])

    def tutor_weight(operand, slot_index):
        return teacher_project(operand, tutors[slot_index])

    weight_sums = None
    vector_sums = [jnp.zeros(vector.shape, jnp.float32) for vector in vectors]
    error_sum = jnp.zeros((), jnp.float32)
    outputs_all = []
    grads_all = []
    for micro_index in range(micro_count):
        hidden = (
            hidden_in[micro_index].astype(jnp.float32).reshape(seq_count * local_rows, width_all)
        )
        lengths = seq_lengths[micro_index]
        targets, unused = forward(hidden, lengths, tutor_weight, tutor_vectors, None)
        output, kept_values = forward(hidden, lengths, student_weight, vectors, clips)
        row_keep = (
            (positions[None, :] < lengths[:, None])
            .astype(jnp.float32)
            .reshape(seq_count * local_rows, 1)
        )
        difference = output - targets
        error_sum = error_sum + 0.5 * jnp.sum(row_keep * difference * difference)
        weight_parts, vector_parts, grad_hidden = backward(
            row_keep * difference, hidden, lengths, latents, vectors, clips, kept_values
        )
        if weight_sums is None:
            weight_sums = list(weight_parts)
        else:
            weight_sums = [running + added for running, added in zip(weight_sums, weight_parts)]
        vector_sums = [running + added for running, added in zip(vector_sums, vector_parts)]
        outputs_all.append(output.astype(jnp.bfloat16).reshape(seq_count, local_rows, width_all))
        grads_all.append(grad_hidden.reshape(seq_count, local_rows, width_all))
    weight_sums = (
        lax.psum_scatter(
            weight_sums[0].astype(jnp.bfloat16), "grp", scatter_dimension=0, tiled=True
        ).astype(jnp.float32),
        lax.psum_scatter(
            weight_sums[1].astype(jnp.bfloat16), "grp", scatter_dimension=0, tiled=True
        ).astype(jnp.float32),
        lax.psum_scatter(
            weight_sums[2].astype(jnp.bfloat16), "grp", scatter_dimension=0, tiled=True
        ).astype(jnp.float32),
        lax.psum_scatter(
            weight_sums[3].astype(jnp.bfloat16), "grp", scatter_dimension=0, tiled=True
        ).astype(jnp.float32),
        lax.psum_scatter(
            weight_sums[4].astype(jnp.bfloat16), "grp", scatter_dimension=0, tiled=True
        ).astype(jnp.float32),
        lax.psum_scatter(
            weight_sums[5].astype(jnp.bfloat16), "grp", scatter_dimension=0, tiled=True
        ).astype(jnp.float32),
    )
    vector_shards = (
        lax.psum_scatter(
            vector_sums[0].astype(jnp.bfloat16), "grp", scatter_dimension=0, tiled=True
        ).astype(jnp.float32),
        lax.psum_scatter(
            vector_sums[1].astype(jnp.bfloat16), "grp", scatter_dimension=0, tiled=True
        ).astype(jnp.float32),
        lax.psum_scatter(
            vector_sums[2].astype(jnp.bfloat16), "grp", scatter_dimension=0, tiled=True
        ).astype(jnp.float32),
        lax.psum_scatter(
            vector_sums[3].astype(jnp.bfloat16), "grp", scatter_dimension=0, tiled=True
        ).astype(jnp.float32),
        lax.psum_scatter(
            vector_sums[4].astype(jnp.bfloat16), "grp", scatter_dimension=0, tiled=True
        ).astype(jnp.float32),
        lax.psum_scatter(
            vector_sums[5].astype(jnp.bfloat16), "grp", scatter_dimension=0, tiled=True
        ).astype(jnp.float32),
        lax.psum_scatter(
            vector_sums[6].astype(jnp.bfloat16), "grp", scatter_dimension=0, tiled=True
        ).astype(jnp.float32),
        lax.psum_scatter(
            vector_sums[7].astype(jnp.bfloat16), "grp", scatter_dimension=0, tiled=True
        ).astype(jnp.float32),
        lax.psum_scatter(
            vector_sums[8].astype(jnp.bfloat16), "grp", scatter_dimension=0, tiled=True
        ).astype(jnp.float32),
    )
    totals = (
        lax.psum(weight_sums[0].astype(jnp.bfloat16), "rep").astype(jnp.float32),
        lax.psum(weight_sums[1].astype(jnp.bfloat16), "rep").astype(jnp.float32),
        lax.psum(weight_sums[2].astype(jnp.bfloat16), "rep").astype(jnp.float32),
        lax.psum(weight_sums[3].astype(jnp.bfloat16), "rep").astype(jnp.float32),
        lax.psum(weight_sums[4].astype(jnp.bfloat16), "rep").astype(jnp.float32),
        lax.psum(weight_sums[5].astype(jnp.bfloat16), "rep").astype(jnp.float32),
        lax.psum(vector_shards[0].astype(jnp.bfloat16), "rep").astype(jnp.float32),
        lax.psum(vector_shards[1].astype(jnp.bfloat16), "rep").astype(jnp.float32),
        lax.psum(vector_shards[2].astype(jnp.bfloat16), "rep").astype(jnp.float32),
        lax.psum(vector_shards[3].astype(jnp.bfloat16), "rep").astype(jnp.float32),
        lax.psum(vector_shards[4].astype(jnp.bfloat16), "rep").astype(jnp.float32),
        lax.psum(vector_shards[5].astype(jnp.bfloat16), "rep").astype(jnp.float32),
        lax.psum(vector_shards[6].astype(jnp.bfloat16), "rep").astype(jnp.float32),
        lax.psum(vector_shards[7].astype(jnp.bfloat16), "rep").astype(jnp.float32),
        lax.psum(vector_shards[8].astype(jnp.bfloat16), "rep").astype(jnp.float32),
    )
    error_all = lax.psum(error_sum, ("rep", "grp"))
    entries = (
        micro_count
        * seq_count
        * lax.axis_size("rep")
        * local_rows
        * lax.axis_size("grp")
        * width_all
    )
    distill_loss = error_all / entries
    return (
        jnp.stack(outputs_all),
        distill_loss,
        jnp.stack(grads_all),
        totals[0],
        totals[1],
        totals[2],
        totals[3],
        totals[4],
        totals[5],
        totals[6],
        totals[7],
        totals[8],
        totals[9],
        totals[10],
        totals[11],
        totals[12],
        totals[13],
        totals[14],
    )


F32 = jnp.float32
BF16 = jnp.bfloat16
ANY = pl.BlockSpec(memory_space=pl.ANY)
VM = pl.BlockSpec(memory_space=pltpu.VMEM)
SM = pl.BlockSpec(memory_space=pltpu.SMEM)
VMEM_LIMIT = 60 * 1024 * 1024

I_CORE, I_REP, I_Z, I_LEN, I_RING = 0, 1, 2, 3, 4


def z_ring(line):
    return list(range(0, line, 2)) + list(range(1, line, 2))[::-1]


def dims(a, b, ca, cb):
    return lax.dot_general(a, b, (((ca,), (cb,)), ((), ())), preferred_element_type=F32)


def params(**kw):
    return pltpu.CompilerParams(vmem_limit_bytes=VMEM_LIMIT, **kw)


def cost(flops, nbytes, trans=0):
    return pl.CostEstimate(flops=int(flops), bytes_accessed=int(nbytes), transcendentals=int(trans))


def wait_all(ref, sem):
    pltpu.make_async_copy(ref, ref, sem).wait()


def binary_rows(latent):
    level = jnp.mean(jnp.abs(latent), axis=1, keepdims=True)
    return jnp.where(latent > 0, level, jnp.where(latent < 0, -level, 0.0)).astype(BF16)


def first_kernel(lo, lu, ld, to, tu, td, mine, up, down, out, sems):
    rep = lax.axis_index("rep")
    rows, width = up.shape
    half = out.shape[0]
    start = pl.multiple_of(rep * rows, rows)
    part = pl.ds(pl.multiple_of(lax.rem(rep, 2) * half, half), half)
    columns = pl.ds(pl.multiple_of(rep * width, width), width)
    last = mine.at[pl.ds(4 * rows, half)]
    copies = (
        pltpu.make_async_copy(lu.at[pl.ds(start, rows)], up, sems.at[0]),
        pltpu.make_async_copy(ld, down, sems.at[1]),
        pltpu.make_async_copy(lo.at[part], out, sems.at[2]),
        pltpu.make_async_copy(
            tu.at[pl.ds(start, rows)], mine.at[pl.ds(2 * rows, rows)], sems.at[3]
        ),
        pltpu.make_async_copy(td.at[:, columns], mine.at[pl.ds(3 * rows, rows)], sems.at[4]),
    )
    for copy in copies:
        copy.start()
    copies[0].wait()
    mine[0:rows] = binary_rows(up[...])
    copies[2].wait()

    @pl.when(rep < 2)
    def _():
        mine[4 * rows :] = binary_rows(out[...])

    @pl.when(rep >= 2)
    def _():
        copy = pltpu.make_async_copy(to.at[part], last, sems.at[5])
        copy.start()
        copy.wait()

    copies[1].wait()
    level = jnp.mean(jnp.abs(down[...]), axis=1, keepdims=True)
    own = down[:, columns]
    mine[rows : 2 * rows] = jnp.where(
        own > 0, level, jnp.where(own < 0, -level, 0.0)
    ).astype(BF16)
    copies[3].wait()
    copies[4].wait()


def first_piece(latents, tutors):
    rows, width = latents[0].shape
    return pl.pallas_call(
        first_kernel,
        out_shape=jax.ShapeDtypeStruct((4 * rows + rows // 2, width), BF16),
        in_specs=[ANY] * 6,
        out_specs=VM,
        scratch_shapes=[
            pltpu.VMEM((rows, width), F32),
            pltpu.VMEM((rows, 4 * width), F32),
            pltpu.VMEM((rows // 2, width), F32),
            pltpu.SemaphoreType.DMA((6,)),
        ],
        compiler_params=params(),
        cost_estimate=cost(1e6, 4e6),
        name="first_piece",
    )(*latents[3:], *tutors[3:])


def pack_kernel(lq, lk, lv, lo, lu, ld, tq, tk, tv, to, tu, td, qkv, own):
    for slot, ref in enumerate((lq, lk, lv)):
        qkv[0, slot] = binary_rows(ref[...])
    for slot, ref in enumerate((tq, tk, tv)):
        qkv[1, slot] = ref[...]
    rows, width = lq.shape
    quarter = own.shape[0]
    half = rows // 2

    def fill(base, up, down):
        for r in range(quarter):
            own[r, base : base + rows] = up[r * rows : (r + 1) * rows]
            own[r, base + rows : base + 2 * rows] = down[:, r * width : (r + 1) * width]

    fill(0, binary_rows(lu[...]), binary_rows(ld[...]))
    fill(2 * rows, tu, td)
    student_out = binary_rows(lo[...])
    for h in range(2):
        own[h, 4 * rows :] = student_out[h * half : (h + 1) * half]
        own[2 + h, 4 * rows :] = to[h * half : (h + 1) * half]


def pack(latents, tutors):
    rows, width = latents[0].shape
    piece = 4 * rows + rows // 2
    return pl.pallas_call(
        pack_kernel,
        out_shape=(
            jax.ShapeDtypeStruct((2, 3, rows, width), BF16),
            jax.ShapeDtypeStruct((4, piece, width), BF16),
        ),
        in_specs=[VM] * 12,
        out_specs=(VM,) * 2,
        compiler_params=params(),
        cost_estimate=cost(4e6, 12e6),
        name="pack",
    )(*latents, *tutors)


def table_kernel(*refs):
    heads_bias, vecs = refs[13:]
    line, _, feats = heads_bias.shape[2:]
    width = line * feats

    def flat(ref):
        return ref[...].reshape(1, ref.shape[0])

    bq, bv, bo, bu, bd, g1, s1, g2, s2 = [flat(ref) for ref in refs[:9]]
    biases, inner, gains, shifts = refs[9:13]
    for net, pair in enumerate(((bq, bv), (biases[0:1], biases[1:2]))):
        for slot, row in enumerate(pair):
            for z in range(line):
                heads_bias[net, slot, z] = row[:, z * feats : (z + 1) * feats]
    rows = (
        (bo, bd, g1, s1, g2, s2),
        (biases[2:3], biases[3:4], gains[0:1], shifts[0:1], gains[1:2], shifts[1:2]),
    )
    for net, up in enumerate((bu, flat(inner))):
        for slot, row in enumerate(rows[net]):
            vecs[net, slot] = row
        for r in range(4):
            vecs[net, V_UP + r] = up[:, r * width : (r + 1) * width]


def table(vectors, tutor_vectors, line):
    width = vectors[0].shape[0]
    return pl.pallas_call(
        table_kernel,
        out_shape=(
            jax.ShapeDtypeStruct((2, 2, line, 1, width // line), F32),
            jax.ShapeDtypeStruct((2, 10, 1, width), F32),
        ),
        in_specs=[VM] * 13,
        out_specs=(VM,) * 2,
        compiler_params=params(),
        cost_estimate=cost(1e5, 2e5),
        name="table",
    )(*vectors, *tutor_vectors)


def load_tokens(info, xs, pieces, sem):
    core = info[I_CORE]
    for k, piece in enumerate(pieces):
        for j in range(2):
            spot = jnp.where(j == 0, core, 1 - core)
            pltpu.make_async_copy(piece.at[j], xs.at[info[I_RING + k], spot], sem).start()


def load_rows(info, ws, own, sib, net, sem):
    core = info[I_CORE]
    for slot in range(3):
        pltpu.make_async_copy(own.at[net, slot], ws.at[slot, core], sem).start()
        pltpu.make_async_copy(sib.at[net, slot], ws.at[slot, 1 - core], sem).start()


def attend_kernel(student, info, *refs):
    pieces, refs = refs[:4], refs[4:]
    own, sib, heads_bias, clip = refs[:4]
    refs = refs[4:]
    net = 0 if student else 1
    if student:
        out, qs, ks, v_out, lse_out, ctx_out, xs, ws, vt, ct, low, sems = refs
    else:
        _, out, xs, ws, qs, ks, vt, ct, low, sems = refs
    load_tokens(info, xs, pieces, sems.at[0])
    load_rows(info, ws, own, sib, net, sems.at[1])
    line, _, half, width = xs.shape
    block = 2 * half
    total, feats = qs.shape[0], ct.shape[0]
    wide = qs.shape[1]
    heads = feats // DH
    place = info[I_Z]
    length = info[I_LEN]
    bq_row, bv_row = heads_bias[net, 0, place], heads_bias[net, 1, place]
    wait_all(xs, sems.at[0])
    wait_all(ws, sems.at[1])

    def project(b, carry):
        rows = pl.ds(pl.multiple_of(b * block, block), block)
        x = xs[b].reshape(block, width)
        if student:
            lim = clip[...]
            x = jnp.clip(x.astype(F32), -lim, lim).astype(BF16)
        q = (dims(x, ws[0].reshape(feats, width), 1, 1) + bq_row).astype(BF16)
        k = dims(x, ws[1].reshape(feats, width), 1, 1).astype(BF16)
        v = (dims(x, ws[2].reshape(feats, width), 1, 1) + bv_row).astype(BF16)
        q = q * jnp.asarray(DH ** (-0.5), BF16)
        places = b * block + lax.broadcasted_iota(jnp.int32, (block, wide - feats), 0)
        extra = lax.broadcasted_iota(jnp.int32, (block, wide - feats), 1) == 0
        ones = jnp.where(extra, 1.0, 0.0).astype(BF16)
        fill = jnp.where(extra & (places >= length), NEG_FILL, 0.0).astype(BF16)
        qs[rows] = jnp.concatenate([q, ones], axis=1)
        ks[rows] = jnp.concatenate([k, fill], axis=1)
        vt[:, rows] = v.astype(F32).T.astype(BF16)
        if student:
            v_out[rows] = v
        return carry

    lax.fori_loop(0, line, project, 0, unroll=True)
    lane = lax.broadcasted_iota(jnp.int32, (1, wide), 1)
    span = total

    def mix(b, carry):
        rows = pl.ds(pl.multiple_of(b * span, span), span)
        q = qs[rows]
        for h in range(heads):
            q_h = jnp.where((lane // DH == h) | (lane >= feats), q, jnp.zeros_like(q))
            scores = dims(ks[...], q_h, 1, 1)
            top = jnp.max(scores, axis=0, keepdims=True)
            weight = jnp.exp(scores - top)
            mass = jnp.sum(weight, axis=0, keepdims=True)
            head = slice(h * DH, (h + 1) * DH)
            mixed = dims(vt[head], weight.astype(BF16), 1, 0) * (1.0 / mass)
            ct[head, rows] = mixed
            if student:
                lse_out[h : h + 1, rows] = top + jnp.log(mass)
        return carry

    lax.fori_loop(0, total // span, mix, 0)
    for b in range(line):
        low[b] = ct[:, b * block : (b + 1) * block].astype(BF16)
        pltpu.make_async_copy(low.at[b], out.at[b, net], sems.at[2 + b]).start()
    if student:
        ctx_out[...] = ct[...]
    for b in range(line):
        pltpu.make_async_copy(low.at[b], out.at[b, net], sems.at[2 + b]).wait()


def attend(info, pieces, own, sib, heads_bias, clip, both=None):
    _, half, width = pieces[0].shape
    line = len(pieces)
    total = line * 2 * half
    rows = own.shape[2]
    feats = 2 * rows
    student = both is None
    wide = (feats // 128 + 1) * 128
    outs = [jax.ShapeDtypeStruct((line, 2, feats, 2 * half), BF16)]
    if student:
        outs += [
            jax.ShapeDtypeStruct((total, wide), BF16),
            jax.ShapeDtypeStruct((total, wide), BF16),
            jax.ShapeDtypeStruct((total, feats), BF16),
            jax.ShapeDtypeStruct((8, total), F32),
            jax.ShapeDtypeStruct((feats, total), F32),
        ]
    own_scratch = [] if student else [pltpu.VMEM((total, wide), BF16)] * 2
    return pl.pallas_call(
        functools.partial(attend_kernel, student),
        out_shape=tuple(outs),
        in_specs=[SM] + [ANY] * 6 + [VM] * 2 + ([] if student else [ANY]),
        out_specs=(ANY,) + (VM,) * (len(outs) - 1),
        scratch_shapes=[
            pltpu.VMEM((line, 2, half, width), BF16),
            pltpu.VMEM((3, 2, rows, width), BF16),
            *own_scratch,
            pltpu.VMEM((feats, total), BF16),
            pltpu.VMEM((feats, total), F32),
            pltpu.VMEM((line, feats, 2 * half), BF16),
            pltpu.SemaphoreType.DMA((2 + line,)),
        ],
        input_output_aliases={} if student else {9: 0},
        compiler_params=params(),
        cost_estimate=cost(6e9, 4e6, 3e6),
        name="attend_student" if student else "attend_tutor",
    )(info, *pieces, own, sib, heads_bias, clip, *([] if student else [both]))


def attend_back_kernel(info, *refs):
    pieces, refs = refs[:4], refs[4:]
    (own, sib, clip, qs, ks, vs, lse, ctx, dctx, part0, part1, part2, part3) = refs[:13]
    keep, send, xs, ws, kt, dct, dq, dk, dv, sems = refs[13:]
    parts = (part0, part1, part2, part3)
    load_tokens(info, xs, pieces, sems.at[0])
    load_rows(info, ws, own, sib, 0, sems.at[1])
    line, _, half, width = xs.shape
    block = 2 * half
    total, feats = dv.shape
    heads = feats // DH
    core = info[I_CORE]
    lim = clip[...]
    for b in range(line):
        cols = slice(b * block, (b + 1) * block)
        kt[:, cols] = ks[cols, 0:feats].astype(F32).T.astype(BF16)
        dct[:, cols] = dctx[b].astype(F32)
    dk[...] = jnp.zeros_like(dk)
    dv[...] = jnp.zeros_like(dv)
    lane = lax.broadcasted_iota(jnp.int32, (1, qs.shape[1]), 1)
    row_head = lax.broadcasted_iota(jnp.int32, (feats, 1), 0) // DH

    def body(b, carry):
        rows = pl.ds(pl.multiple_of(b * block, block), block)
        q = qs[rows]
        g = dctx[b]
        dk_add = dv_add = None
        for h in range(heads):
            head = slice(h * DH, (h + 1) * DH)
            q_h = jnp.where((lane // DH == h) | (lane >= feats), q, jnp.zeros_like(q))
            g_h = jnp.where(row_head == h, g, jnp.zeros_like(g))
            delta = jnp.sum(dct[head, rows] * ctx[head, rows], axis=0, keepdims=True)
            probs = jnp.exp(dims(ks[...], q_h, 1, 1) - lse[h : h + 1, rows])
            dprobs = dims(vs[...], g_h, 1, 0)
            dscores = (probs * (dprobs - delta)).astype(BF16)
            dv_h = dims(probs.astype(BF16), g_h, 1, 1)
            dk_h = dims(dscores, q_h, 1, 0)
            dk_add = dk_h if dk_add is None else dk_add + dk_h
            dv_add = dv_h if dv_add is None else dv_add + dv_h
            dq[head, rows] = dims(kt[head], dscores, 1, 0) * (DH ** (-0.5))
        dk[...] += dk_add
        dv[...] += dv_add
        return carry

    lax.fori_loop(0, line, body, 0)
    wait_all(xs, sems.at[0])
    wait_all(ws, sems.at[1])
    dq_t = dq[...].astype(BF16)
    dq_low = dq_t.astype(F32).T.astype(BF16)
    dk_low = dk[:, 0:feats].astype(BF16)
    dv_low = dv[...].astype(BF16)
    dk_t = dk_low.astype(F32).T.astype(BF16)
    dv_t = dv_low.astype(F32).T.astype(BF16)
    qkv_flat = [ws[slot].reshape(feats, width) for slot in range(3)]
    for k in range(line):
        spot = info[I_RING + k]
        rows = pl.ds(pl.multiple_of(spot * block, block), block)
        dk_rows = dk[rows, 0:feats].astype(BF16)
        dv_rows = dv[rows].astype(BF16)
        dq_rows = dq[:, rows].T.astype(BF16)
        parts[k][...] = (
            dims(dq_rows, qkv_flat[0], 1, 0)
            + dims(dk_rows, qkv_flat[1], 1, 0)
            + dims(dv_rows, qkv_flat[2], 1, 0)
        ).astype(BF16)
    grads = []
    for low_t in (dq_t, dk_t, dv_t):
        acc = None
        for b in range(line):
            x = jnp.clip(xs[b].reshape(block, width).astype(F32), -lim, lim).astype(BF16)
            one = dims(low_t[:, b * block : (b + 1) * block], x, 1, 0)
            acc = one if acc is None else acc + one
        grads.append(acc)
    rows = feats // 2
    bias_q = jnp.sum(dq_low.astype(F32), axis=0, keepdims=True)
    bias_v = jnp.sum(dv_low.astype(F32), axis=0, keepdims=True)
    for rel, ref in ((0, keep), (1, send)):
        for c in range(2):

            @pl.when((core if rel == 0 else 1 - core) == c)
            def _():
                for slot, grad in enumerate(grads):
                    ref[slot * rows : (slot + 1) * rows] = grad[c * rows : (c + 1) * rows].astype(
                        ref.dtype
                    )
                tail = jnp.concatenate(
                    [
                        bias_q[:, c * rows : (c + 1) * rows],
                        bias_v[:, c * rows : (c + 1) * rows],
                        jnp.zeros((1, width - 2 * rows), F32),
                    ],
                    axis=1,
                )
                ref[3 * rows :] = jnp.broadcast_to(tail, (16, width)).astype(ref.dtype)


def attend_back(info, pieces, own, sib, clip, qs, ks, vs, lse, ctx, dctx):
    _, half, width = pieces[0].shape
    line = len(pieces)
    total = line * 2 * half
    rows = own.shape[2]
    feats = 2 * rows
    part = jax.ShapeDtypeStruct((2 * half, width), BF16)
    grad = jax.ShapeDtypeStruct((3 * rows + 16, width), BF16)
    return pl.pallas_call(
        attend_back_kernel,
        out_shape=(part,) * 4 + (grad, grad),
        in_specs=[SM] + [ANY] * 6 + [VM] * 7,
        out_specs=(VM,) * 6,
        scratch_shapes=[
            pltpu.VMEM((line, 2, half, width), BF16),
            pltpu.VMEM((3, 2, rows, width), BF16),
            pltpu.VMEM((feats, total), BF16),
            pltpu.VMEM((feats, total), F32),
            pltpu.VMEM((feats, total), F32),
            pltpu.VMEM(qs.shape, F32),
            pltpu.VMEM((total, feats), F32),
            pltpu.SemaphoreType.DMA((2,)),
        ],
        compiler_params=params(),
        cost_estimate=cost(12e9, 6e6, 3e6),
        name="attend_back",
    )(info, *pieces, own, sib, clip, qs, ks, vs, lse, ctx, dctx)


V_OUT, V_DOWN, V_G1, V_S1, V_G2, V_S2, V_UP = 0, 1, 2, 3, 4, 5, 6
S_OUT, S_DOWN, S_G1, S_S1, S_G2, S_S2, S_UP = 0, 1, 2, 3, 4, 5, 6
PAD = 16


def norm_parts(v):
    centre = v - jnp.mean(v, axis=-1, keepdims=True)
    inv = lax.rsqrt(jnp.mean(centre * centre, axis=-1, keepdims=True) + NORM_EPS)
    return centre * inv, inv


def norm_back(dnormed, normed, inv):
    return inv * (
        dnormed
        - jnp.mean(dnormed, axis=-1, keepdims=True)
        - normed * jnp.mean(dnormed * normed, axis=-1, keepdims=True)
    )


def turned(v):
    return v.T.astype(BF16)


def middle_kernel(counts, info, own, sib, *refs):
    chunks, refs = refs[: 2 * sum(counts)], refs[2 * sum(counts) :]
    (x_own, ctx, vecs) = refs[:3]
    (out_keep, out_send, dfirst_keep, dctx_out) = refs[3:7]
    grads = refs[7:15]
    (weights, w_out, slopes, lower, gup, gdn, sums, base, aim, acc, sems) = refs[15:]
    core, rep, place, length = info[I_CORE], info[I_REP], info[I_Z], info[I_LEN]
    _, quarters, groups, pair, width = weights.shape
    rows = pair // 2
    tokens = ctx.shape[3]
    line = groups // 2
    hidden = groups * rows
    half = rows // 2

    piece = 2 * pair + half
    found = []
    for rel, ref in ((0, own), (1, sib)):
        member = 2 * place + (core if rel == 0 else 1 - core)
        found += [(ref.at[r], 0, piece, r, member) for r in range(quarters)]
    for k in range(1, line):
        for rel in range(2):
            member = 2 * info[I_RING + k] + (core if rel == 0 else 1 - core)
            got = chunks[2 * sum(counts[: k - 1]) + rel * counts[k - 1] :][: counts[k - 1]]
            found += [(got[far], 0, piece, rep ^ far, member) for far in range(3)]
            if counts[k - 1] == 4:
                found.append((got[3], 0, piece, rep ^ 3, member))
            else:
                found.append((got[3], 0, pair, rep ^ 3, member))
                found.append((got[4], pair, piece, rep ^ 3, member))
    fields = (
        (2 * pair, piece, lambda r, g: w_out.at[r // 2, g, lax.rem(r, 2)], 2),
        (pair, 2 * pair, lambda r, g: weights.at[1, r, g], 1),
        (0, pair, lambda r, g: weights.at[0, r, g], 0),
    )
    for lo, hi, target, sem in fields:
        for src, first, last, r, g in found:
            if first <= lo and hi <= last:
                pltpu.make_async_copy(
                    src.at[pl.ds(lo - first, hi - lo)], target(r, g), sems.at[sem]
                ).start()

    def up_rows(net, r):
        return jnp.concatenate(
            [weights[net, q, 2 * r + g, 0:rows] for g in range(2) for q in range(quarters)], axis=0
        )

    def down_rows(net, r):
        return weights[net, r, :, rows:].reshape(width, hidden)

    wait_all(w_out, sems.at[2])
    x_low = jnp.concatenate(
        [x_own[jnp.where(core == j, 0, 1)] for j in range(2)], axis=0
    ).astype(F32)

    def row(net, which):
        return vecs[net, which]

    def context_of(net):
        flat = jnp.concatenate([ctx[zb, net] for zb in range(line)], axis=0)
        return flat, flat.astype(F32).T.astype(BF16)

    def upper(net, ctx):
        first = (
            x_low + dims(ctx, w_out[net].reshape(width, width), 1, 1) + row(net, V_OUT)
        )
        normed, inv = norm_parts(first)
        return normed, inv, normed * row(net, V_G1) + row(net, V_S1)

    def lower_half(net, upper_in, keep):
        acc[...] = jnp.zeros_like(acc)

        def step(r, carry):
            gate = (
                dims(upper_in, up_rows(net, r), 1, 1)
                + vecs[net, V_UP + r]
            )
            below = 0.5 * (1.0 + lax.erf(gate * 0.7071067811865476))
            low = (gate * below).astype(BF16)
            if keep:
                slopes[r] = below + gate * (0.3989422804014327 * jnp.exp(-0.5 * gate * gate))
                lower[r] = low
            acc[...] += dims(low, down_rows(net, r), 1, 1)
            return carry

        lax.fori_loop(0, quarters, step, 0, unroll=True)
        return acc[...]

    _, ctx_tutor = context_of(1)
    _, _, first_norm = upper(1, ctx_tutor)
    ctx_flat, ctx_low = context_of(0)
    normed_one, inv_one, first_norm_s = upper(0, ctx_low)
    base[...] = first_norm_s
    wait_all(weights.at[1], sems.at[1])
    second = first_norm + lower_half(1, first_norm.astype(BF16), False) + row(1, V_DOWN)
    normed, _ = norm_parts(second)
    aim[...] = normed * row(1, V_G2) + row(1, V_S2)

    wait_all(weights.at[0], sems.at[0])
    upper_in = first_norm_s.astype(BF16)
    second = base[...] + lower_half(0, upper_in, True) + row(0, V_DOWN)
    normed_two, inv_two = norm_parts(second)
    output = normed_two * row(0, V_G2) + row(0, V_S2)
    aim[...] = output - aim[...]
    acc[...] = output

    def part_of(ref, j):
        return ref[pl.ds(pl.multiple_of(j * (tokens // 2), tokens // 2), tokens // 2)]

    out_keep[...] = part_of(acc, core).astype(BF16)
    out_send[...] = part_of(acc, 1 - core).astype(BF16)
    where = place * tokens + lax.broadcasted_iota(jnp.int32, (tokens, 1), 0)
    kept = jnp.where(where < length, 1.0, 0.0).astype(F32)
    dout = kept * aim[...]
    sums[...] = jnp.zeros_like(sums)
    error = 0.5 * jnp.sum(dout * dout)
    sums[S_G2] = jnp.sum(dout * normed_two, axis=0, keepdims=True)
    sums[S_S2] = jnp.sum(dout, axis=0, keepdims=True)
    dsecond = norm_back(dout * row(0, V_G2), normed_two, inv_two)
    sums[S_DOWN] = jnp.sum(dsecond, axis=0, keepdims=True)
    g_down = dsecond.astype(BF16)
    g_down_t = turned(dsecond)
    acc[...] = dsecond

    def member_of(rel, z):
        return 2 * z + (core if rel == 0 else 1 - core)

    def send_up(rel, far, k, z, part):
        ref = grads[rel * 4 + (far & 1)].at[far >> 1, k, part]
        src = gup.at[member_of(rel, z), rep ^ far, part]
        pltpu.make_async_copy(src, ref, sems.at[3 + rel * 4 + (far & 1)]).start()

    def send_down(rel, high, low, k, z, r, part):
        ref = grads[rel * 4 + 2 + high].at[low, k, part]
        src = gdn.at[r, member_of(rel, z), part]
        pltpu.make_async_copy(src, ref, sems.at[5 + rel * 4 + high]).start()

    main, rest = pl.ds(0, rows), pl.ds(rows, PAD)

    def back(r, carry):
        low = lower[r]
        gdn[r, :, 0:rows] = dims(g_down_t, low, 1, 0).astype(BF16).reshape(groups, rows, hidden)
        dlower = dims(g_down, down_rows(0, r), 1, 0)
        dgate = dlower * slopes[r]
        sums[S_UP + r] = jnp.sum(dgate, axis=0, keepdims=True)
        gup_r = dims(turned(dgate), upper_in, 1, 0).astype(BF16)
        gup[pl.ds(2 * r, 2), :, 0:rows] = gup_r.reshape(2, quarters, rows, width)
        acc[...] += dims(dgate.astype(BF16), up_rows(0, r), 1, 0)
        hops = 0
        for k in range(1, line):
            hops = jnp.where(info[I_RING + k] == r, k, hops)
        far = r ^ rep
        for rel in range(2):
            for way in range(4):
                send_up(rel, way, hops, r, main)
            for high in range(2):

                @pl.when(far // 2 == high)
                def _():
                    for k in range(line):
                        send_down(rel, high, far & 1, k, info[I_RING + k], r, main)

        return carry

    lax.fori_loop(0, quarters, back, 0)
    dfirst = acc[...]
    sums[S_G1] = jnp.sum(dfirst * normed_one, axis=0, keepdims=True)
    sums[S_S1] = jnp.sum(dfirst, axis=0, keepdims=True)
    dsum = norm_back(dfirst * row(0, V_G1), normed_one, inv_one)
    sums[S_OUT] = jnp.sum(dsum, axis=0, keepdims=True)
    dfirst_keep[...] = dsum
    g_out = dsum.astype(BF16)
    dctx = turned(dims(g_out, w_out[0].reshape(width, width), 1, 0))
    dctx_out[...] = dctx.reshape(dctx_out.shape)
    gout = dims(turned(dsum), ctx_flat, 1, 1).reshape(groups, quarters, rows // quarters, width)
    number = rep * groups + 2 * place + core
    high = error.astype(BF16).astype(F32)
    middle_part = (error - high).astype(BF16).astype(F32)
    lane = lax.broadcasted_iota(jnp.int32, (1, width), 1)
    digits = jnp.zeros((1, width), F32)
    for slot, digit in enumerate((high, middle_part, error - high - middle_part)):
        digits = jnp.where(lane == 3 * number + slot, digit, digits)
    ups = jnp.concatenate([sums[S_UP + r] for r in range(quarters)], axis=1)
    slim = rows // quarters
    for g in range(groups):
        own_rows = [sums[which][:, g * rows : (g + 1) * rows] for which in range(6)]
        vectors = jnp.concatenate(
            [
                jnp.concatenate(own_rows, axis=0),
                jnp.zeros((6, width - rows), F32),
            ],
            axis=1,
        )
        inner = jnp.concatenate(
            [
                ups[:, g * 4 * rows : (g + 1) * 4 * rows],
                jnp.zeros((1, width - 4 * rows), F32),
            ],
            axis=1,
        )
        tail = jnp.concatenate([vectors, inner, digits], axis=0)
        for r in range(quarters):
            gup[g, r, rows:] = gout[g, r, :PAD].astype(BF16)
            gdn[r, g, rows:] = jnp.concatenate([gout[g, r, PAD:slim], tail], axis=0).astype(BF16)

    for rel in range(2):
        for far in range(4):
            for k in range(line):
                z = info[I_RING + k]
                send_up(rel, far, k, z, rest)
                send_down(rel, far >> 1, far & 1, k, z, rep ^ far, rest)
    for slot in range(8):
        wait_all(grads[slot], sems.at[3 + slot])


def middle(info, own, sib, counts, chunks, x_own, ctx, vecs):
    line, _, feats, tokens = ctx.shape
    width = line * feats
    quarters = own.shape[0]
    groups = 2 * line
    rows = width // groups
    half = (tokens // 2, width)
    part = jax.ShapeDtypeStruct((2, line, rows + PAD, width), BF16)
    outs = (
        jax.ShapeDtypeStruct(half, BF16),
        jax.ShapeDtypeStruct(half, BF16),
        jax.ShapeDtypeStruct((tokens, width), F32),
        jax.ShapeDtypeStruct((line, feats, tokens), BF16),
    ) + (part,) * 8
    return pl.pallas_call(
        functools.partial(middle_kernel, counts),
        out_shape=outs,
        in_specs=[SM] + [ANY] * (2 + len(chunks)) + [VM] * 3,
        out_specs=(VM,) * 4 + (ANY,) * 8,
        scratch_shapes=[
            pltpu.VMEM((2, quarters, groups, 2 * rows, width), BF16),
            pltpu.VMEM((2, groups, 2, rows // 2, width), BF16),
            pltpu.VMEM((quarters, tokens, width), F32),
            pltpu.VMEM((quarters, tokens, width), BF16),
            pltpu.VMEM((groups, quarters, rows + PAD, width), BF16),
            pltpu.VMEM((quarters, groups, rows + PAD, width), BF16),
            pltpu.VMEM((S_UP + quarters, 1, width), F32),
            pltpu.VMEM((tokens, width), F32),
            pltpu.VMEM((tokens, width), F32),
            pltpu.VMEM((tokens, width), F32),
            pltpu.SemaphoreType.DMA((11,)),
        ],
        compiler_params=params(),
        cost_estimate=cost(15e9, 30e6, 4e6),
        name="middle",
    )(info, own, sib, *chunks, x_own, ctx, vecs)


def finish_up_kernel(info, *refs):
    pieces, (up, out) = refs[:4], refs[4:]
    rows = up.shape[0] // len(pieces)
    for far, ref in enumerate(pieces):
        quarter = info[I_REP] ^ far
        up[pl.ds(pl.multiple_of(quarter * rows, rows), rows)] = ref[0:rows].astype(F32)
        out[pl.ds(pl.multiple_of(quarter * PAD, PAD), PAD)] = ref[rows:].astype(F32)


def finish_up(info, pieces):
    high, width = pieces[0].shape
    rows = high - PAD
    return pl.pallas_call(
        finish_up_kernel,
        out_shape=(
            jax.ShapeDtypeStruct((4 * rows, width), F32),
            jax.ShapeDtypeStruct((4 * PAD, width), F32),
        ),
        in_specs=[SM] + [VM] * 4,
        out_specs=(VM,) * 2,
        compiler_params=params(),
        cost_estimate=cost(1e6, 3e6),
        name="finish_up",
    )(info, *pieces)


def finish_heads_kernel(grad_qkv, gq, gk, gv, bq, bv):
    rows = gq.shape[0]
    for slot, ref in enumerate((gq, gk, gv)):
        ref[...] = grad_qkv[slot * rows : (slot + 1) * rows].astype(F32)
    bias = grad_qkv[3 * rows :].astype(F32)
    bq[...] = bias[0, :rows]
    bv[...] = bias[0, rows : 2 * rows]


def finish_heads(grad_qkv):
    high, width = grad_qkv.shape
    rows = (high - 16) // 3
    return pl.pallas_call(
        finish_heads_kernel,
        out_shape=(jax.ShapeDtypeStruct((rows, width), F32),) * 3
        + (jax.ShapeDtypeStruct((rows,), F32),) * 2,
        in_specs=[VM],
        out_specs=(VM,) * 5,
        compiler_params=params(),
        cost_estimate=cost(1e6, 2e6),
        name="finish_heads",
    )(grad_qkv)


def finish_kernel(entries, info, *refs):
    pieces, refs = refs[:4], refs[4:]
    firsts, down, out, loss, bu = refs[:5]
    others = refs[5:]
    rows, width = out.shape
    slim = rows // len(pieces)
    for r in range(len(pieces)):
        out[r * slim : r * slim + PAD] = firsts[r * PAD : (r + 1) * PAD]
    for far, ref in enumerate(pieces):
        quarter = info[I_REP] ^ far
        down[:, pl.ds(pl.multiple_of(quarter * width, width), width)] = ref[0:rows].astype(F32)
        last = ref[rows:].astype(F32)
        start = pl.multiple_of(quarter * slim + PAD, slim - PAD)
        out[pl.ds(start, slim - PAD)] = last[: slim - PAD]
        if far == 0:
            tail = last[slim - PAD :]
            for slot, vector in enumerate(others):
                vector[...] = tail[slot, :rows]
            bu[...] = tail[S_UP, : 4 * rows]
            loss[...] = jnp.full((1, 1), jnp.sum(tail[S_UP + 1 : S_UP + 2]) / entries, F32)


def finish(info, pieces, firsts, entries):
    high, width = pieces[0].shape
    rows = high - PAD
    vector = jax.ShapeDtypeStruct((rows,), F32)
    return pl.pallas_call(
        functools.partial(finish_kernel, entries),
        out_shape=(
            jax.ShapeDtypeStruct((rows, 4 * width), F32),
            jax.ShapeDtypeStruct((rows, width), F32),
            jax.ShapeDtypeStruct((1, 1), F32),
            jax.ShapeDtypeStruct((4 * rows,), F32),
        )
        + (vector,) * 6,
        in_specs=[SM] + [VM] * 5,
        out_specs=(VM,) * 10,
        compiler_params=params(),
        cost_estimate=cost(1e6, 4e6),
        name="finish",
    )(info, *pieces, firsts)


def add_low(*terms):
    total = terms[0].astype(F32)
    for term in terms[1:]:
        total = total + term.astype(F32)
    return total.astype(BF16)


def after(value, *others):
    return lax.optimization_barrier((value,) + others)[0]


def line_shards(line, *args):
    hidden_in, seq_lengths = args[0], args[1]
    latents, vectors, clip_input = args[2:8], args[8:17], args[17]
    tutors, tutor_vectors = args[18:24], args[24:28]
    micro_count, _, local_rows, width = hidden_in.shape
    rows = latents[0].shape[0]
    rep, grp = lax.axis_index("rep"), lax.axis_index("grp")
    core = lax.rem(grp, 2)
    ring = z_ring(line)

    def over_z(x, pairs):
        return lax.ppermute(x, "grp", [(2 * a + c, 2 * b + c) for a, b in pairs for c in range(2)])

    def next_z(x):
        return over_z(x, [(ring[i], ring[(i + 1) % line]) for i in range(line)])

    def swap(x):
        return lax.ppermute(x, "grp", [(g, g ^ 1) for g in range(2 * line)])

    def to_rep(x, bit):
        return lax.ppermute(x, "rep", [(i, i ^ bit) for i in range(4)])

    def to_tokens(x):
        groups = [[2 * z + c for z in range(line)] for c in range(2)]
        return lax.all_to_all(x, "grp", 0, 0, axis_index_groups=groups, tiled=True)

    scalars = [
        [g % 2, 0, g // 2, 0] + [ring[(ring.index(g // 2) - k) % line] for k in range(line)]
        for g in range(2 * line)
    ]
    lane = jnp.arange(4 + line, dtype=jnp.int32)
    info = jnp.sum(
        jnp.where(jnp.arange(2 * line)[:, None] == grp, jnp.asarray(scalars, jnp.int32), 0), axis=0
    )
    length = jnp.where(core == 0, seq_lengths[0, 0], seq_lengths[1, 0])
    info = jnp.where(lane == I_REP, rep, jnp.where(lane == I_LEN, length, info)).astype(jnp.int32)
    clip = clip_input.reshape(1, width)
    tokens = hidden_in[:, 0]
    keep = jnp.where(core == 0, tokens[0], tokens[1])
    swapped = swap(jnp.where(core == 0, tokens[1], tokens[0]))
    x_own = jnp.stack([keep, swapped])
    piece = first_piece(latents, tutors)
    heads_bias, vecs = table(vectors, tutor_vectors, line)

    def to_sides(value):
        return [value, to_rep(value, 1), to_rep(value, 2)]

    def to_far(got, *ready):
        got.append(to_rep(after(got[1][: 2 * rows], *ready), 2))
        got.append(to_rep(after(got[2][2 * rows :], *ready), 1))

    piece_1 = next_z(piece)
    x_1 = next_z(after(x_own, piece))
    qkv_own, own = pack((after(latents[0], x_own, piece_1),) + latents[1:], tutors)
    qkv_sib = swap(qkv_own)
    sib = swap(own)
    got_1 = to_sides(piece_1)
    x_2 = next_z(after(x_1, piece_1))
    x_3 = next_z(after(x_2, *got_1))
    piece_2 = next_z(after(piece_1, x_2))
    to_far(got_1, x_2)
    tokens_in = [x_own, x_1, x_2, x_3]
    swapped_1 = [swap(one) for one in got_1[:3]]
    tokens_in[0] = after(x_own, *swapped_1)
    mixed, *saved = attend(info, tokens_in, qkv_own, qkv_sib, heads_bias, clip)
    mixed = after(mixed, piece_2, *got_1)
    piece_2 = after(piece_2, mixed)
    piece_3 = next_z(piece_2)
    got_2 = to_sides(piece_2)
    (mixed,) = attend(info, tokens_in, qkv_own, qkv_sib, heads_bias, clip, mixed)
    got_3 = to_sides(after(piece_3, mixed))
    mixed = to_tokens(mixed)
    to_far(got_3, got_3[1], got_3[2])
    to_far(got_2, got_3[1], got_3[2])
    counts = tuple(len(got) for got in (got_1, got_2, got_3))
    chunks = []
    for got in (got_1, got_2, got_3):
        ready = mixed if got is got_3 else got_3[0]
        chunks += got
        if got is got_1:
            chunks += swapped_1 + [swap(after(far, got_3[0])) for far in got[3:]]
            continue
        chunks += [swap(after(one, got_3[0])) for one in got[:3]]
        chunks += [swap(after(far, ready)) for far in got[3:]]
    (
        out_keep,
        out_send,
        dfirst,
        dctx,
        a_keep,
        a_send,
        b_keep,
        b_send,
        a_keep_sib,
        a_send_sib,
        b_keep_sib,
        b_send_sib,
    ) = middle(info, own, sib, counts, chunks, x_own, mixed, vecs)

    def by_micro(kept, got):
        return jnp.where(core == 0, jnp.stack([kept, got]), jnp.stack([got, kept]))[:, None]

    dctx = to_tokens(dctx)
    a_out = add_low(a_send, swap(a_send_sib))
    b_out = add_low(b_send, swap(b_send_sib))
    a_in, b_in = to_rep(a_out, 1), to_rep(b_out, 2)
    a_keep_sib, b_keep_sib = swap(a_keep_sib), swap(b_keep_sib)
    part0, part1, part2, part3, gqkv, gqkv_sib = attend_back(
        info, tokens_in, qkv_own, qkv_sib, clip, *saved, after(dctx, a_out, b_out)
    )
    moving_1 = next_z(part1)
    gqkv_sib = swap(gqkv_sib)
    a_next = add_low(a_keep[1], a_keep_sib[1], after(a_in, part1)[1])
    b_next = add_low(b_keep[1], b_keep_sib[1], after(b_in, part1)[1])
    moving_2 = next_z(after(add_low(moving_1, part2), a_next, b_next))
    a_next, b_next = to_rep(a_next, 2), to_rep(b_next, 1)
    part_a = add_low(a_keep[0], a_keep_sib[0], a_in[0], a_next)
    part_b = add_low(b_keep[0], b_keep_sib[0], b_in[0], b_next)
    moving_3 = next_z(add_low(moving_2, part3))
    layer_out = by_micro(out_keep, swap(after(out_send, moving_2)))
    gqkv = add_low(gqkv, gqkv_sib)
    a_1, b_1 = next_z(part_a[1]), next_z(part_b[1])
    gqkv = add_low(gqkv, to_rep(after(gqkv, moving_2), 1))
    a_2, b_2 = next_z(add_low(a_1, part_a[2])), next_z(after(add_low(b_1, part_b[2]), gqkv))
    gqkv = add_low(gqkv, to_rep(gqkv, 2))
    a_3, b_3 = next_z(add_low(a_2, part_a[3])), next_z(after(add_low(b_2, part_b[3]), gqkv))
    grad_q, grad_k, grad_v, bq, bv = finish_heads(gqkv)
    a_all, b_all = add_low(a_3, part_a[0]), add_low(b_3, part_b[0])
    a_all = after(a_all, grad_q)
    a_all = to_sides(a_all) + [to_rep(a_all, 3)]
    b_all = to_sides(b_all) + [to_rep(b_all, 3)]
    grad_up, firsts = finish_up(info, a_all)
    entries = micro_count * 4 * 2 * line * local_rows * width
    grad_down, grad_out, loss, bu, bo, bd, g1, s1, g2, s2 = finish(info, b_all, firsts, entries)

    hidden_tokens = jnp.where(core == 0, x_own, x_own[::-1])
    hidden_tokens = hidden_tokens.reshape(2 * local_rows, width).astype(F32)
    dxin = moving_3.astype(F32) + part0.astype(F32)
    grad_input = dfirst + jnp.where(jnp.abs(hidden_tokens) < clip, dxin, 0.0)
    halves = grad_input.reshape(2, local_rows, width)
    grad_input = by_micro(
        jnp.where(core == 0, halves[0], halves[1]),
        swap(jnp.where(core == 0, halves[1], halves[0])),
    )
    return (
        layer_out,
        loss.reshape(()),
        grad_input,
        grad_q,
        grad_k,
        grad_v,
        grad_out,
        grad_up,
        grad_down,
        bq,
        bv,
        bo,
        bu,
        bd,
        g1,
        s1,
        g2,
        s2,
    )


def fits_line(mesh, args):
    line = mesh.shape["grp"] // 2
    micro_count, seq_count, total, width = args[0].shape
    hidden = args[6].shape[0]
    return (
        mesh.shape["rep"] == 4
        and line == 4
        and H % line == 0
        and micro_count == 2
        and seq_count == mesh.shape["rep"]
        and total == 8 * 128
        and hidden == 4 * width
    )


def solution(mesh):
    def mapped(body):
        return jax.shard_map(
        body,
        mesh=mesh,
        in_specs=(
            P(None, "rep", "grp", None),
            P(None, "rep"),
            P("grp", None),
            P("grp", None),
            P("grp", None),
            P("grp", None),
            P("grp", None),
            P("grp", None),
            P(),
            P(),
            P(),
            P(),
            P(),
            P(),
            P(),
            P(),
            P(),
            P(),
            P("grp", None),
            P("grp", None),
            P("grp", None),
            P("grp", None),
            P("grp", None),
            P("grp", None),
            P(),
            P(),
            P(),
            P(),
        ),
        out_specs=(
            P(None, "rep", "grp", None),
            P(),
            P(None, "rep", "grp", None),
            P("grp", None),
            P("grp", None),
            P("grp", None),
            P("grp", None),
            P("grp", None),
            P("grp", None),
            P("grp"),
            P("grp"),
            P("grp"),
            P("grp"),
            P("grp"),
            P("grp"),
            P("grp"),
            P("grp"),
            P("grp"),
        ),
        check_vma=False,
    )

    def step(*args):
        if fits_line(mesh, args):
            line = mesh.shape["grp"] // 2
            return mapped(functools.partial(line_shards, line))(*args)
        return mapped(shards)(*args)

    return step
```
